32 devices in a mesh: dp: 4 (over y, x), seq: 8 (over z, core).
Axes of the slice: x: 2, y: 2, z: 4, core: 2. Of those that a mesh axis runs over, the one named last changes fastest.
Arguments:
- tokens: bfloat16 [8, 1024, 1024], P('dp', 'seq'), may hold values from -6 to 6
- lengths: int32 [8], P('dp'), may hold values from 32 to 1024, as said below
- w_query: bfloat16 [1024, 1024], P(('dp', 'seq')), may hold values from -0.1875 to 0.1875
- w_key: bfloat16 [1024, 1024], P(('dp', 'seq')), may hold values from -0.1875 to 0.1875
- w_value: bfloat16 [1024, 1024], P(('dp', 'seq')), may hold values from -0.1875 to 0.1875
- w_out: bfloat16 [1024, 1024], P(('dp', 'seq')), may hold values from -6 to 6
- w_up: bfloat16 [1024, 4096], P(('dp', 'seq')), may hold values from -0.1875 to 0.1875
- w_down: bfloat16 [4096, 1024], P(('dp', 'seq')), may hold values from -0.09375 to 0.09375
- b_query: bfloat16 [1024], P(('dp', 'seq')), may hold values from -3 to 3
- b_value: bfloat16 [1024], P(('dp', 'seq')), may hold values from -3 to 3
- b_out: bfloat16 [1024], P(('dp', 'seq')), may hold values from -3 to 3
- attn_gain: bfloat16 [1024], P(('dp', 'seq')), may hold values from 0.099609375 to 1.8984375
- attn_shift: bfloat16 [1024], P(('dp', 'seq')), may hold values from -3 to 3
- b_up: bfloat16 [4096], P(('dp', 'seq')), may hold values from -3 to 3
- b_down: bfloat16 [1024], P(('dp', 'seq')), may hold values from -3 to 3
- ffn_gain: bfloat16 [1024], P(('dp', 'seq')), may hold values from 0.099609375 to 1.8984375
- ffn_shift: bfloat16 [1024], P(('dp', 'seq')), may hold values from -3 to 3
- cotangent: bfloat16 [8, 1024, 1024], P('dp', 'seq'), may hold values from -6 to 6
Outputs:
- out_tokens: bfloat16 [8, 1024, 1024], P('dp', 'seq')
- grad_tokens: bfloat16 [8, 1024, 1024], P('dp', 'seq')
- query_grad: float32 [1024, 1024], P(('dp', 'seq'))
- key_grad: float32 [1024, 1024], P(('dp', 'seq'))
- value_grad: float32 [1024, 1024], P(('dp', 'seq'))
- outproj_grad: float32 [1024, 1024], P(('dp', 'seq'))
- upproj_grad: float32 [1024, 4096], P(('dp', 'seq'))
- downproj_grad: float32 [4096, 1024], P(('dp', 'seq'))
- querybias_grad: float32 [1024], P(('dp', 'seq'))
- valuebias_grad: float32 [1024], P(('dp', 'seq'))
- outbias_grad: float32 [1024], P(('dp', 'seq'))
- attngain_grad: float32 [1024], P(('dp', 'seq'))
- attnshift_grad: float32 [1024], P(('dp', 'seq'))
- upbias_grad: float32 [4096], P(('dp', 'seq'))
- downbias_grad: float32 [1024], P(('dp', 'seq'))
- ffngain_grad: float32 [1024], P(('dp', 'seq'))
- ffnshift_grad: float32 [1024], P(('dp', 'seq'))
The draws below stay inside these ranges and needn't reach their ends.
Inputs may be any that keep to these rules, and one draw needn't show every extreme that they name: Positions 0 to lengths - 1 of a sequence are its valid tokens; in every draw one sequence has all 1024 valid.
All inputs are finite; a program needn't handle non-finite values.
Results may differ from the reference program's by a relative error of at most 0.025.
Values may be sent and summed in bfloat16 or wider, within the bound.
No kernel may reach another device: no remote copies, remote signals or barrier semaphores. Data moves between devices by JAX's collectives and lax.ppermute only.
A program may use at most 256 MiB of HBM per device.

```python
import math
import jax
import jax.numpy as jnp
from jax import lax

D = 1024
HEADS = 16
HEAD_DIM = 64
FF = 4096
LENGTH = 1024
SEQUENCES = 8


def draw_lengths(key, part):
    key_base, key_halve, key_pick = jax.random.split(key, 3)
    base_len = jax.random.randint(key_base, (SEQUENCES,), LENGTH // 2, LENGTH + 1)
    halvings = jax.random.randint(key_halve, (SEQUENCES,), 0, 5)
    shrunk = base_len // jnp.left_shift(jnp.ones_like(halvings), halvings)
    chosen = jax.random.randint(key_pick, (), 0, SEQUENCES)
    return jnp.where(jnp.arange(SEQUENCES) == chosen, LENGTH, shrunk).astype(jnp.int32)


def levels(stream_key, extent, shards, least, top_value):
    level, own = 1.0, jax.random.fold_in(stream_key, 6)
    for axis_at, shards_of in shards:
        draws = jnp.exp(jax.random.uniform(jax.random.fold_in(own, axis_at), (shards_of,), jnp.float32, least / len(shards), top_value / len(shards)))
        level = level * jnp.repeat(draws, extent[axis_at] // shards_of).reshape([-1 if axis == axis_at else 1 for axis in range(len(extent))])
    return level


def noise(own_key, shape, spread, bound, shards=(), kind=jnp.bfloat16):
    array = jax.random.normal(own_key, shape, jnp.float32) * spread
    if len(shards) > 0:
        array = levels(own_key, shape, shards, -0.22, 0.18) * array
    return jnp.clip(array, min=-bound, max=bound).astype(kind)


def setup_inputs(seed: int = 0) -> dict:
    keys = jax.random.split(jax.random.key(seed), 19)
    return {
        "tokens": noise(keys[0], (SEQUENCES, LENGTH, D), 1.0, 6.0, ((0, 4), (1, 8))),
        "lengths": draw_lengths(jax.random.fold_in(keys[18], 71), 0),
        "w_query": noise(keys[2], (D, D), D ** -0.5, 0.1875, ((0, 32),)),
        "w_key": noise(keys[3], (D, D), D ** -0.5, 0.1875, ((0, 32),)),
        "w_value": noise(keys[4], (D, D), D ** -0.5, 0.1875, ((0, 32),)),
        "w_out": noise(keys[5], (D, D), 1 ** -0.5, 6.0, ((0, 32),)),
        "w_up": noise(keys[6], (D, FF), D ** -0.5, 0.1875, ((0, 32),)),
        "w_down": noise(keys[7], (FF, D), FF ** -0.5, 0.09375, ((0, 32),)),
        "b_query": noise(keys[8], (D,), 0.5, 3.0, ((0, 32),)),
        "b_value": noise(keys[9], (D,), 0.5, 3.0, ((0, 32),)),
        "b_out": noise(keys[10], (D,), 0.5, 3.0, ((0, 32),)),
        "attn_gain": jnp.clip(1.0 + 0.18 * jax.random.normal(keys[11], (D,), jnp.float32), 0.099609375, 1.8984375).astype(jnp.bfloat16),
        "attn_shift": noise(keys[12], (D,), 0.5, 3.0, ((0, 32),)),
        "b_up": noise(keys[13], (FF,), 0.5, 3.0, ((0, 32),)),
        "b_down": noise(keys[14], (D,), 0.5, 3.0, ((0, 32),)),
        "ffn_gain": jnp.clip(1.0 + 0.18 * jax.random.normal(keys[15], (D,), jnp.float32), 0.099609375, 1.8984375).astype(jnp.bfloat16),
        "ffn_shift": noise(keys[16], (D,), 0.5, 3.0, ((0, 32),)),
        "cotangent": noise(keys[17], (SEQUENCES, LENGTH, D), 1.0, 6.0, ((0, 4), (1, 8))),
    }


highest = lax.Precision.HIGHEST
score_scale = 0.125
epsilon = 1e-05
masked_score = -1e+30

@jax.custom_vjp
def low(v):
    return lax.optimization_barrier(v.astype(jnp.bfloat16)).astype(jnp.float32)

@jax.custom_vjp
def low_back(v):
    return v

def low_keep(v):
    return (low(v), None)

def low_pass(kept, grad):
    return (grad,)

def back_keep(v):
    return (v, None)

def back_low(kept, grad):
    return (low(grad),)
low.defvjp(low_keep, low_pass)
low_back.defvjp(back_keep, back_low)

def round_both(values):
    return low_back(low(values))

def matmul(left, right):
    return jnp.dot(left, right, precision=highest)

def layer_norm(values, gain, shift):
    average = lax.optimization_barrier(jnp.mean(values, axis=-1, keepdims=True))
    centred = values - average
    variance = lax.optimization_barrier(jnp.mean(centred * centred, axis=-1, keepdims=True))
    return centred * lax.rsqrt(variance + epsilon) * gain + shift

def sequence_forward(inputs_seq, length, params):
    w_query, w_key, w_value, w_out, w_up, w_down, b_query, b_value, b_out, attn_gain, attn_shift, b_up, b_down, ffn_gain, ffn_shift = params
    query = round_both(matmul(inputs_seq, w_query) + b_query)
    keys_all = round_both(matmul(inputs_seq, w_key))
    values_all = round_both(matmul(inputs_seq, w_value) + b_value)
    query_heads = query.reshape(LENGTH, HEADS, HEAD_DIM)
    key_heads = keys_all.reshape(LENGTH, HEADS, HEAD_DIM)
    value_heads = values_all.reshape(LENGTH, HEADS, HEAD_DIM)
    keep_mask = jnp.arange(LENGTH, dtype=jnp.int32) < length
    block_rows = math.gcd(512, LENGTH)

    def one_block(first_index):
        query_block = lax.dynamic_slice_in_dim(query_heads, first_index, block_rows, 0)
        scores = low_back(jnp.einsum('qhd,khd->hqk', query_block, key_heads, precision=highest) * score_scale)
        masked = jnp.where(keep_mask[None, None, :], scores, masked_score)
        row_max = lax.optimization_barrier(jnp.max(masked, axis=-1, keepdims=True))
        exp_scores = jnp.exp(masked - row_max)
        probs_all = low(exp_scores / lax.optimization_barrier(jnp.sum(exp_scores, axis=-1, keepdims=True)))
        return jnp.einsum('hqk,khd->qhd', probs_all, value_heads, precision=highest)
    starts = jnp.arange(LENGTH // block_rows, dtype=jnp.int32) * block_rows
    context = lax.map(jax.checkpoint(one_block), starts).reshape(LENGTH, D)
    attn = round_both(context)
    attn_out = low_back(matmul(attn, w_out) + b_out)
    first = low(layer_norm(inputs_seq + attn_out, attn_gain, attn_shift))
    inner = low_back(matmul(first, w_up) + b_up)
    active = low(jax.nn.gelu(inner, approximate=False))
    outer = low_back(matmul(active, w_down) + b_down)
    return layer_norm(first + outer, ffn_gain, ffn_shift)

def reference(tokens, lengths, w_query, w_key, w_value, w_out, w_up, w_down, b_query, b_value, b_out, attn_gain, attn_shift, b_up, b_down, ffn_gain, ffn_shift, cotangent):
    params = (w_query, w_key, w_value, w_out, w_up, w_down, b_query, b_value, b_out, attn_gain, attn_shift, b_up, b_down, ffn_gain, ffn_shift)
    params = tuple((item.astype(jnp.float32) for item in params))
    inputs = tokens.astype(jnp.float32)

    def forward(inputs_all, params_all):

        def one_sequence(pair):
            return sequence_forward(pair[0], pair[1], params_all)
        return lax.map(jax.checkpoint(one_sequence), (inputs_all, lengths))
    output, pullback = jax.vjp(forward, inputs, params)
    grad_inputs, grads = pullback(cotangent.astype(jnp.float32))
    g_query, g_key, g_value, g_out, g_up, g_down, g_bquery, g_bvalue, g_bout, g_again, g_ashift, g_bup, g_bdown, g_fgain, g_fshift = grads
    return (output.astype(jnp.bfloat16), grad_inputs.astype(jnp.bfloat16), g_query, g_key, g_value, g_out, g_up, g_down, g_bquery, g_bvalue, g_bout, g_again, g_ashift, g_bup, g_bdown, g_fgain, g_fshift)
```

```python
import functools

import jax
import jax.numpy as jnp
from jax import lax
from jax.sharding import PartitionSpec as P

HEADS = 16


score_scale = 0.125
epsilon = 1e-05
masked_score = -1e30


def layer_norm(values, gain, shift):
    average = jnp.mean(values, axis=-1, keepdims=True)
    centred = values - average
    variance = jnp.mean(centred * centred, axis=-1, keepdims=True)
    return centred * lax.rsqrt(variance + epsilon) * gain + shift


def gelu_exact(values):
    return jax.nn.gelu(values, approximate=False)


def project(values, weight):
    return jnp.einsum("srd,de->sre", values, weight, preferred_element_type=jnp.float32)


def project_back(grads, weight):
    return jnp.einsum("sre,de->srd", grads, weight, preferred_element_type=jnp.float32)


def outer_sum(values, grads):
    return jnp.einsum("srd,sre->de", values, grads, preferred_element_type=jnp.float32)


def row_total(grads):
    return jnp.sum(grads.astype(jnp.float32), axis=(0, 1))


def key_valid(lengths, first_index, key_count):
    places = first_index + jnp.arange(key_count, dtype=jnp.int32)
    return (places[None, :] < lengths[:, None])[:, None, None, :]


def local_gathered(
    tokens,
    lengths,
    w_query,
    w_key,
    w_value,
    w_out,
    w_up,
    w_down,
    b_query,
    b_value,
    b_out,
    attn_gain,
    attn_shift,
    b_up,
    b_down,
    ffn_gain,
    ffn_shift,
    cotangent,
):
    local_seqs, local_rows, model_width = tokens.shape
    head_count = HEADS
    head_size = model_width // head_count
    row_offset = lax.axis_index("seq") * local_rows
    bf_type = jnp.bfloat16
    fl_type = jnp.float32
    gathered = (
        lax.all_gather(w_query, ("dp", "seq"), axis=0, tiled=True),
        lax.all_gather(w_key, ("dp", "seq"), axis=0, tiled=True),
        lax.all_gather(w_value, ("dp", "seq"), axis=0, tiled=True),
        lax.all_gather(w_out, ("dp", "seq"), axis=0, tiled=True),
        lax.all_gather(w_up, ("dp", "seq"), axis=0, tiled=True),
        lax.all_gather(w_down, ("dp", "seq"), axis=0, tiled=True),
        lax.all_gather(b_query, ("dp", "seq"), axis=0, tiled=True),
        lax.all_gather(b_value, ("dp", "seq"), axis=0, tiled=True),
        lax.all_gather(b_out, ("dp", "seq"), axis=0, tiled=True),
        lax.all_gather(attn_gain, ("dp", "seq"), axis=0, tiled=True),
        lax.all_gather(attn_shift, ("dp", "seq"), axis=0, tiled=True),
        lax.all_gather(b_up, ("dp", "seq"), axis=0, tiled=True),
        lax.all_gather(b_down, ("dp", "seq"), axis=0, tiled=True),
        lax.all_gather(ffn_gain, ("dp", "seq"), axis=0, tiled=True),
        lax.all_gather(ffn_shift, ("dp", "seq"), axis=0, tiled=True),
    )
    full_query, full_key, full_value, full_out, full_up, full_down = gathered[:6]
    small_vectors = [item.astype(fl_type) for item in gathered[6:]]
    (
        bias_query,
        bias_value,
        bias_out,
        gain_one,
        shift_one,
        bias_up,
        bias_down,
        gain_two,
        shift_two,
    ) = small_vectors
    query = (project(tokens, full_query) + bias_query).astype(bf_type)
    key_rows = project(tokens, full_key).astype(bf_type)
    value_rows = (project(tokens, full_value) + bias_value).astype(bf_type)
    query_heads = query.reshape(local_seqs, local_rows, head_count, head_size)
    key_local = key_rows.reshape(local_seqs, local_rows, head_count, head_size)
    value_local = value_rows.reshape(local_seqs, local_rows, head_count, head_size)
    stat_shape = (local_seqs, head_count, local_rows)
    running_max = jnp.full(stat_shape, masked_score, fl_type)
    key_block = lax.all_gather(key_rows, "seq", axis=1, tiled=True)
    value_block = lax.all_gather(value_rows, "seq", axis=1, tiled=True)
    key_count = key_block.shape[1]
    key_heads = key_block.reshape(local_seqs, key_count, head_count, head_size)
    value_heads = value_block.reshape(local_seqs, key_count, head_count, head_size)
    scores = (
        jnp.einsum("sqhd,skhd->shqk", query_heads, key_heads, preferred_element_type=fl_type)
        * score_scale
    )
    keep_mask = key_valid(lengths, jnp.int32(0), key_count)
    new_max = jnp.maximum(running_max, jnp.max(jnp.where(keep_mask, scores, masked_score), axis=-1))
    exp_scores = jnp.where(keep_mask, jnp.exp(scores - new_max[..., None]), 0.0)
    running_sum = jnp.sum(exp_scores, axis=-1)
    update = jnp.einsum(
        "shqk,skhd->sqhd", exp_scores.astype(bf_type), value_heads, preferred_element_type=fl_type
    )
    context_sum = update
    final_max, final_sum, context_sum = (new_max, running_sum, context_sum)
    context_heads = context_sum / jnp.transpose(final_sum, (0, 2, 1))[..., None]
    log_sum = jnp.transpose(final_max + jnp.log(final_sum), (0, 2, 1))
    attn = context_heads.reshape(local_seqs, local_rows, model_width).astype(bf_type)
    resid = tokens.astype(fl_type) + project(attn, full_out) + bias_out
    first_f = layer_norm(resid, gain_one, shift_one)
    first = first_f.astype(bf_type)
    inner = project(first, full_up) + bias_up
    active = gelu_exact(inner).astype(bf_type)
    second = first.astype(fl_type) + project(active, full_down) + bias_down
    out_f, norm_two_pull = jax.vjp(layer_norm, second, gain_two, shift_two)
    out_tokens = out_f.astype(bf_type)
    back_weights = (
        lax.all_gather(w_query, ("dp", "seq"), axis=0, tiled=True),
        lax.all_gather(w_key, ("dp", "seq"), axis=0, tiled=True),
        lax.all_gather(w_value, ("dp", "seq"), axis=0, tiled=True),
        lax.all_gather(w_out, ("dp", "seq"), axis=0, tiled=True),
        lax.all_gather(w_up, ("dp", "seq"), axis=0, tiled=True),
        lax.all_gather(w_down, ("dp", "seq"), axis=0, tiled=True),
        lax.all_gather(b_query, ("dp", "seq"), axis=0, tiled=True),
        lax.all_gather(b_value, ("dp", "seq"), axis=0, tiled=True),
        lax.all_gather(b_out, ("dp", "seq"), axis=0, tiled=True),
        lax.all_gather(attn_gain, ("dp", "seq"), axis=0, tiled=True),
        lax.all_gather(attn_shift, ("dp", "seq"), axis=0, tiled=True),
        lax.all_gather(b_up, ("dp", "seq"), axis=0, tiled=True),
        lax.all_gather(b_down, ("dp", "seq"), axis=0, tiled=True),
        lax.all_gather(ffn_gain, ("dp", "seq"), axis=0, tiled=True),
        lax.all_gather(ffn_shift, ("dp", "seq"), axis=0, tiled=True),
    )
    back_query, back_key, back_value, back_out, back_up, back_down = back_weights[:6]
    d_second, ffngain_grad, ffnshift_grad = norm_two_pull(cotangent.astype(fl_type))
    d_outer = d_second.astype(bf_type)
    downbias_grad = row_total(d_outer)
    downproj_grad = outer_sum(active, d_outer)
    d_active = project_back(d_outer, back_down)
    gelu_value, gelu_pull = jax.vjp(gelu_exact, inner)
    d_inner = gelu_pull(d_active)[0].astype(bf_type)
    upbias_grad = row_total(d_inner)
    upproj_grad = outer_sum(first, d_inner)
    d_first = d_second + project_back(d_inner, back_up)
    norm_one_value, norm_one_pull = jax.vjp(layer_norm, resid, gain_one, shift_one)
    d_resid, attngain_grad, attnshift_grad = norm_one_pull(d_first)
    d_attnout = d_resid.astype(bf_type)
    outbias_grad = row_total(d_attnout)
    outproj_grad = outer_sum(attn, d_attnout)
    d_attn = project_back(d_attnout, back_out).astype(bf_type)
    d_attn_heads = d_attn.reshape(local_seqs, local_rows, head_count, head_size)
    row_delta = jnp.sum(d_attn_heads.astype(fl_type) * context_heads, axis=-1)
    lse_heads = jnp.transpose(log_sum, (0, 2, 1))
    delta_heads = jnp.transpose(row_delta, (0, 2, 1))
    key_block = lax.all_gather(key_rows, "seq", axis=1, tiled=True)
    value_block = lax.all_gather(value_rows, "seq", axis=1, tiled=True)
    key_count = key_block.shape[1]
    key_heads = key_block.reshape(local_seqs, key_count, head_count, head_size)
    value_heads = value_block.reshape(local_seqs, key_count, head_count, head_size)
    scores = (
        jnp.einsum("sqhd,skhd->shqk", query_heads, key_heads, preferred_element_type=fl_type)
        * score_scale
    )
    keep_mask = key_valid(lengths, jnp.int32(0), key_count)
    probs_block = jnp.where(keep_mask, jnp.exp(scores - lse_heads[..., None]), 0.0)
    d_probs = jnp.einsum(
        "sqhd,skhd->shqk", d_attn_heads, value_heads, preferred_element_type=fl_type
    )
    d_scores = (probs_block * (d_probs - delta_heads[..., None])).astype(bf_type)
    d_query_f = jnp.einsum("shqk,skhd->sqhd", d_scores, key_heads, preferred_element_type=fl_type)
    all_lse, all_delta = (
        lax.all_gather(log_sum, "seq", axis=1, tiled=True),
        lax.all_gather(row_delta, "seq", axis=1, tiled=True),
    )
    local_mask = key_valid(lengths, row_offset, local_rows)
    query_block = lax.all_gather(query, "seq", axis=1, tiled=True)
    grad_block = lax.all_gather(d_attn, "seq", axis=1, tiled=True)
    query_count = query_block.shape[1]
    remote_query = query_block.reshape(local_seqs, query_count, head_count, head_size)
    remote_grad = grad_block.reshape(local_seqs, query_count, head_count, head_size)
    remote_lse = jnp.transpose(all_lse, (0, 2, 1))
    remote_delta = jnp.transpose(all_delta, (0, 2, 1))
    scores = (
        jnp.einsum("sqhd,skhd->shqk", remote_query, key_local, preferred_element_type=fl_type)
        * score_scale
    )
    probs_block = jnp.where(local_mask, jnp.exp(scores - remote_lse[..., None]), 0.0)
    d_value_sum = jnp.einsum(
        "shqk,sqhd->skhd", probs_block.astype(bf_type), remote_grad, preferred_element_type=fl_type
    )
    d_probs = jnp.einsum(
        "sqhd,skhd->shqk", remote_grad, value_local, preferred_element_type=fl_type
    )
    d_scores = (probs_block * (d_probs - remote_delta[..., None])).astype(bf_type)
    d_key_sum = jnp.einsum(
        "shqk,sqhd->skhd", d_scores, remote_query, preferred_element_type=fl_type
    )
    flat_shape = (local_seqs, local_rows, model_width)
    d_query = (d_query_f * score_scale).reshape(flat_shape).astype(bf_type)
    d_key = (d_key_sum * score_scale).reshape(flat_shape).astype(bf_type)
    d_value = d_value_sum.reshape(flat_shape).astype(bf_type)
    querybias_grad = row_total(d_query)
    valuebias_grad = row_total(d_value)
    query_grad = outer_sum(tokens, d_query)
    key_grad = outer_sum(tokens, d_key)
    value_grad = outer_sum(tokens, d_value)
    grad_inputs = (
        d_resid
        + project_back(d_query, back_query)
        + project_back(d_key, back_key)
        + project_back(d_value, back_value)
    )
    shards = (
        lax.psum_scatter(query_grad, ("dp", "seq"), scatter_dimension=0, tiled=True),
        lax.psum_scatter(key_grad, ("dp", "seq"), scatter_dimension=0, tiled=True),
        lax.psum_scatter(value_grad, ("dp", "seq"), scatter_dimension=0, tiled=True),
        lax.psum_scatter(outproj_grad, ("dp", "seq"), scatter_dimension=0, tiled=True),
        lax.psum_scatter(upproj_grad, ("dp", "seq"), scatter_dimension=0, tiled=True),
        lax.psum_scatter(downproj_grad, ("dp", "seq"), scatter_dimension=0, tiled=True),
        lax.psum_scatter(querybias_grad, ("dp", "seq"), scatter_dimension=0, tiled=True),
        lax.psum_scatter(valuebias_grad, ("dp", "seq"), scatter_dimension=0, tiled=True),
        lax.psum_scatter(outbias_grad, ("dp", "seq"), scatter_dimension=0, tiled=True),
        lax.psum_scatter(attngain_grad, ("dp", "seq"), scatter_dimension=0, tiled=True),
        lax.psum_scatter(attnshift_grad, ("dp", "seq"), scatter_dimension=0, tiled=True),
        lax.psum_scatter(upbias_grad, ("dp", "seq"), scatter_dimension=0, tiled=True),
        lax.psum_scatter(downbias_grad, ("dp", "seq"), scatter_dimension=0, tiled=True),
        lax.psum_scatter(ffngain_grad, ("dp", "seq"), scatter_dimension=0, tiled=True),
        lax.psum_scatter(ffnshift_grad, ("dp", "seq"), scatter_dimension=0, tiled=True),
    )
    return (
        out_tokens,
        grad_inputs.astype(bf_type),
        shards[0],
        shards[1],
        shards[2],
        shards[3],
        shards[4],
        shards[5],
        shards[6],
        shards[7],
        shards[8],
        shards[9],
        shards[10],
        shards[11],
        shards[12],
        shards[13],
        shards[14],
    )


BOTH = ("dp", "seq")
SMALL_ROWS = 8


def exchange(values, axis, split, join):
    return lax.all_to_all(values, axis, split_axis=split, concat_axis=join, tiled=True)


def local_heads(
    dp_size,
    seq_size,
    tokens,
    lengths,
    w_query,
    w_key,
    w_value,
    w_out,
    w_up,
    w_down,
    b_query,
    b_value,
    b_out,
    attn_gain,
    attn_shift,
    b_up,
    b_down,
    ffn_gain,
    ffn_shift,
    cotangent,
):
    bf_type = jnp.bfloat16
    fl_type = jnp.float32
    count = dp_size * seq_size
    seqs, rows, width = tokens.shape
    full_rows = rows * seq_size
    own_rows = w_query.shape[0]
    own_units = w_down.shape[0]
    head_size = width // HEADS
    own_heads = HEADS // seq_size
    columns = own_heads * head_size
    seq_at = lax.axis_index("seq")

    stacked = jnp.stack((w_query, w_key, w_value), axis=1).reshape(own_rows, 3, seq_size, columns)
    by_owner = jnp.transpose(stacked, (2, 0, 1, 3)).reshape(seq_size, own_rows, 3 * columns)
    vectors = (b_up, b_query, b_value, b_out, attn_gain, attn_shift, b_down, ffn_gain, ffn_shift)
    small_own = jnp.concatenate(vectors)
    small_room = SMALL_ROWS * 3 * columns
    small_block = jnp.pad(small_own, (0, small_room - small_own.shape[0])).reshape(SMALL_ROWS, 3 * columns)
    payload = jnp.concatenate(
        (by_owner, jnp.broadcast_to(small_block[None], (seq_size, SMALL_ROWS, 3 * columns))), axis=1
    )
    payload = jnp.broadcast_to(payload[None], (dp_size,) + payload.shape)
    payload = payload.reshape(count, own_rows + SMALL_ROWS, 3 * columns)
    arrived = exchange(payload, BOTH, 0, 0)
    head_weights = arrived[:, :own_rows].reshape(width, 3 * columns)
    small_all = arrived[:, own_rows:].reshape(count, small_room)
    full_vectors = []
    at = 0
    for item in vectors:
        size = item.shape[0]
        full_vectors.append(small_all[:, at : at + size].reshape(count * size).astype(fl_type))
        at += size
    (
        bias_up,
        bias_query,
        bias_value,
        bias_out,
        gain_one,
        shift_one,
        bias_down,
        gain_two,
        shift_two,
    ) = full_vectors

    all_tokens = lax.all_gather(tokens, "seq", axis=1, tiled=True)
    out_up = lax.all_gather(jnp.concatenate((w_out, w_up), axis=1), BOTH, axis=0, tiled=True)
    full_out, full_up = out_up[:, :width], out_up[:, width:]
    full_down = lax.all_gather(w_down, BOTH, axis=0, tiled=True)
    full_qkv = lax.all_gather(jnp.concatenate((w_query, w_key, w_value), axis=1), BOTH, axis=0, tiled=True)

    own_bias = jnp.concatenate(
        (
            lax.dynamic_slice_in_dim(bias_query, seq_at * columns, columns),
            jnp.zeros((columns,), fl_type),
            lax.dynamic_slice_in_dim(bias_value, seq_at * columns, columns),
        )
    )
    mixed = (project(all_tokens, head_weights) + own_bias).astype(bf_type)
    mixed = mixed.reshape(seqs, full_rows, 3, own_heads, head_size)
    query, keys, values = mixed[:, :, 0], mixed[:, :, 1], mixed[:, :, 2]
    keep = key_valid(lengths, jnp.int32(0), full_rows)
    scores = jnp.einsum("sqhd,skhd->shqk", query, keys, preferred_element_type=fl_type) * score_scale
    row_max = jnp.max(jnp.where(keep, scores, masked_score), axis=-1)
    exps = jnp.where(keep, jnp.exp(scores - row_max[..., None]), 0.0)
    row_sum = jnp.sum(exps, axis=-1)
    context = jnp.einsum("shqk,skhd->sqhd", exps.astype(bf_type), values, preferred_element_type=fl_type)
    context = context / jnp.transpose(row_sum, (0, 2, 1))[..., None]
    log_sum = row_max + jnp.log(row_sum)
    attn = exchange(context.reshape(seqs, full_rows, columns).astype(bf_type), "seq", 1, 2)

    resid = tokens.astype(fl_type) + project(attn, full_out) + bias_out
    first = layer_norm(resid, gain_one, shift_one).astype(bf_type)
    inner = project(first, full_up) + bias_up
    active = gelu_exact(inner).astype(bf_type)
    second = first.astype(fl_type) + project(active, full_down) + bias_down
    out_f, norm_two_pull = jax.vjp(layer_norm, second, gain_two, shift_two)
    out_tokens = out_f.astype(bf_type)

    d_second, ffngain_grad, ffnshift_grad = norm_two_pull(cotangent.astype(fl_type))
    d_outer = d_second.astype(bf_type)
    downbias_grad = row_total(d_outer)
    downproj_grad = outer_sum(active, d_outer)
    d_active = project_back(d_outer, full_down)
    gelu_value, gelu_pull = jax.vjp(gelu_exact, inner)
    d_inner = gelu_pull(d_active)[0].astype(bf_type)
    upbias_grad = row_total(d_inner)
    upproj_grad = outer_sum(first, d_inner)
    d_first = d_second + project_back(d_inner, full_up)
    norm_one_value, norm_one_pull = jax.vjp(layer_norm, resid, gain_one, shift_one)
    d_resid, attngain_grad, attnshift_grad = norm_one_pull(d_first)
    d_attnout = d_resid.astype(bf_type)
    outbias_grad = row_total(d_attnout)
    outproj_grad = outer_sum(attn, d_attnout)
    d_attn_rows = project_back(d_attnout, full_out).astype(bf_type)

    down_shard = lax.psum_scatter(downproj_grad.astype(bf_type), BOTH, scatter_dimension=0, tiled=True)
    outup_grad = jnp.concatenate((outproj_grad.astype(bf_type), upproj_grad.astype(bf_type)), axis=1)
    outup_shard = lax.psum_scatter(outup_grad, BOTH, scatter_dimension=0, tiled=True).astype(fl_type)

    d_attn = exchange(d_attn_rows, "seq", 2, 1).reshape(seqs, full_rows, own_heads, head_size)
    delta = jnp.transpose(jnp.sum(d_attn.astype(fl_type) * context, axis=-1), (0, 2, 1))
    scores = jnp.einsum("sqhd,skhd->shqk", query, keys, preferred_element_type=fl_type) * score_scale
    probs = jnp.where(keep, jnp.exp(scores - log_sum[..., None]), 0.0)
    d_probs = jnp.einsum("sqhd,skhd->shqk", d_attn, values, preferred_element_type=fl_type)
    d_scores = (probs * (d_probs - delta[..., None])).astype(bf_type)
    d_query = jnp.einsum("shqk,skhd->sqhd", d_scores, keys, preferred_element_type=fl_type) * score_scale
    d_keys = jnp.einsum("shqk,sqhd->skhd", d_scores, query, preferred_element_type=fl_type) * score_scale
    d_values = jnp.einsum("shqk,sqhd->skhd", probs.astype(bf_type), d_attn, preferred_element_type=fl_type)
    d_mixed = jnp.stack((d_query, d_keys, d_values), axis=2).astype(bf_type)
    d_mixed = d_mixed.reshape(seqs, full_rows, 3 * columns)

    mixed_grad = outer_sum(all_tokens, d_mixed).astype(bf_type).reshape(count, own_rows, 3 * columns)
    bias_mixed = row_total(d_mixed)
    empty = jnp.zeros((width,), fl_type)
    querybias_grad = lax.dynamic_update_slice_in_dim(empty, bias_mixed[:columns], seq_at * columns, 0)
    valuebias_grad = lax.dynamic_update_slice_in_dim(empty, bias_mixed[2 * columns :], seq_at * columns, 0)
    vector_grads = (
        upbias_grad,
        querybias_grad,
        valuebias_grad,
        outbias_grad,
        attngain_grad,
        attnshift_grad,
        downbias_grad,
        ffngain_grad,
        ffnshift_grad,
    )
    small_grads = jnp.concatenate([item.reshape(count, -1) for item in vector_grads], axis=1)
    small_size = small_grads.shape[1]
    small_grads = jnp.pad(small_grads, ((0, 0), (0, small_room - small_size)))
    small_grads = small_grads.reshape(count, SMALL_ROWS, 3 * columns).astype(bf_type)
    arrived = exchange(jnp.concatenate((mixed_grad, small_grads), axis=1), BOTH, 0, 0).astype(fl_type)
    qkv_shard = jnp.sum(arrived[:, :own_rows].reshape(dp_size, seq_size, own_rows, 3, columns), axis=0)
    qkv_shard = jnp.transpose(qkv_shard, (2, 1, 0, 3)).reshape(3, own_rows, width)
    small_sums = jnp.sum(arrived[:, own_rows:], axis=0).reshape(small_room)
    vector_shards = []
    at = 0
    for item in vectors:
        vector_shards.append(small_sums[at : at + item.shape[0]])
        at += item.shape[0]

    d_rows = exchange(d_mixed.reshape(seqs, full_rows, 3, columns), "seq", 1, 3)
    d_rows = d_rows.reshape(seqs, rows, 3 * width)
    grad_inputs = d_resid + project_back(d_rows, full_qkv)
    return (
        out_tokens,
        grad_inputs.astype(bf_type),
        qkv_shard[0],
        qkv_shard[1],
        qkv_shard[2],
        outup_shard[:, :width],
        outup_shard[:, width:],
        down_shard.astype(fl_type),
        vector_shards[1],
        vector_shards[2],
        vector_shards[3],
        vector_shards[4],
        vector_shards[5],
        vector_shards[0],
        vector_shards[6],
        vector_shards[7],
        vector_shards[8],
    )


def solution(mesh):
    seq_size = mesh.shape["seq"]
    by_heads = HEADS % seq_size == 0
    body = functools.partial(local_heads, mesh.shape["dp"], seq_size) if by_heads else local_gathered
    return jax.shard_map(
        body,
        mesh=mesh,
        in_specs=(
            P("dp", "seq", None),
            P("dp"),
            P(("dp", "seq"), None),
            P(("dp", "seq"), None),
            P(("dp", "seq"), None),
            P(("dp", "seq"), None),
            P(("dp", "seq"), None),
            P(("dp", "seq"), None),
            P(("dp", "seq")),
            P(("dp", "seq")),
            P(("dp", "seq")),
            P(("dp", "seq")),
            P(("dp", "seq")),
            P(("dp", "seq")),
            P(("dp", "seq")),
            P(("dp", "seq")),
            P(("dp", "seq")),
            P("dp", "seq", None),
        ),
        out_specs=(
            P("dp", "seq", None),
            P("dp", "seq", None),
            P(("dp", "seq"), None),
            P(("dp", "seq"), None),
            P(("dp", "seq"), None),
            P(("dp", "seq"), None),
            P(("dp", "seq"), None),
            P(("dp", "seq"), None),
            P(("dp", "seq")),
            P(("dp", "seq")),
            P(("dp", "seq")),
            P(("dp", "seq")),
            P(("dp", "seq")),
            P(("dp", "seq")),
            P(("dp", "seq")),
            P(("dp", "seq")),
            P(("dp", "seq")),
        ),
        check_vma=False,
    )
```

```python
import functools

import jax
import jax.numpy as jnp
from jax import lax
from jax.sharding import PartitionSpec as P

HEADS = 16


score_scale = 0.125
epsilon = 1e-05
masked_score = -1e30


def layer_norm(values, gain, shift):
    average = jnp.mean(values, axis=-1, keepdims=True)
    centred = values - average
    variance = jnp.mean(centred * centred, axis=-1, keepdims=True)
    return centred * lax.rsqrt(variance + epsilon) * gain + shift


def gelu_exact(values):
    return jax.nn.gelu(values, approximate=False)


def project(values, weight):
    return jnp.einsum("srd,de->sre", values, weight, preferred_element_type=jnp.float32)


def project_back(grads, weight):
    return jnp.einsum("sre,de->srd", grads, weight, preferred_element_type=jnp.float32)


def outer_sum(values, grads):
    return jnp.einsum("srd,sre->de", values, grads, preferred_element_type=jnp.float32)


def row_total(grads):
    return jnp.sum(grads.astype(jnp.float32), axis=(0, 1))


def key_valid(lengths, first_index, key_count):
    places = first_index + jnp.arange(key_count, dtype=jnp.int32)
    return (places[None, :] < lengths[:, None])[:, None, None, :]


def local_gathered(
    tokens,
    lengths,
    w_query,
    w_key,
    w_value,
    w_out,
    w_up,
    w_down,
    b_query,
    b_value,
    b_out,
    attn_gain,
    attn_shift,
    b_up,
    b_down,
    ffn_gain,
    ffn_shift,
    cotangent,
):
    local_seqs, local_rows, model_width = tokens.shape
    head_count = HEADS
    head_size = model_width // head_count
    row_offset = lax.axis_index("seq") * local_rows
    bf_type = jnp.bfloat16
    fl_type = jnp.float32
    gathered = (
        lax.all_gather(w_query, ("dp", "seq"), axis=0, tiled=True),
        lax.all_gather(w_key, ("dp", "seq"), axis=0, tiled=True),
        lax.all_gather(w_value, ("dp", "seq"), axis=0, tiled=True),
        lax.all_gather(w_out, ("dp", "seq"), axis=0, tiled=True),
        lax.all_gather(w_up, ("dp", "seq"), axis=0, tiled=True),
        lax.all_gather(w_down, ("dp", "seq"), axis=0, tiled=True),
        lax.all_gather(b_query, ("dp", "seq"), axis=0, tiled=True),
        lax.all_gather(b_value, ("dp", "seq"), axis=0, tiled=True),
        lax.all_gather(b_out, ("dp", "seq"), axis=0, tiled=True),
        lax.all_gather(attn_gain, ("dp", "seq"), axis=0, tiled=True),
        lax.all_gather(attn_shift, ("dp", "seq"), axis=0, tiled=True),
        lax.all_gather(b_up, ("dp", "seq"), axis=0, tiled=True),
        lax.all_gather(b_down, ("dp", "seq"), axis=0, tiled=True),
        lax.all_gather(ffn_gain, ("dp", "seq"), axis=0, tiled=True),
        lax.all_gather(ffn_shift, ("dp", "seq"), axis=0, tiled=True),
    )
    full_query, full_key, full_value, full_out, full_up, full_down = gathered[:6]
    small_vectors = [item.astype(fl_type) for item in gathered[6:]]
    (
        bias_query,
        bias_value,
        bias_out,
        gain_one,
        shift_one,
        bias_up,
        bias_down,
        gain_two,
        shift_two,
    ) = small_vectors
    query = (project(tokens, full_query) + bias_query).astype(bf_type)
    key_rows = project(tokens, full_key).astype(bf_type)
    value_rows = (project(tokens, full_value) + bias_value).astype(bf_type)
    query_heads = query.reshape(local_seqs, local_rows, head_count, head_size)
    key_local = key_rows.reshape(local_seqs, local_rows, head_count, head_size)
    value_local = value_rows.reshape(local_seqs, local_rows, head_count, head_size)
    stat_shape = (local_seqs, head_count, local_rows)
    running_max = jnp.full(stat_shape, masked_score, fl_type)
    key_block = lax.all_gather(key_rows, "seq", axis=1, tiled=True)
    value_block = lax.all_gather(value_rows, "seq", axis=1, tiled=True)
    key_count = key_block.shape[1]
    key_heads = key_block.reshape(local_seqs, key_count, head_count, head_size)
    value_heads = value_block.reshape(local_seqs, key_count, head_count, head_size)
    scores = (
        jnp.einsum("sqhd,skhd->shqk", query_heads, key_heads, preferred_element_type=fl_type)
        * score_scale
    )
    keep_mask = key_valid(lengths, jnp.int32(0), key_count)
    new_max = jnp.maximum(running_max, jnp.max(jnp.where(keep_mask, scores, masked_score), axis=-1))
    exp_scores = jnp.where(keep_mask, jnp.exp(scores - new_max[..., None]), 0.0)
    running_sum = jnp.sum(exp_scores, axis=-1)
    update = jnp.einsum(
        "shqk,skhd->sqhd", exp_scores.astype(bf_type), value_heads, preferred_element_type=fl_type
    )
    context_sum = update
    final_max, final_sum, context_sum = (new_max, running_sum, context_sum)
    context_heads = context_sum / jnp.transpose(final_sum, (0, 2, 1))[..., None]
    log_sum = jnp.transpose(final_max + jnp.log(final_sum), (0, 2, 1))
    attn = context_heads.reshape(local_seqs, local_rows, model_width).astype(bf_type)
    resid = tokens.astype(fl_type) + project(attn, full_out) + bias_out
    first_f = layer_norm(resid, gain_one, shift_one)
    first = first_f.astype(bf_type)
    inner = project(first, full_up) + bias_up
    active = gelu_exact(inner).astype(bf_type)
    second = first.astype(fl_type) + project(active, full_down) + bias_down
    out_f, norm_two_pull = jax.vjp(layer_norm, second, gain_two, shift_two)
    out_tokens = out_f.astype(bf_type)
    back_weights = (
        lax.all_gather(w_query, ("dp", "seq"), axis=0, tiled=True),
        lax.all_gather(w_key, ("dp", "seq"), axis=0, tiled=True),
        lax.all_gather(w_value, ("dp", "seq"), axis=0, tiled=True),
        lax.all_gather(w_out, ("dp", "seq"), axis=0, tiled=True),
        lax.all_gather(w_up, ("dp", "seq"), axis=0, tiled=True),
        lax.all_gather(w_down, ("dp", "seq"), axis=0, tiled=True),
        lax.all_gather(b_query, ("dp", "seq"), axis=0, tiled=True),
        lax.all_gather(b_value, ("dp", "seq"), axis=0, tiled=True),
        lax.all_gather(b_out, ("dp", "seq"), axis=0, tiled=True),
        lax.all_gather(attn_gain, ("dp", "seq"), axis=0, tiled=True),
        lax.all_gather(attn_shift, ("dp", "seq"), axis=0, tiled=True),
        lax.all_gather(b_up, ("dp", "seq"), axis=0, tiled=True),
        lax.all_gather(b_down, ("dp", "seq"), axis=0, tiled=True),
        lax.all_gather(ffn_gain, ("dp", "seq"), axis=0, tiled=True),
        lax.all_gather(ffn_shift, ("dp", "seq"), axis=0, tiled=True),
    )
    back_query, back_key, back_value, back_out, back_up, back_down = back_weights[:6]
    d_second, ffngain_grad, ffnshift_grad = norm_two_pull(cotangent.astype(fl_type))
    d_outer = d_second.astype(bf_type)
    downbias_grad = row_total(d_outer)
    downproj_grad = outer_sum(active, d_outer)
    d_active = project_back(d_outer, back_down)
    gelu_value, gelu_pull = jax.vjp(gelu_exact, inner)
    d_inner = gelu_pull(d_active)[0].astype(bf_type)
    upbias_grad = row_total(d_inner)
    upproj_grad = outer_sum(first, d_inner)
    d_first = d_second + project_back(d_inner, back_up)
    norm_one_value, norm_one_pull = jax.vjp(layer_norm, resid, gain_one, shift_one)
    d_resid, attngain_grad, attnshift_grad = norm_one_pull(d_first)
    d_attnout = d_resid.astype(bf_type)
    outbias_grad = row_total(d_attnout)
    outproj_grad = outer_sum(attn, d_attnout)
    d_attn = project_back(d_attnout, back_out).astype(bf_type)
    d_attn_heads = d_attn.reshape(local_seqs, local_rows, head_count, head_size)
    row_delta = jnp.sum(d_attn_heads.astype(fl_type) * context_heads, axis=-1)
    lse_heads = jnp.transpose(log_sum, (0, 2, 1))
    delta_heads = jnp.transpose(row_delta, (0, 2, 1))
    key_block = lax.all_gather(key_rows, "seq", axis=1, tiled=True)
    value_block = lax.all_gather(value_rows, "seq", axis=1, tiled=True)
    key_count = key_block.shape[1]
    key_heads = key_block.reshape(local_seqs, key_count, head_count, head_size)
    value_heads = value_block.reshape(local_seqs, key_count, head_count, head_size)
    scores = (
        jnp.einsum("sqhd,skhd->shqk", query_heads, key_heads, preferred_element_type=fl_type)
        * score_scale
    )
    keep_mask = key_valid(lengths, jnp.int32(0), key_count)
    probs_block = jnp.where(keep_mask, jnp.exp(scores - lse_heads[..., None]), 0.0)
    d_probs = jnp.einsum(
        "sqhd,skhd->shqk", d_attn_heads, value_heads, preferred_element_type=fl_type
    )
    d_scores = (probs_block * (d_probs - delta_heads[..., None])).astype(bf_type)
    d_query_f = jnp.einsum("shqk,skhd->sqhd", d_scores, key_heads, preferred_element_type=fl_type)
    all_lse, all_delta = (
        lax.all_gather(log_sum, "seq", axis=1, tiled=True),
        lax.all_gather(row_delta, "seq", axis=1, tiled=True),
    )
    local_mask = key_valid(lengths, row_offset, local_rows)
    query_block = lax.all_gather(query, "seq", axis=1, tiled=True)
    grad_block = lax.all_gather(d_attn, "seq", axis=1, tiled=True)
    query_count = query_block.shape[1]
    remote_query = query_block.reshape(local_seqs, query_count, head_count, head_size)
    remote_grad = grad_block.reshape(local_seqs, query_count, head_count, head_size)
    remote_lse = jnp.transpose(all_lse, (0, 2, 1))
    remote_delta = jnp.transpose(all_delta, (0, 2, 1))
    scores = (
        jnp.einsum("sqhd,skhd->shqk", remote_query, key_local, preferred_element_type=fl_type)
        * score_scale
    )
    probs_block = jnp.where(local_mask, jnp.exp(scores - remote_lse[..., None]), 0.0)
    d_value_sum = jnp.einsum(
        "shqk,sqhd->skhd", probs_block.astype(bf_type), remote_grad, preferred_element_type=fl_type
    )
    d_probs = jnp.einsum(
        "sqhd,skhd->shqk", remote_grad, value_local, preferred_element_type=fl_type
    )
    d_scores = (probs_block * (d_probs - remote_delta[..., None])).astype(bf_type)
    d_key_sum = jnp.einsum(
        "shqk,sqhd->skhd", d_scores, remote_query, preferred_element_type=fl_type
    )
    flat_shape = (local_seqs, local_rows, model_width)
    d_query = (d_query_f * score_scale).reshape(flat_shape).astype(bf_type)
    d_key = (d_key_sum * score_scale).reshape(flat_shape).astype(bf_type)
    d_value = d_value_sum.reshape(flat_shape).astype(bf_type)
    querybias_grad = row_total(d_query)
    valuebias_grad = row_total(d_value)
    query_grad = outer_sum(tokens, d_query)
    key_grad = outer_sum(tokens, d_key)
    value_grad = outer_sum(tokens, d_value)
    grad_inputs = (
        d_resid
        + project_back(d_query, back_query)
        + project_back(d_key, back_key)
        + project_back(d_value, back_value)
    )
    shards = (
        lax.psum_scatter(query_grad, ("dp", "seq"), scatter_dimension=0, tiled=True),
        lax.psum_scatter(key_grad, ("dp", "seq"), scatter_dimension=0, tiled=True),
        lax.psum_scatter(value_grad, ("dp", "seq"), scatter_dimension=0, tiled=True),
        lax.psum_scatter(outproj_grad, ("dp", "seq"), scatter_dimension=0, tiled=True),
        lax.psum_scatter(upproj_grad, ("dp", "seq"), scatter_dimension=0, tiled=True),
        lax.psum_scatter(downproj_grad, ("dp", "seq"), scatter_dimension=0, tiled=True),
        lax.psum_scatter(querybias_grad, ("dp", "seq"), scatter_dimension=0, tiled=True),
        lax.psum_scatter(valuebias_grad, ("dp", "seq"), scatter_dimension=0, tiled=True),
        lax.psum_scatter(outbias_grad, ("dp", "seq"), scatter_dimension=0, tiled=True),
        lax.psum_scatter(attngain_grad, ("dp", "seq"), scatter_dimension=0, tiled=True),
        lax.psum_scatter(attnshift_grad, ("dp", "seq"), scatter_dimension=0, tiled=True),
        lax.psum_scatter(upbias_grad, ("dp", "seq"), scatter_dimension=0, tiled=True),
        lax.psum_scatter(downbias_grad, ("dp", "seq"), scatter_dimension=0, tiled=True),
        lax.psum_scatter(ffngain_grad, ("dp", "seq"), scatter_dimension=0, tiled=True),
        lax.psum_scatter(ffnshift_grad, ("dp", "seq"), scatter_dimension=0, tiled=True),
    )
    return (
        out_tokens,
        grad_inputs.astype(bf_type),
        shards[0],
        shards[1],
        shards[2],
        shards[3],
        shards[4],
        shards[5],
        shards[6],
        shards[7],
        shards[8],
        shards[9],
        shards[10],
        shards[11],
        shards[12],
        shards[13],
        shards[14],
    )


BOTH = ("dp", "seq")
SMALL_ROWS = 8


def exchange(values, axis, split, join):
    return lax.all_to_all(values, axis, split_axis=split, concat_axis=join, tiled=True)


def pick(values, at, axis):
    return lax.dynamic_index_in_dim(values, at, axis, keepdims=False)


def swap(values, count, flip):
    return lax.ppermute(values, BOTH, [(source, source ^ flip) for source in range(count)])


def add_rounded(left, right):
    return (left.astype(jnp.float32) + right.astype(jnp.float32)).astype(jnp.bfloat16)


def halve(values, axis, at, count, flip):
    other = swap(pick(values, 1 - at, axis), count, flip)
    return add_rounded(pick(values, at, axis), other)


def tie(*values):
    return lax.optimization_barrier(values)


class Scatter:
    def __init__(self, dp_size, seq_size):
        self.count, self.near, self.far = dp_size * seq_size, seq_size, 2 * seq_size
        self.lines = seq_size // 2
        dp_at, seq_at = lax.axis_index("dp"), lax.axis_index("seq")
        self.core, self.line = seq_at % 2, seq_at // 2
        self.side, self.deep = dp_at % 2, dp_at // 2

    def cores(self, terms):
        rows = terms.shape[0] // self.count
        blocks = terms.reshape(2, 2, self.lines, 2, rows, terms.shape[1])
        return halve(blocks, 3, self.core, self.count, 1)

    def plane_one(self, blocks):
        half = blocks.shape[3] // 2
        one = halve(blocks[..., :half, :], 1, self.side, self.count, self.near)
        two = halve(blocks[..., half:, :], 0, self.deep, self.count, self.far)
        return one, two

    def plane_two(self, one, two):
        one = halve(one, 0, self.deep, self.count, self.far)
        two = halve(two, 0, self.side, self.count, self.near)
        return jnp.concatenate((one, two), axis=1)

    def line_sum(self, both):
        total = pick(both, self.line, 0).astype(jnp.float32)
        for step in range(1, self.lines):
            other = swap(pick(both, self.line ^ step, 0), self.count, 2 * step)
            total = total + other.astype(jnp.float32)
        return total


def local_heads(
    dp_size,
    seq_size,
    tokens,
    lengths,
    w_query,
    w_key,
    w_value,
    w_out,
    w_up,
    w_down,
    b_query,
    b_value,
    b_out,
    attn_gain,
    attn_shift,
    b_up,
    b_down,
    ffn_gain,
    ffn_shift,
    cotangent,
):
    bf_type = jnp.bfloat16
    fl_type = jnp.float32
    count = dp_size * seq_size
    seqs, rows, width = tokens.shape
    full_rows = rows * seq_size
    own_rows = w_query.shape[0]
    own_units = w_down.shape[0]
    head_size = width // HEADS
    own_heads = HEADS // seq_size
    columns = own_heads * head_size
    seq_at = lax.axis_index("seq")

    stacked = jnp.stack((w_query, w_key, w_value), axis=1).reshape(own_rows, 3, seq_size, columns)
    by_owner = jnp.transpose(stacked, (2, 0, 1, 3)).reshape(seq_size, own_rows, 3 * columns)
    vectors = (b_up, b_query, b_value, b_out, attn_gain, attn_shift, b_down, ffn_gain, ffn_shift)
    small_own = jnp.concatenate(vectors)
    small_room = SMALL_ROWS * 3 * columns
    small_block = jnp.pad(small_own, (0, small_room - small_own.shape[0])).reshape(SMALL_ROWS, 3 * columns)
    payload = jnp.concatenate(
        (by_owner, jnp.broadcast_to(small_block[None], (seq_size, SMALL_ROWS, 3 * columns))), axis=1
    )
    payload = jnp.broadcast_to(payload[None], (dp_size,) + payload.shape)
    payload = payload.reshape(count, own_rows + SMALL_ROWS, 3 * columns)
    arrived = exchange(payload, BOTH, 0, 0)
    head_weights = arrived[:, :own_rows].reshape(width, 3 * columns)
    small_all = arrived[:, own_rows:].reshape(count, small_room)
    full_vectors = []
    at = 0
    for item in vectors:
        size = item.shape[0]
        full_vectors.append(small_all[:, at : at + size].reshape(count * size).astype(fl_type))
        at += size
    (
        bias_up,
        bias_query,
        bias_value,
        bias_out,
        gain_one,
        shift_one,
        bias_down,
        gain_two,
        shift_two,
    ) = full_vectors

    all_tokens = lax.all_gather(tokens, "seq", axis=1, tiled=True)
    out_up = lax.all_gather(jnp.concatenate((w_out, w_up), axis=1), BOTH, axis=0, tiled=True)
    full_out, full_up = out_up[:, :width], out_up[:, width:]
    full_down = lax.all_gather(w_down, BOTH, axis=0, tiled=True)
    full_qkv = lax.all_gather(jnp.concatenate((w_query, w_key, w_value), axis=1), BOTH, axis=0, tiled=True)

    own_bias = jnp.concatenate(
        (
            lax.dynamic_slice_in_dim(bias_query, seq_at * columns, columns),
            jnp.zeros((columns,), fl_type),
            lax.dynamic_slice_in_dim(bias_value, seq_at * columns, columns),
        )
    )
    mixed = (project(all_tokens, head_weights) + own_bias).astype(bf_type)
    mixed = mixed.reshape(seqs, full_rows, 3, own_heads, head_size)
    query, keys, values = mixed[:, :, 0], mixed[:, :, 1], mixed[:, :, 2]
    keep = key_valid(lengths, jnp.int32(0), full_rows)
    scores = jnp.einsum("sqhd,skhd->shqk", query, keys, preferred_element_type=fl_type) * score_scale
    row_max = jnp.max(jnp.where(keep, scores, masked_score), axis=-1)
    exps = jnp.where(keep, jnp.exp(scores - row_max[..., None]), 0.0)
    row_sum = jnp.sum(exps, axis=-1)
    context = jnp.einsum("shqk,skhd->sqhd", exps.astype(bf_type), values, preferred_element_type=fl_type)
    context = context / jnp.transpose(row_sum, (0, 2, 1))[..., None]
    log_sum = row_max + jnp.log(row_sum)
    attn = exchange(context.reshape(seqs, full_rows, columns).astype(bf_type), "seq", 1, 2)

    resid = tokens.astype(fl_type) + project(attn, full_out) + bias_out
    first = layer_norm(resid, gain_one, shift_one).astype(bf_type)
    inner = project(first, full_up) + bias_up
    active = gelu_exact(inner).astype(bf_type)
    second = first.astype(fl_type) + project(active, full_down) + bias_down
    out_f, norm_two_pull = jax.vjp(layer_norm, second, gain_two, shift_two)
    out_tokens = out_f.astype(bf_type)

    scatter = Scatter(dp_size, seq_size)
    d_second, ffngain_grad, ffnshift_grad = norm_two_pull(cotangent.astype(fl_type))
    d_outer = d_second.astype(bf_type)
    downbias_grad = row_total(d_outer)
    down_terms = scatter.cores(outer_sum(active, d_outer).astype(bf_type))
    d_active = project_back(d_outer, full_down)
    gelu_value, gelu_pull = jax.vjp(gelu_exact, inner)
    d_inner = gelu_pull(d_active)[0].astype(bf_type)
    d_inner, down_terms = tie(d_inner, down_terms)
    down_one, down_two = scatter.plane_one(down_terms)
    upbias_grad = row_total(d_inner)
    upproj_grad = outer_sum(first, d_inner)
    d_first = d_second + project_back(d_inner, full_up)
    norm_one_value, norm_one_pull = jax.vjp(layer_norm, resid, gain_one, shift_one)
    d_resid, attngain_grad, attnshift_grad = norm_one_pull(d_first)
    d_attnout = d_resid.astype(bf_type)
    outbias_grad = row_total(d_attnout)
    outproj_grad = outer_sum(attn, d_attnout)
    d_attn_rows = project_back(d_attnout, full_out).astype(bf_type)
    outup_grad = jnp.concatenate((outproj_grad.astype(bf_type), upproj_grad.astype(bf_type)), axis=1)
    outup_terms = scatter.cores(outup_grad)

    d_attn = exchange(d_attn_rows, "seq", 2, 1).reshape(seqs, full_rows, own_heads, head_size)
    d_attn, outup_terms, full_qkv = tie(d_attn, outup_terms, full_qkv)
    outup_one, outup_two = scatter.plane_one(outup_terms)

    def attention_back(at, grad):
        part = slice(at, at + 1)
        query_s, keys_s, values_s, keep_s = query[part], keys[part], values[part], keep[part]
        delta = jnp.transpose(jnp.sum(grad.astype(fl_type) * context[part], axis=-1), (0, 2, 1))
        scores = jnp.einsum("sqhd,skhd->shqk", query_s, keys_s, preferred_element_type=fl_type) * score_scale
        probs = jnp.where(keep_s, jnp.exp(scores - log_sum[part][..., None]), 0.0)
        d_probs = jnp.einsum("sqhd,skhd->shqk", grad, values_s, preferred_element_type=fl_type)
        d_scores = (probs * (d_probs - delta[..., None])).astype(bf_type)
        d_query = jnp.einsum("shqk,skhd->sqhd", d_scores, keys_s, preferred_element_type=fl_type) * score_scale
        d_keys = jnp.einsum("shqk,sqhd->skhd", d_scores, query_s, preferred_element_type=fl_type) * score_scale
        d_values = jnp.einsum("shqk,sqhd->skhd", probs.astype(bf_type), grad, preferred_element_type=fl_type)
        d_mixed = jnp.stack((d_query, d_keys, d_values), axis=2).astype(bf_type)
        return d_mixed.reshape(1, full_rows, 3 * columns)

    def to_rows(d_mixed):
        spread = exchange(d_mixed.reshape(1, full_rows, 3, columns), "seq", 1, 3)
        return spread.reshape(1, rows, 3 * width)

    d_parts, d_rows = [], []
    for at in range(seqs):
        d_parts.append(attention_back(at, d_attn[at : at + 1]))
        d_rows.append(to_rows(d_parts[-1]))
        if at == 0:
            d_attn, down_one, down_two = tie(d_attn, down_one, down_two)
            down_both = scatter.plane_two(down_one, down_two)
    d_mixed = jnp.concatenate(d_parts, axis=0)
    d_mixed, down_both, outup_one, outup_two = tie(d_mixed, down_both, outup_one, outup_two)
    down_shard = scatter.line_sum(down_both)
    outup_both = scatter.plane_two(outup_one, outup_two)
    outup_shard = scatter.line_sum(outup_both)

    mixed_grad = outer_sum(all_tokens, d_mixed).astype(bf_type).reshape(count, own_rows, 3 * columns)
    bias_mixed = row_total(d_mixed)
    empty = jnp.zeros((width,), fl_type)
    querybias_grad = lax.dynamic_update_slice_in_dim(empty, bias_mixed[:columns], seq_at * columns, 0)
    valuebias_grad = lax.dynamic_update_slice_in_dim(empty, bias_mixed[2 * columns :], seq_at * columns, 0)
    vector_grads = (
        upbias_grad,
        querybias_grad,
        valuebias_grad,
        outbias_grad,
        attngain_grad,
        attnshift_grad,
        downbias_grad,
        ffngain_grad,
        ffnshift_grad,
    )
    small_grads = jnp.concatenate([item.reshape(count, -1) for item in vector_grads], axis=1)
    small_size = small_grads.shape[1]
    small_grads = jnp.pad(small_grads, ((0, 0), (0, small_room - small_size)))
    small_grads = small_grads.reshape(count, SMALL_ROWS, 3 * columns).astype(bf_type)
    arrived = exchange(jnp.concatenate((mixed_grad, small_grads), axis=1), BOTH, 0, 0).astype(fl_type)
    qkv_shard = jnp.sum(arrived[:, :own_rows].reshape(dp_size, seq_size, own_rows, 3, columns), axis=0)
    qkv_shard = jnp.transpose(qkv_shard, (2, 1, 0, 3)).reshape(3, own_rows, width)
    small_sums = jnp.sum(arrived[:, own_rows:], axis=0).reshape(small_room)
    vector_shards = []
    at = 0
    for item in vectors:
        vector_shards.append(small_sums[at : at + item.shape[0]])
        at += item.shape[0]

    d_rows = jnp.concatenate(d_rows, axis=0)
    grad_inputs = d_resid + project_back(d_rows, full_qkv)
    return (
        out_tokens,
        grad_inputs.astype(bf_type),
        qkv_shard[0],
        qkv_shard[1],
        qkv_shard[2],
        outup_shard[:, :width],
        outup_shard[:, width:],
        down_shard,
        vector_shards[1],
        vector_shards[2],
        vector_shards[3],
        vector_shards[4],
        vector_shards[5],
        vector_shards[0],
        vector_shards[6],
        vector_shards[7],
        vector_shards[8],
    )


def solution(mesh):
    seq_size = mesh.shape["seq"]
    by_heads = HEADS % seq_size == 0 and mesh.shape["dp"] == 4 and seq_size in (2, 4, 8, 16)
    body = functools.partial(local_heads, mesh.shape["dp"], seq_size) if by_heads else local_gathered
    return jax.shard_map(
        body,
        mesh=mesh,
        in_specs=(
            P("dp", "seq", None),
            P("dp"),
            P(("dp", "seq"), None),
            P(("dp", "seq"), None),
            P(("dp", "seq"), None),
            P(("dp", "seq"), None),
            P(("dp", "seq"), None),
            P(("dp", "seq"), None),
            P(("dp", "seq")),
            P(("dp", "seq")),
            P(("dp", "seq")),
            P(("dp", "seq")),
            P(("dp", "seq")),
            P(("dp", "seq")),
            P(("dp", "seq")),
            P(("dp", "seq")),
            P(("dp", "seq")),
            P("dp", "seq", None),
        ),
        out_specs=(
            P("dp", "seq", None),
            P("dp", "seq", None),
            P(("dp", "seq"), None),
            P(("dp", "seq"), None),
            P(("dp", "seq"), None),
            P(("dp", "seq"), None),
            P(("dp", "seq"), None),
            P(("dp", "seq"), None),
            P(("dp", "seq")),
            P(("dp", "seq")),
            P(("dp", "seq")),
            P(("dp", "seq")),
            P(("dp", "seq")),
            P(("dp", "seq")),
            P(("dp", "seq")),
            P(("dp", "seq")),
            P(("dp", "seq")),
        ),
        check_vma=False,
    )
```

```python
import functools

import jax
import jax.numpy as jnp
from jax import lax
from jax.sharding import PartitionSpec as P

HEADS = 16


score_scale = 0.125
epsilon = 1e-05
masked_score = -1e30


def layer_norm(values, gain, shift):
    average = jnp.mean(values, axis=-1, keepdims=True)
    centred = values - average
    variance = jnp.mean(centred * centred, axis=-1, keepdims=True)
    return centred * lax.rsqrt(variance + epsilon) * gain + shift


def gelu_exact(values):
    return jax.nn.gelu(values, approximate=False)


def project(values, weight):
    return jnp.einsum("srd,de->sre", values, weight, preferred_element_type=jnp.float32)


def project_back(grads, weight):
    return jnp.einsum("sre,de->srd", grads, weight, preferred_element_type=jnp.float32)


def outer_sum(values, grads):
    return jnp.einsum("srd,sre->de", values, grads, preferred_element_type=jnp.float32)


def row_total(grads):
    return jnp.sum(grads.astype(jnp.float32), axis=(0, 1))


def key_valid(lengths, first_index, key_count):
    places = first_index + jnp.arange(key_count, dtype=jnp.int32)
    return (places[None, :] < lengths[:, None])[:, None, None, :]


def local_gathered(
    tokens,
    lengths,
    w_query,
    w_key,
    w_value,
    w_out,
    w_up,
    w_down,
    b_query,
    b_value,
    b_out,
    attn_gain,
    attn_shift,
    b_up,
    b_down,
    ffn_gain,
    ffn_shift,
    cotangent,
):
    local_seqs, local_rows, model_width = tokens.shape
    head_count = HEADS
    head_size = model_width // head_count
    row_offset = lax.axis_index("seq") * local_rows
    bf_type = jnp.bfloat16
    fl_type = jnp.float32
    gathered = (
        lax.all_gather(w_query, ("dp", "seq"), axis=0, tiled=True),
        lax.all_gather(w_key, ("dp", "seq"), axis=0, tiled=True),
        lax.all_gather(w_value, ("dp", "seq"), axis=0, tiled=True),
        lax.all_gather(w_out, ("dp", "seq"), axis=0, tiled=True),
        lax.all_gather(w_up, ("dp", "seq"), axis=0, tiled=True),
        lax.all_gather(w_down, ("dp", "seq"), axis=0, tiled=True),
        lax.all_gather(b_query, ("dp", "seq"), axis=0, tiled=True),
        lax.all_gather(b_value, ("dp", "seq"), axis=0, tiled=True),
        lax.all_gather(b_out, ("dp", "seq"), axis=0, tiled=True),
        lax.all_gather(attn_gain, ("dp", "seq"), axis=0, tiled=True),
        lax.all_gather(attn_shift, ("dp", "seq"), axis=0, tiled=True),
        lax.all_gather(b_up, ("dp", "seq"), axis=0, tiled=True),
        lax.all_gather(b_down, ("dp", "seq"), axis=0, tiled=True),
        lax.all_gather(ffn_gain, ("dp", "seq"), axis=0, tiled=True),
        lax.all_gather(ffn_shift, ("dp", "seq"), axis=0, tiled=True),
    )
    full_query, full_key, full_value, full_out, full_up, full_down = gathered[:6]
    small_vectors = [item.astype(fl_type) for item in gathered[6:]]
    (
        bias_query,
        bias_value,
        bias_out,
        gain_one,
        shift_one,
        bias_up,
        bias_down,
        gain_two,
        shift_two,
    ) = small_vectors
    query = (project(tokens, full_query) + bias_query).astype(bf_type)
    key_rows = project(tokens, full_key).astype(bf_type)
    value_rows = (project(tokens, full_value) + bias_value).astype(bf_type)
    query_heads = query.reshape(local_seqs, local_rows, head_count, head_size)
    key_local = key_rows.reshape(local_seqs, local_rows, head_count, head_size)
    value_local = value_rows.reshape(local_seqs, local_rows, head_count, head_size)
    stat_shape = (local_seqs, head_count, local_rows)
    running_max = jnp.full(stat_shape, masked_score, fl_type)
    key_block = lax.all_gather(key_rows, "seq", axis=1, tiled=True)
    value_block = lax.all_gather(value_rows, "seq", axis=1, tiled=True)
    key_count = key_block.shape[1]
    key_heads = key_block.reshape(local_seqs, key_count, head_count, head_size)
    value_heads = value_block.reshape(local_seqs, key_count, head_count, head_size)
    scores = (
        jnp.einsum("sqhd,skhd->shqk", query_heads, key_heads, preferred_element_type=fl_type)
        * score_scale
    )
    keep_mask = key_valid(lengths, jnp.int32(0), key_count)
    new_max = jnp.maximum(running_max, jnp.max(jnp.where(keep_mask, scores, masked_score), axis=-1))
    exp_scores = jnp.where(keep_mask, jnp.exp(scores - new_max[..., None]), 0.0)
    running_sum = jnp.sum(exp_scores, axis=-1)
    update = jnp.einsum(
        "shqk,skhd->sqhd", exp_scores.astype(bf_type), value_heads, preferred_element_type=fl_type
    )
    context_sum = update
    final_max, final_sum, context_sum = (new_max, running_sum, context_sum)
    context_heads = context_sum / jnp.transpose(final_sum, (0, 2, 1))[..., None]
    log_sum = jnp.transpose(final_max + jnp.log(final_sum), (0, 2, 1))
    attn = context_heads.reshape(local_seqs, local_rows, model_width).astype(bf_type)
    resid = tokens.astype(fl_type) + project(attn, full_out) + bias_out
    first_f = layer_norm(resid, gain_one, shift_one)
    first = first_f.astype(bf_type)
    inner = project(first, full_up) + bias_up
    active = gelu_exact(inner).astype(bf_type)
    second = first.astype(fl_type) + project(active, full_down) + bias_down
    out_f, norm_two_pull = jax.vjp(layer_norm, second, gain_two, shift_two)
    out_tokens = out_f.astype(bf_type)
    back_weights = (
        lax.all_gather(w_query, ("dp", "seq"), axis=0, tiled=True),
        lax.all_gather(w_key, ("dp", "seq"), axis=0, tiled=True),
        lax.all_gather(w_value, ("dp", "seq"), axis=0, tiled=True),
        lax.all_gather(w_out, ("dp", "seq"), axis=0, tiled=True),
        lax.all_gather(w_up, ("dp", "seq"), axis=0, tiled=True),
        lax.all_gather(w_down, ("dp", "seq"), axis=0, tiled=True),
        lax.all_gather(b_query, ("dp", "seq"), axis=0, tiled=True),
        lax.all_gather(b_value, ("dp", "seq"), axis=0, tiled=True),
        lax.all_gather(b_out, ("dp", "seq"), axis=0, tiled=True),
        lax.all_gather(attn_gain, ("dp", "seq"), axis=0, tiled=True),
        lax.all_gather(attn_shift, ("dp", "seq"), axis=0, tiled=True),
        lax.all_gather(b_up, ("dp", "seq"), axis=0, tiled=True),
        lax.all_gather(b_down, ("dp", "seq"), axis=0, tiled=True),
        lax.all_gather(ffn_gain, ("dp", "seq"), axis=0, tiled=True),
        lax.all_gather(ffn_shift, ("dp", "seq"), axis=0, tiled=True),
    )
    back_query, back_key, back_value, back_out, back_up, back_down = back_weights[:6]
    d_second, ffngain_grad, ffnshift_grad = norm_two_pull(cotangent.astype(fl_type))
    d_outer = d_second.astype(bf_type)
    downbias_grad = row_total(d_outer)
    downproj_grad = outer_sum(active, d_outer)
    d_active = project_back(d_outer, back_down)
    gelu_value, gelu_pull = jax.vjp(gelu_exact, inner)
    d_inner = gelu_pull(d_active)[0].astype(bf_type)
    upbias_grad = row_total(d_inner)
    upproj_grad = outer_sum(first, d_inner)
    d_first = d_second + project_back(d_inner, back_up)
    norm_one_value, norm_one_pull = jax.vjp(layer_norm, resid, gain_one, shift_one)
    d_resid, attngain_grad, attnshift_grad = norm_one_pull(d_first)
    d_attnout = d_resid.astype(bf_type)
    outbias_grad = row_total(d_attnout)
    outproj_grad = outer_sum(attn, d_attnout)
    d_attn = project_back(d_attnout, back_out).astype(bf_type)
    d_attn_heads = d_attn.reshape(local_seqs, local_rows, head_count, head_size)
    row_delta = jnp.sum(d_attn_heads.astype(fl_type) * context_heads, axis=-1)
    lse_heads = jnp.transpose(log_sum, (0, 2, 1))
    delta_heads = jnp.transpose(row_delta, (0, 2, 1))
    key_block = lax.all_gather(key_rows, "seq", axis=1, tiled=True)
    value_block = lax.all_gather(value_rows, "seq", axis=1, tiled=True)
    key_count = key_block.shape[1]
    key_heads = key_block.reshape(local_seqs, key_count, head_count, head_size)
    value_heads = value_block.reshape(local_seqs, key_count, head_count, head_size)
    scores = (
        jnp.einsum("sqhd,skhd->shqk", query_heads, key_heads, preferred_element_type=fl_type)
        * score_scale
    )
    keep_mask = key_valid(lengths, jnp.int32(0), key_count)
    probs_block = jnp.where(keep_mask, jnp.exp(scores - lse_heads[..., None]), 0.0)
    d_probs = jnp.einsum(
        "sqhd,skhd->shqk", d_attn_heads, value_heads, preferred_element_type=fl_type
    )
    d_scores = (probs_block * (d_probs - delta_heads[..., None])).astype(bf_type)
    d_query_f = jnp.einsum("shqk,skhd->sqhd", d_scores, key_heads, preferred_element_type=fl_type)
    all_lse, all_delta = (
        lax.all_gather(log_sum, "seq", axis=1, tiled=True),
        lax.all_gather(row_delta, "seq", axis=1, tiled=True),
    )
    local_mask = key_valid(lengths, row_offset, local_rows)
    query_block = lax.all_gather(query, "seq", axis=1, tiled=True)
    grad_block = lax.all_gather(d_attn, "seq", axis=1, tiled=True)
    query_count = query_block.shape[1]
    remote_query = query_block.reshape(local_seqs, query_count, head_count, head_size)
    remote_grad = grad_block.reshape(local_seqs, query_count, head_count, head_size)
    remote_lse = jnp.transpose(all_lse, (0, 2, 1))
    remote_delta = jnp.transpose(all_delta, (0, 2, 1))
    scores = (
        jnp.einsum("sqhd,skhd->shqk", remote_query, key_local, preferred_element_type=fl_type)
        * score_scale
    )
    probs_block = jnp.where(local_mask, jnp.exp(scores - remote_lse[..., None]), 0.0)
    d_value_sum = jnp.einsum(
        "shqk,sqhd->skhd", probs_block.astype(bf_type), remote_grad, preferred_element_type=fl_type
    )
    d_probs = jnp.einsum(
        "sqhd,skhd->shqk", remote_grad, value_local, preferred_element_type=fl_type
    )
    d_scores = (probs_block * (d_probs - remote_delta[..., None])).astype(bf_type)
    d_key_sum = jnp.einsum(
        "shqk,sqhd->skhd", d_scores, remote_query, preferred_element_type=fl_type
    )
    flat_shape = (local_seqs, local_rows, model_width)
    d_query = (d_query_f * score_scale).reshape(flat_shape).astype(bf_type)
    d_key = (d_key_sum * score_scale).reshape(flat_shape).astype(bf_type)
    d_value = d_value_sum.reshape(flat_shape).astype(bf_type)
    querybias_grad = row_total(d_query)
    valuebias_grad = row_total(d_value)
    query_grad = outer_sum(tokens, d_query)
    key_grad = outer_sum(tokens, d_key)
    value_grad = outer_sum(tokens, d_value)
    grad_inputs = (
        d_resid
        + project_back(d_query, back_query)
        + project_back(d_key, back_key)
        + project_back(d_value, back_value)
    )
    shards = (
        lax.psum_scatter(query_grad, ("dp", "seq"), scatter_dimension=0, tiled=True),
        lax.psum_scatter(key_grad, ("dp", "seq"), scatter_dimension=0, tiled=True),
        lax.psum_scatter(value_grad, ("dp", "seq"), scatter_dimension=0, tiled=True),
        lax.psum_scatter(outproj_grad, ("dp", "seq"), scatter_dimension=0, tiled=True),
        lax.psum_scatter(upproj_grad, ("dp", "seq"), scatter_dimension=0, tiled=True),
        lax.psum_scatter(downproj_grad, ("dp", "seq"), scatter_dimension=0, tiled=True),
        lax.psum_scatter(querybias_grad, ("dp", "seq"), scatter_dimension=0, tiled=True),
        lax.psum_scatter(valuebias_grad, ("dp", "seq"), scatter_dimension=0, tiled=True),
        lax.psum_scatter(outbias_grad, ("dp", "seq"), scatter_dimension=0, tiled=True),
        lax.psum_scatter(attngain_grad, ("dp", "seq"), scatter_dimension=0, tiled=True),
        lax.psum_scatter(attnshift_grad, ("dp", "seq"), scatter_dimension=0, tiled=True),
        lax.psum_scatter(upbias_grad, ("dp", "seq"), scatter_dimension=0, tiled=True),
        lax.psum_scatter(downbias_grad, ("dp", "seq"), scatter_dimension=0, tiled=True),
        lax.psum_scatter(ffngain_grad, ("dp", "seq"), scatter_dimension=0, tiled=True),
        lax.psum_scatter(ffnshift_grad, ("dp", "seq"), scatter_dimension=0, tiled=True),
    )
    return (
        out_tokens,
        grad_inputs.astype(bf_type),
        shards[0],
        shards[1],
        shards[2],
        shards[3],
        shards[4],
        shards[5],
        shards[6],
        shards[7],
        shards[8],
        shards[9],
        shards[10],
        shards[11],
        shards[12],
        shards[13],
        shards[14],
    )


BOTH = ("dp", "seq")
SMALL_ROWS = 8


def exchange(values, axis, split, join):
    return lax.all_to_all(values, axis, split_axis=split, concat_axis=join, tiled=True)


def pick(values, at, axis):
    return lax.dynamic_index_in_dim(values, at, axis, keepdims=False)


def swap(values, count, flip):
    return lax.ppermute(values, BOTH, [(source, source ^ flip) for source in range(count)])


def add_rounded(left, right):
    return (left.astype(jnp.float32) + right.astype(jnp.float32)).astype(jnp.bfloat16)


def halve(values, axis, at, count, flip):
    other = swap(pick(values, 1 - at, axis), count, flip)
    return add_rounded(pick(values, at, axis), other)


def tie(*values):
    return lax.optimization_barrier(values)


class Scatter:
    def __init__(self, dp_size, seq_size):
        self.count, self.near, self.far = dp_size * seq_size, seq_size, 2 * seq_size
        self.lines = seq_size // 2
        dp_at, seq_at = lax.axis_index("dp"), lax.axis_index("seq")
        self.core, self.line = seq_at % 2, seq_at // 2
        self.side, self.deep = dp_at % 2, dp_at // 2

    def cores(self, terms):
        rows = terms.shape[0] // self.count
        blocks = terms.reshape(2, 2, self.lines, 2, rows, terms.shape[1])
        return halve(blocks, 3, self.core, self.count, 1)

    def plane_one(self, blocks):
        half = blocks.shape[3] // 2
        one = halve(blocks[..., :half, :], 1, self.side, self.count, self.near)
        two = halve(blocks[..., half:, :], 0, self.deep, self.count, self.far)
        return one, two

    def plane_two(self, one, two):
        one = halve(one, 0, self.deep, self.count, self.far)
        two = halve(two, 0, self.side, self.count, self.near)
        return jnp.concatenate((one, two), axis=1)

    def line_sum(self, both):
        total = pick(both, self.line, 0).astype(jnp.float32)
        for step in range(1, self.lines):
            other = swap(pick(both, self.line ^ step, 0), self.count, 2 * step)
            total = total + other.astype(jnp.float32)
        return total


def join(own, other, at, axis):
    own, other = jnp.expand_dims(own, axis), jnp.expand_dims(other, axis)
    shape = own.shape[:axis] + (2,) + own.shape[axis + 1 :]
    return jnp.where(lax.broadcasted_iota(jnp.int32, shape, axis) == at, own, other)


class Gather(Scatter):
    def line_all(self, own):
        shape = (self.lines,) + own.shape
        apart = lax.broadcasted_iota(jnp.int32, shape, 0) ^ self.line
        blocks = jnp.broadcast_to(own, shape)
        for step in range(1, self.lines):
            blocks = jnp.where(apart == step, swap(own, self.count, 2 * step), blocks)
        return blocks

    def open_one(self, blocks):
        half = blocks.shape[1] // 2
        one, two = blocks[:, :half], blocks[:, half:]
        one = join(one, swap(one, self.count, self.near), self.side, 0)
        two = join(two, swap(two, self.count, self.far), self.deep, 0)
        return one, two

    def open_two(self, one, two):
        one = join(one, swap(one, self.count, self.far), self.deep, 0)
        two = join(two, swap(two, self.count, self.near), self.side, 1)
        return jnp.concatenate((one, two), axis=3)

    def open_cores(self, blocks):
        whole = join(blocks, swap(blocks, self.count, 1), self.core, 3)
        return whole.reshape(-1, blocks.shape[-1])


def local_heads(
    dp_size,
    seq_size,
    tokens,
    lengths,
    w_query,
    w_key,
    w_value,
    w_out,
    w_up,
    w_down,
    b_query,
    b_value,
    b_out,
    attn_gain,
    attn_shift,
    b_up,
    b_down,
    ffn_gain,
    ffn_shift,
    cotangent,
):
    bf_type = jnp.bfloat16
    fl_type = jnp.float32
    count = dp_size * seq_size
    seqs, rows, width = tokens.shape
    full_rows = rows * seq_size
    own_rows = w_query.shape[0]
    own_units = w_down.shape[0]
    head_size = width // HEADS
    own_heads = HEADS // seq_size
    columns = own_heads * head_size
    seq_at = lax.axis_index("seq")

    stacked = jnp.stack((w_query, w_key, w_value), axis=1).reshape(own_rows, 3, seq_size, columns)
    by_owner = jnp.transpose(stacked, (2, 0, 1, 3)).reshape(seq_size, own_rows, 3 * columns)
    vectors = (b_up, b_query, b_value, b_out, attn_gain, attn_shift, b_down, ffn_gain, ffn_shift)
    small_own = jnp.concatenate(vectors)
    small_room = SMALL_ROWS * 3 * columns
    small_block = jnp.pad(small_own, (0, small_room - small_own.shape[0])).reshape(SMALL_ROWS, 3 * columns)
    payload = jnp.concatenate(
        (by_owner, jnp.broadcast_to(small_block[None], (seq_size, SMALL_ROWS, 3 * columns))), axis=1
    )
    payload = jnp.broadcast_to(payload[None], (dp_size,) + payload.shape)
    payload = payload.reshape(count, own_rows + SMALL_ROWS, 3 * columns)
    arrived = exchange(payload, BOTH, 0, 0)
    head_weights = arrived[:, :own_rows].reshape(width, 3 * columns)
    small_all = arrived[:, own_rows:].reshape(count, small_room)
    full_vectors = []
    at = 0
    for item in vectors:
        size = item.shape[0]
        full_vectors.append(small_all[:, at : at + size].reshape(count * size).astype(fl_type))
        at += size
    (
        bias_up,
        bias_query,
        bias_value,
        bias_out,
        gain_one,
        shift_one,
        bias_down,
        gain_two,
        shift_two,
    ) = full_vectors

    all_tokens = lax.all_gather(tokens, "seq", axis=1, tiled=True)
    gather = Gather(dp_size, seq_size)
    out_up = gather.line_all(jnp.concatenate((w_out, w_up), axis=1))
    down = gather.line_all(w_down)
    head_weights, out_up, down = tie(head_weights, out_up, down)
    out_up = gather.open_one(out_up)
    down = gather.open_one(down)

    own_bias = jnp.concatenate(
        (
            lax.dynamic_slice_in_dim(bias_query, seq_at * columns, columns),
            jnp.zeros((columns,), fl_type),
            lax.dynamic_slice_in_dim(bias_value, seq_at * columns, columns),
        )
    )
    mixed = (project(all_tokens, head_weights) + own_bias).astype(bf_type)
    mixed = mixed.reshape(seqs, full_rows, 3, own_heads, head_size)
    query, keys, values = mixed[:, :, 0], mixed[:, :, 1], mixed[:, :, 2]
    keep = key_valid(lengths, jnp.int32(0), full_rows)

    def attention(at, query_s, keys_s, values_s):
        keep_s = keep[at : at + 1]
        scores = jnp.einsum("sqhd,skhd->shqk", query_s, keys_s, preferred_element_type=fl_type) * score_scale
        row_max = jnp.max(jnp.where(keep_s, scores, masked_score), axis=-1)
        exps = jnp.where(keep_s, jnp.exp(scores - row_max[..., None]), 0.0)
        row_sum = jnp.sum(exps, axis=-1)
        context = jnp.einsum("shqk,skhd->sqhd", exps.astype(bf_type), values_s, preferred_element_type=fl_type)
        context = context / jnp.transpose(row_sum, (0, 2, 1))[..., None]
        return context, row_max + jnp.log(row_sum)

    contexts, log_sums = [], []
    for at in range(seqs):
        part = slice(at, at + 1)
        context_s, log_sum_s = attention(at, query[part], keys[part], values[part])
        contexts.append(context_s)
        log_sums.append(log_sum_s)
        if at == 0:
            contexts[0], query, out_up = tie(contexts[0], query, out_up)
            out_up = gather.open_two(*out_up)
    context = jnp.concatenate(contexts, axis=0)
    log_sum = jnp.concatenate(log_sums, axis=0)
    attn_heads = context.reshape(seqs, full_rows, columns).astype(bf_type)
    attn_heads, down = tie(attn_heads, down)
    down = gather.open_two(*down)
    attn = exchange(attn_heads, "seq", 1, 2)
    attn, out_up = tie(attn, out_up)
    out_up = gather.open_cores(out_up)
    full_out, full_up = out_up[:, :width], out_up[:, width:]
    resid = tokens.astype(fl_type) + project(attn, full_out) + bias_out
    first = layer_norm(resid, gain_one, shift_one).astype(bf_type)
    own_qkv = jnp.concatenate((w_query, w_key, w_value), axis=1)
    first, down, own_qkv = tie(first, down, own_qkv)
    full_qkv = lax.all_gather(own_qkv, BOTH, axis=0, tiled=True)
    full_down = gather.open_cores(down)
    inner = project(first, full_up) + bias_up
    active = gelu_exact(inner).astype(bf_type)
    second = first.astype(fl_type) + project(active, full_down) + bias_down
    out_f, norm_two_pull = jax.vjp(layer_norm, second, gain_two, shift_two)
    out_tokens = out_f.astype(bf_type)

    scatter = Scatter(dp_size, seq_size)
    d_second, ffngain_grad, ffnshift_grad = norm_two_pull(cotangent.astype(fl_type))
    d_outer = d_second.astype(bf_type)
    downbias_grad = row_total(d_outer)
    down_terms = scatter.cores(outer_sum(active, d_outer).astype(bf_type))
    d_active = project_back(d_outer, full_down)
    gelu_value, gelu_pull = jax.vjp(gelu_exact, inner)
    d_inner = gelu_pull(d_active)[0].astype(bf_type)
    d_inner, down_terms = tie(d_inner, down_terms)
    down_one, down_two = scatter.plane_one(down_terms)
    upbias_grad = row_total(d_inner)
    upproj_grad = outer_sum(first, d_inner)
    d_first = d_second + project_back(d_inner, full_up)
    norm_one_value, norm_one_pull = jax.vjp(layer_norm, resid, gain_one, shift_one)
    d_resid, attngain_grad, attnshift_grad = norm_one_pull(d_first)
    d_attnout = d_resid.astype(bf_type)
    outbias_grad = row_total(d_attnout)
    outproj_grad = outer_sum(attn, d_attnout)
    d_attn_rows = project_back(d_attnout, full_out).astype(bf_type)
    outup_grad = jnp.concatenate((outproj_grad.astype(bf_type), upproj_grad.astype(bf_type)), axis=1)
    outup_terms = scatter.cores(outup_grad)

    d_attn = exchange(d_attn_rows, "seq", 2, 1).reshape(seqs, full_rows, own_heads, head_size)
    d_attn, outup_terms, full_qkv = tie(d_attn, outup_terms, full_qkv)
    outup_one, outup_two = scatter.plane_one(outup_terms)

    def attention_back(at, grad):
        part = slice(at, at + 1)
        query_s, keys_s, values_s, keep_s = query[part], keys[part], values[part], keep[part]
        delta = jnp.transpose(jnp.sum(grad.astype(fl_type) * context[part], axis=-1), (0, 2, 1))
        scores = jnp.einsum("sqhd,skhd->shqk", query_s, keys_s, preferred_element_type=fl_type) * score_scale
        probs = jnp.where(keep_s, jnp.exp(scores - log_sum[part][..., None]), 0.0)
        d_probs = jnp.einsum("sqhd,skhd->shqk", grad, values_s, preferred_element_type=fl_type)
        d_scores = (probs * (d_probs - delta[..., None])).astype(bf_type)
        d_query = jnp.einsum("shqk,skhd->sqhd", d_scores, keys_s, preferred_element_type=fl_type) * score_scale
        d_keys = jnp.einsum("shqk,sqhd->skhd", d_scores, query_s, preferred_element_type=fl_type) * score_scale
        d_values = jnp.einsum("shqk,sqhd->skhd", probs.astype(bf_type), grad, preferred_element_type=fl_type)
        d_mixed = jnp.stack((d_query, d_keys, d_values), axis=2).astype(bf_type)
        return d_mixed.reshape(1, full_rows, 3 * columns)

    def to_rows(d_mixed):
        spread = exchange(d_mixed.reshape(1, full_rows, 3, columns), "seq", 1, 3)
        return spread.reshape(1, rows, 3 * width)

    d_parts, d_rows = [], []
    for at in range(seqs):
        d_parts.append(attention_back(at, d_attn[at : at + 1]))
        d_rows.append(to_rows(d_parts[-1]))
        if at == 0:
            d_attn, down_one, down_two = tie(d_attn, down_one, down_two)
            down_both = scatter.plane_two(down_one, down_two)
    d_mixed = jnp.concatenate(d_parts, axis=0)
    d_mixed, down_both, outup_one, outup_two = tie(d_mixed, down_both, outup_one, outup_two)
    down_shard = scatter.line_sum(down_both)
    outup_both = scatter.plane_two(outup_one, outup_two)
    outup_shard = scatter.line_sum(outup_both)

    mixed_grad = outer_sum(all_tokens, d_mixed).astype(bf_type).reshape(count, own_rows, 3 * columns)
    bias_mixed = row_total(d_mixed)
    empty = jnp.zeros((width,), fl_type)
    querybias_grad = lax.dynamic_update_slice_in_dim(empty, bias_mixed[:columns], seq_at * columns, 0)
    valuebias_grad = lax.dynamic_update_slice_in_dim(empty, bias_mixed[2 * columns :], seq_at * columns, 0)
    vector_grads = (
        upbias_grad,
        querybias_grad,
        valuebias_grad,
        outbias_grad,
        attngain_grad,
        attnshift_grad,
        downbias_grad,
        ffngain_grad,
        ffnshift_grad,
    )
    small_grads = jnp.concatenate([item.reshape(count, -1) for item in vector_grads], axis=1)
    small_size = small_grads.shape[1]
    small_grads = jnp.pad(small_grads, ((0, 0), (0, small_room - small_size)))
    small_grads = small_grads.reshape(count, SMALL_ROWS, 3 * columns).astype(bf_type)
    arrived = exchange(jnp.concatenate((mixed_grad, small_grads), axis=1), BOTH, 0, 0).astype(fl_type)
    qkv_shard = jnp.sum(arrived[:, :own_rows].reshape(dp_size, seq_size, own_rows, 3, columns), axis=0)
    qkv_shard = jnp.transpose(qkv_shard, (2, 1, 0, 3)).reshape(3, own_rows, width)
    small_sums = jnp.sum(arrived[:, own_rows:], axis=0).reshape(small_room)
    vector_shards = []
    at = 0
    for item in vectors:
        vector_shards.append(small_sums[at : at + item.shape[0]])
        at += item.shape[0]

    d_rows = jnp.concatenate(d_rows, axis=0)
    grad_inputs = d_resid + project_back(d_rows, full_qkv)
    return (
        out_tokens,
        grad_inputs.astype(bf_type),
        qkv_shard[0],
        qkv_shard[1],
        qkv_shard[2],
        outup_shard[:, :width],
        outup_shard[:, width:],
        down_shard,
        vector_shards[1],
        vector_shards[2],
        vector_shards[3],
        vector_shards[4],
        vector_shards[5],
        vector_shards[0],
        vector_shards[6],
        vector_shards[7],
        vector_shards[8],
    )


def solution(mesh):
    seq_size = mesh.shape["seq"]
    by_heads = HEADS % seq_size == 0 and mesh.shape["dp"] == 4 and seq_size in (2, 4, 8, 16)
    body = functools.partial(local_heads, mesh.shape["dp"], seq_size) if by_heads else local_gathered
    return jax.shard_map(
        body,
        mesh=mesh,
        in_specs=(
            P("dp", "seq", None),
            P("dp"),
            P(("dp", "seq"), None),
            P(("dp", "seq"), None),
            P(("dp", "seq"), None),
            P(("dp", "seq"), None),
            P(("dp", "seq"), None),
            P(("dp", "seq"), None),
            P(("dp", "seq")),
            P(("dp", "seq")),
            P(("dp", "seq")),
            P(("dp", "seq")),
            P(("dp", "seq")),
            P(("dp", "seq")),
            P(("dp", "seq")),
            P(("dp", "seq")),
            P(("dp", "seq")),
            P("dp", "seq", None),
        ),
        out_specs=(
            P("dp", "seq", None),
            P("dp", "seq", None),
            P(("dp", "seq"), None),
            P(("dp", "seq"), None),
            P(("dp", "seq"), None),
            P(("dp", "seq"), None),
            P(("dp", "seq"), None),
            P(("dp", "seq"), None),
            P(("dp", "seq")),
            P(("dp", "seq")),
            P(("dp", "seq")),
            P(("dp", "seq")),
            P(("dp", "seq")),
            P(("dp", "seq")),
            P(("dp", "seq")),
            P(("dp", "seq")),
            P(("dp", "seq")),
        ),
        check_vma=False,
    )
```

```python
import functools

import jax
import jax.numpy as jnp
from jax import lax
from jax.sharding import PartitionSpec as P

HEADS = 16


score_scale = 0.125
epsilon = 1e-05
masked_score = -1e30


def layer_norm(values, gain, shift):
    average = jnp.mean(values, axis=-1, keepdims=True)
    centred = values - average
    variance = jnp.mean(centred * centred, axis=-1, keepdims=True)
    return centred * lax.rsqrt(variance + epsilon) * gain + shift


def gelu_exact(values):
    return jax.nn.gelu(values, approximate=False)


def project(values, weight):
    return jnp.einsum("srd,de->sre", values, weight, preferred_element_type=jnp.float32)


def project_back(grads, weight):
    return jnp.einsum("sre,de->srd", grads, weight, preferred_element_type=jnp.float32)


def outer_sum(values, grads):
    return jnp.einsum("srd,sre->de", values, grads, preferred_element_type=jnp.float32)


def row_total(grads):
    return jnp.sum(grads.astype(jnp.float32), axis=(0, 1))


def key_valid(lengths, first_index, key_count):
    places = first_index + jnp.arange(key_count, dtype=jnp.int32)
    return (places[None, :] < lengths[:, None])[:, None, None, :]


def local_gathered(
    tokens,
    lengths,
    w_query,
    w_key,
    w_value,
    w_out,
    w_up,
    w_down,
    b_query,
    b_value,
    b_out,
    attn_gain,
    attn_shift,
    b_up,
    b_down,
    ffn_gain,
    ffn_shift,
    cotangent,
):
    local_seqs, local_rows, model_width = tokens.shape
    head_count = HEADS
    head_size = model_width // head_count
    row_offset = lax.axis_index("seq") * local_rows
    bf_type = jnp.bfloat16
    fl_type = jnp.float32
    gathered = (
        lax.all_gather(w_query, ("dp", "seq"), axis=0, tiled=True),
        lax.all_gather(w_key, ("dp", "seq"), axis=0, tiled=True),
        lax.all_gather(w_value, ("dp", "seq"), axis=0, tiled=True),
        lax.all_gather(w_out, ("dp", "seq"), axis=0, tiled=True),
        lax.all_gather(w_up, ("dp", "seq"), axis=0, tiled=True),
        lax.all_gather(w_down, ("dp", "seq"), axis=0, tiled=True),
        lax.all_gather(b_query, ("dp", "seq"), axis=0, tiled=True),
        lax.all_gather(b_value, ("dp", "seq"), axis=0, tiled=True),
        lax.all_gather(b_out, ("dp", "seq"), axis=0, tiled=True),
        lax.all_gather(attn_gain, ("dp", "seq"), axis=0, tiled=True),
        lax.all_gather(attn_shift, ("dp", "seq"), axis=0, tiled=True),
        lax.all_gather(b_up, ("dp", "seq"), axis=0, tiled=True),
        lax.all_gather(b_down, ("dp", "seq"), axis=0, tiled=True),
        lax.all_gather(ffn_gain, ("dp", "seq"), axis=0, tiled=True),
        lax.all_gather(ffn_shift, ("dp", "seq"), axis=0, tiled=True),
    )
    full_query, full_key, full_value, full_out, full_up, full_down = gathered[:6]
    small_vectors = [item.astype(fl_type) for item in gathered[6:]]
    (
        bias_query,
        bias_value,
        bias_out,
        gain_one,
        shift_one,
        bias_up,
        bias_down,
        gain_two,
        shift_two,
    ) = small_vectors
    query = (project(tokens, full_query) + bias_query).astype(bf_type)
    key_rows = project(tokens, full_key).astype(bf_type)
    value_rows = (project(tokens, full_value) + bias_value).astype(bf_type)
    query_heads = query.reshape(local_seqs, local_rows, head_count, head_size)
    key_local = key_rows.reshape(local_seqs, local_rows, head_count, head_size)
    value_local = value_rows.reshape(local_seqs, local_rows, head_count, head_size)
    stat_shape = (local_seqs, head_count, local_rows)
    running_max = jnp.full(stat_shape, masked_score, fl_type)
    key_block = lax.all_gather(key_rows, "seq", axis=1, tiled=True)
    value_block = lax.all_gather(value_rows, "seq", axis=1, tiled=True)
    key_count = key_block.shape[1]
    key_heads = key_block.reshape(local_seqs, key_count, head_count, head_size)
    value_heads = value_block.reshape(local_seqs, key_count, head_count, head_size)
    scores = (
        jnp.einsum("sqhd,skhd->shqk", query_heads, key_heads, preferred_element_type=fl_type)
        * score_scale
    )
    keep_mask = key_valid(lengths, jnp.int32(0), key_count)
    new_max = jnp.maximum(running_max, jnp.max(jnp.where(keep_mask, scores, masked_score), axis=-1))
    exp_scores = jnp.where(keep_mask, jnp.exp(scores - new_max[..., None]), 0.0)
    running_sum = jnp.sum(exp_scores, axis=-1)
    update = jnp.einsum(
        "shqk,skhd->sqhd", exp_scores.astype(bf_type), value_heads, preferred_element_type=fl_type
    )
    context_sum = update
    final_max, final_sum, context_sum = (new_max, running_sum, context_sum)
    context_heads = context_sum / jnp.transpose(final_sum, (0, 2, 1))[..., None]
    log_sum = jnp.transpose(final_max + jnp.log(final_sum), (0, 2, 1))
    attn = context_heads.reshape(local_seqs, local_rows, model_width).astype(bf_type)
    resid = tokens.astype(fl_type) + project(attn, full_out) + bias_out
    first_f = layer_norm(resid, gain_one, shift_one)
    first = first_f.astype(bf_type)
    inner = project(first, full_up) + bias_up
    active = gelu_exact(inner).astype(bf_type)
    second = first.astype(fl_type) + project(active, full_down) + bias_down
    out_f, norm_two_pull = jax.vjp(layer_norm, second, gain_two, shift_two)
    out_tokens = out_f.astype(bf_type)
    back_weights = (
        lax.all_gather(w_query, ("dp", "seq"), axis=0, tiled=True),
        lax.all_gather(w_key, ("dp", "seq"), axis=0, tiled=True),
        lax.all_gather(w_value, ("dp", "seq"), axis=0, tiled=True),
        lax.all_gather(w_out, ("dp", "seq"), axis=0, tiled=True),
        lax.all_gather(w_up, ("dp", "seq"), axis=0, tiled=True),
        lax.all_gather(w_down, ("dp", "seq"), axis=0, tiled=True),
        lax.all_gather(b_query, ("dp", "seq"), axis=0, tiled=True),
        lax.all_gather(b_value, ("dp", "seq"), axis=0, tiled=True),
        lax.all_gather(b_out, ("dp", "seq"), axis=0, tiled=True),
        lax.all_gather(attn_gain, ("dp", "seq"), axis=0, tiled=True),
        lax.all_gather(attn_shift, ("dp", "seq"), axis=0, tiled=True),
        lax.all_gather(b_up, ("dp", "seq"), axis=0, tiled=True),
        lax.all_gather(b_down, ("dp", "seq"), axis=0, tiled=True),
        lax.all_gather(ffn_gain, ("dp", "seq"), axis=0, tiled=True),
        lax.all_gather(ffn_shift, ("dp", "seq"), axis=0, tiled=True),
    )
    back_query, back_key, back_value, back_out, back_up, back_down = back_weights[:6]
    d_second, ffngain_grad, ffnshift_grad = norm_two_pull(cotangent.astype(fl_type))
    d_outer = d_second.astype(bf_type)
    downbias_grad = row_total(d_outer)
    downproj_grad = outer_sum(active, d_outer)
    d_active = project_back(d_outer, back_down)
    gelu_value, gelu_pull = jax.vjp(gelu_exact, inner)
    d_inner = gelu_pull(d_active)[0].astype(bf_type)
    upbias_grad = row_total(d_inner)
    upproj_grad = outer_sum(first, d_inner)
    d_first = d_second + project_back(d_inner, back_up)
    norm_one_value, norm_one_pull = jax.vjp(layer_norm, resid, gain_one, shift_one)
    d_resid, attngain_grad, attnshift_grad = norm_one_pull(d_first)
    d_attnout = d_resid.astype(bf_type)
    outbias_grad = row_total(d_attnout)
    outproj_grad = outer_sum(attn, d_attnout)
    d_attn = project_back(d_attnout, back_out).astype(bf_type)
    d_attn_heads = d_attn.reshape(local_seqs, local_rows, head_count, head_size)
    row_delta = jnp.sum(d_attn_heads.astype(fl_type) * context_heads, axis=-1)
    lse_heads = jnp.transpose(log_sum, (0, 2, 1))
    delta_heads = jnp.transpose(row_delta, (0, 2, 1))
    key_block = lax.all_gather(key_rows, "seq", axis=1, tiled=True)
    value_block = lax.all_gather(value_rows, "seq", axis=1, tiled=True)
    key_count = key_block.shape[1]
    key_heads = key_block.reshape(local_seqs, key_count, head_count, head_size)
    value_heads = value_block.reshape(local_seqs, key_count, head_count, head_size)
    scores = (
        jnp.einsum("sqhd,skhd->shqk", query_heads, key_heads, preferred_element_type=fl_type)
        * score_scale
    )
    keep_mask = key_valid(lengths, jnp.int32(0), key_count)
    probs_block = jnp.where(keep_mask, jnp.exp(scores - lse_heads[..., None]), 0.0)
    d_probs = jnp.einsum(
        "sqhd,skhd->shqk", d_attn_heads, value_heads, preferred_element_type=fl_type
    )
    d_scores = (probs_block * (d_probs - delta_heads[..., None])).astype(bf_type)
    d_query_f = jnp.einsum("shqk,skhd->sqhd", d_scores, key_heads, preferred_element_type=fl_type)
    all_lse, all_delta = (
        lax.all_gather(log_sum, "seq", axis=1, tiled=True),
        lax.all_gather(row_delta, "seq", axis=1, tiled=True),
    )
    local_mask = key_valid(lengths, row_offset, local_rows)
    query_block = lax.all_gather(query, "seq", axis=1, tiled=True)
    grad_block = lax.all_gather(d_attn, "seq", axis=1, tiled=True)
    query_count = query_block.shape[1]
    remote_query = query_block.reshape(local_seqs, query_count, head_count, head_size)
    remote_grad = grad_block.reshape(local_seqs, query_count, head_count, head_size)
    remote_lse = jnp.transpose(all_lse, (0, 2, 1))
    remote_delta = jnp.transpose(all_delta, (0, 2, 1))
    scores = (
        jnp.einsum("sqhd,skhd->shqk", remote_query, key_local, preferred_element_type=fl_type)
        * score_scale
    )
    probs_block = jnp.where(local_mask, jnp.exp(scores - remote_lse[..., None]), 0.0)
    d_value_sum = jnp.einsum(
        "shqk,sqhd->skhd", probs_block.astype(bf_type), remote_grad, preferred_element_type=fl_type
    )
    d_probs = jnp.einsum(
        "sqhd,skhd->shqk", remote_grad, value_local, preferred_element_type=fl_type
    )
    d_scores = (probs_block * (d_probs - remote_delta[..., None])).astype(bf_type)
    d_key_sum = jnp.einsum(
        "shqk,sqhd->skhd", d_scores, remote_query, preferred_element_type=fl_type
    )
    flat_shape = (local_seqs, local_rows, model_width)
    d_query = (d_query_f * score_scale).reshape(flat_shape).astype(bf_type)
    d_key = (d_key_sum * score_scale).reshape(flat_shape).astype(bf_type)
    d_value = d_value_sum.reshape(flat_shape).astype(bf_type)
    querybias_grad = row_total(d_query)
    valuebias_grad = row_total(d_value)
    query_grad = outer_sum(tokens, d_query)
    key_grad = outer_sum(tokens, d_key)
    value_grad = outer_sum(tokens, d_value)
    grad_inputs = (
        d_resid
        + project_back(d_query, back_query)
        + project_back(d_key, back_key)
        + project_back(d_value, back_value)
    )
    shards = (
        lax.psum_scatter(query_grad, ("dp", "seq"), scatter_dimension=0, tiled=True),
        lax.psum_scatter(key_grad, ("dp", "seq"), scatter_dimension=0, tiled=True),
        lax.psum_scatter(value_grad, ("dp", "seq"), scatter_dimension=0, tiled=True),
        lax.psum_scatter(outproj_grad, ("dp", "seq"), scatter_dimension=0, tiled=True),
        lax.psum_scatter(upproj_grad, ("dp", "seq"), scatter_dimension=0, tiled=True),
        lax.psum_scatter(downproj_grad, ("dp", "seq"), scatter_dimension=0, tiled=True),
        lax.psum_scatter(querybias_grad, ("dp", "seq"), scatter_dimension=0, tiled=True),
        lax.psum_scatter(valuebias_grad, ("dp", "seq"), scatter_dimension=0, tiled=True),
        lax.psum_scatter(outbias_grad, ("dp", "seq"), scatter_dimension=0, tiled=True),
        lax.psum_scatter(attngain_grad, ("dp", "seq"), scatter_dimension=0, tiled=True),
        lax.psum_scatter(attnshift_grad, ("dp", "seq"), scatter_dimension=0, tiled=True),
        lax.psum_scatter(upbias_grad, ("dp", "seq"), scatter_dimension=0, tiled=True),
        lax.psum_scatter(downbias_grad, ("dp", "seq"), scatter_dimension=0, tiled=True),
        lax.psum_scatter(ffngain_grad, ("dp", "seq"), scatter_dimension=0, tiled=True),
        lax.psum_scatter(ffnshift_grad, ("dp", "seq"), scatter_dimension=0, tiled=True),
    )
    return (
        out_tokens,
        grad_inputs.astype(bf_type),
        shards[0],
        shards[1],
        shards[2],
        shards[3],
        shards[4],
        shards[5],
        shards[6],
        shards[7],
        shards[8],
        shards[9],
        shards[10],
        shards[11],
        shards[12],
        shards[13],
        shards[14],
    )


BOTH = ("dp", "seq")
SMALL_ROWS = 8


def exchange(values, axis, split, join):
    return lax.all_to_all(values, axis, split_axis=split, concat_axis=join, tiled=True)


def pick(values, at, axis):
    return lax.dynamic_index_in_dim(values, at, axis, keepdims=False)


def swap(values, count, flip):
    return lax.ppermute(values, BOTH, [(source, source ^ flip) for source in range(count)])


def add_rounded(left, right):
    return (left.astype(jnp.float32) + right.astype(jnp.float32)).astype(jnp.bfloat16)


def halve(values, axis, at, count, flip):
    other = swap(pick(values, 1 - at, axis), count, flip)
    return add_rounded(pick(values, at, axis), other)


def tie(*values):
    return lax.optimization_barrier(values)


class Scatter:
    def __init__(self, dp_size, seq_size):
        self.count, self.near, self.far = dp_size * seq_size, seq_size, 2 * seq_size
        self.lines = seq_size // 2
        dp_at, seq_at = lax.axis_index("dp"), lax.axis_index("seq")
        self.core, self.line = seq_at % 2, seq_at // 2
        self.side, self.deep = dp_at % 2, dp_at // 2

    def cores(self, terms):
        rows = terms.shape[0] // self.count
        blocks = terms.reshape(2, 2, self.lines, 2, rows, terms.shape[1])
        return halve(blocks, 3, self.core, self.count, 1)

    def plane_one(self, blocks):
        half = blocks.shape[3] // 2
        one = halve(blocks[..., :half, :], 1, self.side, self.count, self.near)
        two = halve(blocks[..., half:, :], 0, self.deep, self.count, self.far)
        return one, two

    def plane_two(self, one, two):
        one = halve(one, 0, self.deep, self.count, self.far)
        two = halve(two, 0, self.side, self.count, self.near)
        return jnp.concatenate((one, two), axis=1)

    def line_sum(self, both):
        total = pick(both, self.line, 0).astype(jnp.float32)
        for step in range(1, self.lines):
            other = swap(pick(both, self.line ^ step, 0), self.count, 2 * step)
            total = total + other.astype(jnp.float32)
        return total


def join(own, other, at, axis):
    own, other = jnp.expand_dims(own, axis), jnp.expand_dims(other, axis)
    shape = own.shape[:axis] + (2,) + own.shape[axis + 1 :]
    return jnp.where(lax.broadcasted_iota(jnp.int32, shape, axis) == at, own, other)


class Gather(Scatter):
    def line_all(self, own):
        shape = (self.lines,) + own.shape
        apart = lax.broadcasted_iota(jnp.int32, shape, 0) ^ self.line
        blocks = jnp.broadcast_to(own, shape)
        for step in range(1, self.lines):
            blocks = jnp.where(apart == step, swap(own, self.count, 2 * step), blocks)
        return blocks

    def open_one(self, blocks):
        half = blocks.shape[1] // 2
        one, two = blocks[:, :half], blocks[:, half:]
        one = join(one, swap(one, self.count, self.near), self.side, 0)
        two = join(two, swap(two, self.count, self.far), self.deep, 0)
        return one, two

    def open_two(self, one, two):
        one = join(one, swap(one, self.count, self.far), self.deep, 0)
        two = join(two, swap(two, self.count, self.near), self.side, 1)
        return jnp.concatenate((one, two), axis=3)

    def open_cores(self, blocks):
        whole = join(blocks, swap(blocks, self.count, 1), self.core, 3)
        return whole.reshape(-1, blocks.shape[-1])


def local_heads(
    dp_size,
    seq_size,
    tokens,
    lengths,
    w_query,
    w_key,
    w_value,
    w_out,
    w_up,
    w_down,
    b_query,
    b_value,
    b_out,
    attn_gain,
    attn_shift,
    b_up,
    b_down,
    ffn_gain,
    ffn_shift,
    cotangent,
):
    bf_type = jnp.bfloat16
    fl_type = jnp.float32
    count = dp_size * seq_size
    seqs, rows, width = tokens.shape
    full_rows = rows * seq_size
    own_rows = w_query.shape[0]
    own_units = w_down.shape[0]
    head_size = width // HEADS
    own_heads = HEADS // seq_size
    columns = own_heads * head_size
    seq_at = lax.axis_index("seq")

    stacked = jnp.stack((w_query, w_key, w_value), axis=1).reshape(own_rows, 3, seq_size, columns)
    by_owner = jnp.transpose(stacked, (2, 0, 1, 3)).reshape(seq_size, own_rows, 3 * columns)
    vectors = (b_up, b_query, b_value, b_out, attn_gain, attn_shift, b_down, ffn_gain, ffn_shift)
    small_own = jnp.concatenate(vectors)
    small_room = SMALL_ROWS * 3 * columns
    small_block = jnp.pad(small_own, (0, small_room - small_own.shape[0])).reshape(SMALL_ROWS, 3 * columns)
    payload = jnp.concatenate(
        (by_owner, jnp.broadcast_to(small_block[None], (seq_size, SMALL_ROWS, 3 * columns))), axis=1
    )
    payload = jnp.broadcast_to(payload[None], (dp_size,) + payload.shape)
    payload = payload.reshape(count, own_rows + SMALL_ROWS, 3 * columns)
    arrived = exchange(payload, BOTH, 0, 0)
    head_weights = arrived[:, :own_rows].reshape(width, 3 * columns)
    small_all = arrived[:, own_rows:].reshape(count, small_room)
    full_vectors = []
    at = 0
    for item in vectors:
        size = item.shape[0]
        full_vectors.append(small_all[:, at : at + size].reshape(count * size).astype(fl_type))
        at += size
    (
        bias_up,
        bias_query,
        bias_value,
        bias_out,
        gain_one,
        shift_one,
        bias_down,
        gain_two,
        shift_two,
    ) = full_vectors

    all_tokens = lax.all_gather(tokens, "seq", axis=1, tiled=True)
    out_up = lax.all_gather(jnp.concatenate((w_out, w_up), axis=1), BOTH, axis=0, tiled=True)
    gather = Gather(dp_size, seq_size)

    own_bias = jnp.concatenate(
        (
            lax.dynamic_slice_in_dim(bias_query, seq_at * columns, columns),
            jnp.zeros((columns,), fl_type),
            lax.dynamic_slice_in_dim(bias_value, seq_at * columns, columns),
        )
    )
    mixed = (project(all_tokens, head_weights) + own_bias).astype(bf_type)
    mixed, own_down = tie(mixed, w_down)
    down = gather.line_all(own_down)
    mixed = mixed.reshape(seqs, full_rows, 3, own_heads, head_size)
    query, keys, values = mixed[:, :, 0], mixed[:, :, 1], mixed[:, :, 2]
    keep = key_valid(lengths, jnp.int32(0), full_rows)
    scores = jnp.einsum("sqhd,skhd->shqk", query, keys, preferred_element_type=fl_type) * score_scale
    row_max = jnp.max(jnp.where(keep, scores, masked_score), axis=-1)
    exps = jnp.where(keep, jnp.exp(scores - row_max[..., None]), 0.0)
    row_sum = jnp.sum(exps, axis=-1)
    context = jnp.einsum("shqk,skhd->sqhd", exps.astype(bf_type), values, preferred_element_type=fl_type)
    context = context / jnp.transpose(row_sum, (0, 2, 1))[..., None]
    log_sum = row_max + jnp.log(row_sum)
    attn_heads = context.reshape(seqs, full_rows, columns).astype(bf_type)
    attn_heads, down = tie(attn_heads, down)
    down = gather.open_one(down)
    attn = exchange(attn_heads, "seq", 1, 2)
    attn, down = tie(attn, down)
    down = gather.open_two(*down)
    out_up, down = tie(out_up, down)
    full_down = gather.open_cores(down)
    full_out, full_up = out_up[:, :width], out_up[:, width:]
    own_qkv = jnp.concatenate((w_query, w_key, w_value), axis=1)
    full_qkv = lax.all_gather(own_qkv, BOTH, axis=0, tiled=True)

    resid = tokens.astype(fl_type) + project(attn, full_out) + bias_out
    first = layer_norm(resid, gain_one, shift_one).astype(bf_type)
    inner = project(first, full_up) + bias_up
    active = gelu_exact(inner).astype(bf_type)
    second = first.astype(fl_type) + project(active, full_down) + bias_down
    out_f, norm_two_pull = jax.vjp(layer_norm, second, gain_two, shift_two)
    out_tokens = out_f.astype(bf_type)

    scatter = Scatter(dp_size, seq_size)
    d_second, ffngain_grad, ffnshift_grad = norm_two_pull(cotangent.astype(fl_type))
    d_outer = d_second.astype(bf_type)
    downbias_grad = row_total(d_outer)
    down_terms = scatter.cores(outer_sum(active, d_outer).astype(bf_type))
    d_active = project_back(d_outer, full_down)
    gelu_value, gelu_pull = jax.vjp(gelu_exact, inner)
    d_inner = gelu_pull(d_active)[0].astype(bf_type)
    d_inner, down_terms, full_qkv = tie(d_inner, down_terms, full_qkv)
    down_one, down_two = scatter.plane_one(down_terms)
    upbias_grad = row_total(d_inner)
    upproj_grad = outer_sum(first, d_inner)
    d_first = d_second + project_back(d_inner, full_up)
    norm_one_value, norm_one_pull = jax.vjp(layer_norm, resid, gain_one, shift_one)
    d_resid, attngain_grad, attnshift_grad = norm_one_pull(d_first)
    d_attnout = d_resid.astype(bf_type)
    outbias_grad = row_total(d_attnout)
    outproj_grad = outer_sum(attn, d_attnout)
    d_attn_rows = project_back(d_attnout, full_out).astype(bf_type)
    d_attn_rows, down_one, down_two = tie(d_attn_rows, down_one, down_two)
    down_both = scatter.plane_two(down_one, down_two)
    outup_grad = jnp.concatenate((outproj_grad.astype(bf_type), upproj_grad.astype(bf_type)), axis=1)
    outup_terms = scatter.cores(outup_grad)

    d_attn = exchange(d_attn_rows, "seq", 2, 1).reshape(seqs, full_rows, own_heads, head_size)
    d_attn, outup_terms, down_both = tie(d_attn, outup_terms, down_both)
    outup_one, outup_two = scatter.plane_one(outup_terms)
    down_shard = scatter.line_sum(down_both)

    def attention_back(at, grad):
        part = slice(at, at + 1)
        query_s, keys_s, values_s, keep_s = query[part], keys[part], values[part], keep[part]
        delta = jnp.transpose(jnp.sum(grad.astype(fl_type) * context[part], axis=-1), (0, 2, 1))
        scores = jnp.einsum("sqhd,skhd->shqk", query_s, keys_s, preferred_element_type=fl_type) * score_scale
        probs = jnp.where(keep_s, jnp.exp(scores - log_sum[part][..., None]), 0.0)
        d_probs = jnp.einsum("sqhd,skhd->shqk", grad, values_s, preferred_element_type=fl_type)
        d_scores = (probs * (d_probs - delta[..., None])).astype(bf_type)
        d_query = jnp.einsum("shqk,skhd->sqhd", d_scores, keys_s, preferred_element_type=fl_type) * score_scale
        d_keys = jnp.einsum("shqk,sqhd->skhd", d_scores, query_s, preferred_element_type=fl_type) * score_scale
        d_values = jnp.einsum("shqk,sqhd->skhd", probs.astype(bf_type), grad, preferred_element_type=fl_type)
        d_mixed = jnp.stack((d_query, d_keys, d_values), axis=2).astype(bf_type)
        return d_mixed.reshape(1, full_rows, 3 * columns)

    def to_rows(d_mixed):
        spread = exchange(d_mixed.reshape(1, full_rows, 3, columns), "seq", 1, 3)
        return spread.reshape(1, rows, 3 * width)

    d_parts, d_rows = [], []
    for at in range(seqs):
        d_parts.append(attention_back(at, d_attn[at : at + 1]))
        d_rows.append(to_rows(d_parts[-1]))
        if at == 0:
            d_attn, outup_one, outup_two, down_shard = tie(d_attn, outup_one, outup_two, down_shard)
            outup_both = scatter.plane_two(outup_one, outup_two)
    d_mixed = jnp.concatenate(d_parts, axis=0)
    d_mixed, outup_both = tie(d_mixed, outup_both)
    outup_shard = scatter.line_sum(outup_both)

    mixed_grad = outer_sum(all_tokens, d_mixed).astype(bf_type).reshape(count, own_rows, 3 * columns)
    bias_mixed = row_total(d_mixed)
    empty = jnp.zeros((width,), fl_type)
    querybias_grad = lax.dynamic_update_slice_in_dim(empty, bias_mixed[:columns], seq_at * columns, 0)
    valuebias_grad = lax.dynamic_update_slice_in_dim(empty, bias_mixed[2 * columns :], seq_at * columns, 0)
    vector_grads = (
        upbias_grad,
        querybias_grad,
        valuebias_grad,
        outbias_grad,
        attngain_grad,
        attnshift_grad,
        downbias_grad,
        ffngain_grad,
        ffnshift_grad,
    )
    small_grads = jnp.concatenate([item.reshape(count, -1) for item in vector_grads], axis=1)
    small_size = small_grads.shape[1]
    small_grads = jnp.pad(small_grads, ((0, 0), (0, small_room - small_size)))
    small_grads = small_grads.reshape(count, SMALL_ROWS, 3 * columns).astype(bf_type)
    arrived = exchange(jnp.concatenate((mixed_grad, small_grads), axis=1), BOTH, 0, 0).astype(fl_type)
    qkv_shard = jnp.sum(arrived[:, :own_rows].reshape(dp_size, seq_size, own_rows, 3, columns), axis=0)
    qkv_shard = jnp.transpose(qkv_shard, (2, 1, 0, 3)).reshape(3, own_rows, width)
    small_sums = jnp.sum(arrived[:, own_rows:], axis=0).reshape(small_room)
    vector_shards = []
    at = 0
    for item in vectors:
        vector_shards.append(small_sums[at : at + item.shape[0]])
        at += item.shape[0]

    d_rows = jnp.concatenate(d_rows, axis=0)
    grad_inputs = d_resid + project_back(d_rows, full_qkv)
    return (
        out_tokens,
        grad_inputs.astype(bf_type),
        qkv_shard[0],
        qkv_shard[1],
        qkv_shard[2],
        outup_shard[:, :width],
        outup_shard[:, width:],
        down_shard,
        vector_shards[1],
        vector_shards[2],
        vector_shards[3],
        vector_shards[4],
        vector_shards[5],
        vector_shards[0],
        vector_shards[6],
        vector_shards[7],
        vector_shards[8],
    )


def solution(mesh):
    seq_size = mesh.shape["seq"]
    by_heads = HEADS % seq_size == 0 and mesh.shape["dp"] == 4 and seq_size in (2, 4, 8, 16)
    body = functools.partial(local_heads, mesh.shape["dp"], seq_size) if by_heads else local_gathered
    return jax.shard_map(
        body,
        mesh=mesh,
        in_specs=(
            P("dp", "seq", None),
            P("dp"),
            P(("dp", "seq"), None),
            P(("dp", "seq"), None),
            P(("dp", "seq"), None),
            P(("dp", "seq"), None),
            P(("dp", "seq"), None),
            P(("dp", "seq"), None),
            P(("dp", "seq")),
            P(("dp", "seq")),
            P(("dp", "seq")),
            P(("dp", "seq")),
            P(("dp", "seq")),
            P(("dp", "seq")),
            P(("dp", "seq")),
            P(("dp", "seq")),
            P(("dp", "seq")),
            P("dp", "seq", None),
        ),
        out_specs=(
            P("dp", "seq", None),
            P("dp", "seq", None),
            P(("dp", "seq"), None),
            P(("dp", "seq"), None),
            P(("dp", "seq"), None),
            P(("dp", "seq"), None),
            P(("dp", "seq"), None),
            P(("dp", "seq"), None),
            P(("dp", "seq")),
            P(("dp", "seq")),
            P(("dp", "seq")),
            P(("dp", "seq")),
            P(("dp", "seq")),
            P(("dp", "seq")),
            P(("dp", "seq")),
            P(("dp", "seq")),
            P(("dp", "seq")),
        ),
        check_vma=False,
    )
```

```python
import functools

import jax
import jax.numpy as jnp
from jax import lax
from jax.sharding import PartitionSpec as P

HEADS = 16


score_scale = 0.125
epsilon = 1e-05
masked_score = -1e30


def layer_norm(values, gain, shift):
    average = jnp.mean(values, axis=-1, keepdims=True)
    centred = values - average
    variance = jnp.mean(centred * centred, axis=-1, keepdims=True)
    return centred * lax.rsqrt(variance + epsilon) * gain + shift


def gelu_exact(values):
    return jax.nn.gelu(values, approximate=False)


def project(values, weight):
    return jnp.einsum("srd,de->sre", values, weight, preferred_element_type=jnp.float32)


def project_back(grads, weight):
    return jnp.einsum("sre,de->srd", grads, weight, preferred_element_type=jnp.float32)


def outer_sum(values, grads):
    return jnp.einsum("srd,sre->de", values, grads, preferred_element_type=jnp.float32)


def row_total(grads):
    return jnp.sum(grads.astype(jnp.float32), axis=(0, 1))


def key_valid(lengths, first_index, key_count):
    places = first_index + jnp.arange(key_count, dtype=jnp.int32)
    return (places[None, :] < lengths[:, None])[:, None, None, :]


def local_gathered(
    tokens,
    lengths,
    w_query,
    w_key,
    w_value,
    w_out,
    w_up,
    w_down,
    b_query,
    b_value,
    b_out,
    attn_gain,
    attn_shift,
    b_up,
    b_down,
    ffn_gain,
    ffn_shift,
    cotangent,
):
    local_seqs, local_rows, model_width = tokens.shape
    head_count = HEADS
    head_size = model_width // head_count
    row_offset = lax.axis_index("seq") * local_rows
    bf_type = jnp.bfloat16
    fl_type = jnp.float32
    gathered = (
        lax.all_gather(w_query, ("dp", "seq"), axis=0, tiled=True),
        lax.all_gather(w_key, ("dp", "seq"), axis=0, tiled=True),
        lax.all_gather(w_value, ("dp", "seq"), axis=0, tiled=True),
        lax.all_gather(w_out, ("dp", "seq"), axis=0, tiled=True),
        lax.all_gather(w_up, ("dp", "seq"), axis=0, tiled=True),
        lax.all_gather(w_down, ("dp", "seq"), axis=0, tiled=True),
        lax.all_gather(b_query, ("dp", "seq"), axis=0, tiled=True),
        lax.all_gather(b_value, ("dp", "seq"), axis=0, tiled=True),
        lax.all_gather(b_out, ("dp", "seq"), axis=0, tiled=True),
        lax.all_gather(attn_gain, ("dp", "seq"), axis=0, tiled=True),
        lax.all_gather(attn_shift, ("dp", "seq"), axis=0, tiled=True),
        lax.all_gather(b_up, ("dp", "seq"), axis=0, tiled=True),
        lax.all_gather(b_down, ("dp", "seq"), axis=0, tiled=True),
        lax.all_gather(ffn_gain, ("dp", "seq"), axis=0, tiled=True),
        lax.all_gather(ffn_shift, ("dp", "seq"), axis=0, tiled=True),
    )
    full_query, full_key, full_value, full_out, full_up, full_down = gathered[:6]
    small_vectors = [item.astype(fl_type) for item in gathered[6:]]
    (
        bias_query,
        bias_value,
        bias_out,
        gain_one,
        shift_one,
        bias_up,
        bias_down,
        gain_two,
        shift_two,
    ) = small_vectors
    query = (project(tokens, full_query) + bias_query).astype(bf_type)
    key_rows = project(tokens, full_key).astype(bf_type)
    value_rows = (project(tokens, full_value) + bias_value).astype(bf_type)
    query_heads = query.reshape(local_seqs, local_rows, head_count, head_size)
    key_local = key_rows.reshape(local_seqs, local_rows, head_count, head_size)
    value_local = value_rows.reshape(local_seqs, local_rows, head_count, head_size)
    stat_shape = (local_seqs, head_count, local_rows)
    running_max = jnp.full(stat_shape, masked_score, fl_type)
    key_block = lax.all_gather(key_rows, "seq", axis=1, tiled=True)
    value_block = lax.all_gather(value_rows, "seq", axis=1, tiled=True)
    key_count = key_block.shape[1]
    key_heads = key_block.reshape(local_seqs, key_count, head_count, head_size)
    value_heads = value_block.reshape(local_seqs, key_count, head_count, head_size)
    scores = (
        jnp.einsum("sqhd,skhd->shqk", query_heads, key_heads, preferred_element_type=fl_type)
        * score_scale
    )
    keep_mask = key_valid(lengths, jnp.int32(0), key_count)
    new_max = jnp.maximum(running_max, jnp.max(jnp.where(keep_mask, scores, masked_score), axis=-1))
    exp_scores = jnp.where(keep_mask, jnp.exp(scores - new_max[..., None]), 0.0)
    running_sum = jnp.sum(exp_scores, axis=-1)
    update = jnp.einsum(
        "shqk,skhd->sqhd", exp_scores.astype(bf_type), value_heads, preferred_element_type=fl_type
    )
    context_sum = update
    final_max, final_sum, context_sum = (new_max, running_sum, context_sum)
    context_heads = context_sum / jnp.transpose(final_sum, (0, 2, 1))[..., None]
    log_sum = jnp.transpose(final_max + jnp.log(final_sum), (0, 2, 1))
    attn = context_heads.reshape(local_seqs, local_rows, model_width).astype(bf_type)
    resid = tokens.astype(fl_type) + project(attn, full_out) + bias_out
    first_f = layer_norm(resid, gain_one, shift_one)
    first = first_f.astype(bf_type)
    inner = project(first, full_up) + bias_up
    active = gelu_exact(inner).astype(bf_type)
    second = first.astype(fl_type) + project(active, full_down) + bias_down
    out_f, norm_two_pull = jax.vjp(layer_norm, second, gain_two, shift_two)
    out_tokens = out_f.astype(bf_type)
    back_weights = (
        lax.all_gather(w_query, ("dp", "seq"), axis=0, tiled=True),
        lax.all_gather(w_key, ("dp", "seq"), axis=0, tiled=True),
        lax.all_gather(w_value, ("dp", "seq"), axis=0, tiled=True),
        lax.all_gather(w_out, ("dp", "seq"), axis=0, tiled=True),
        lax.all_gather(w_up, ("dp", "seq"), axis=0, tiled=True),
        lax.all_gather(w_down, ("dp", "seq"), axis=0, tiled=True),
        lax.all_gather(b_query, ("dp", "seq"), axis=0, tiled=True),
        lax.all_gather(b_value, ("dp", "seq"), axis=0, tiled=True),
        lax.all_gather(b_out, ("dp", "seq"), axis=0, tiled=True),
        lax.all_gather(attn_gain, ("dp", "seq"), axis=0, tiled=True),
        lax.all_gather(attn_shift, ("dp", "seq"), axis=0, tiled=True),
        lax.all_gather(b_up, ("dp", "seq"), axis=0, tiled=True),
        lax.all_gather(b_down, ("dp", "seq"), axis=0, tiled=True),
        lax.all_gather(ffn_gain, ("dp", "seq"), axis=0, tiled=True),
        lax.all_gather(ffn_shift, ("dp", "seq"), axis=0, tiled=True),
    )
    back_query, back_key, back_value, back_out, back_up, back_down = back_weights[:6]
    d_second, ffngain_grad, ffnshift_grad = norm_two_pull(cotangent.astype(fl_type))
    d_outer = d_second.astype(bf_type)
    downbias_grad = row_total(d_outer)
    downproj_grad = outer_sum(active, d_outer)
    d_active = project_back(d_outer, back_down)
    gelu_value, gelu_pull = jax.vjp(gelu_exact, inner)
    d_inner = gelu_pull(d_active)[0].astype(bf_type)
    upbias_grad = row_total(d_inner)
    upproj_grad = outer_sum(first, d_inner)
    d_first = d_second + project_back(d_inner, back_up)
    norm_one_value, norm_one_pull = jax.vjp(layer_norm, resid, gain_one, shift_one)
    d_resid, attngain_grad, attnshift_grad = norm_one_pull(d_first)
    d_attnout = d_resid.astype(bf_type)
    outbias_grad = row_total(d_attnout)
    outproj_grad = outer_sum(attn, d_attnout)
    d_attn = project_back(d_attnout, back_out).astype(bf_type)
    d_attn_heads = d_attn.reshape(local_seqs, local_rows, head_count, head_size)
    row_delta = jnp.sum(d_attn_heads.astype(fl_type) * context_heads, axis=-1)
    lse_heads = jnp.transpose(log_sum, (0, 2, 1))
    delta_heads = jnp.transpose(row_delta, (0, 2, 1))
    key_block = lax.all_gather(key_rows, "seq", axis=1, tiled=True)
    value_block = lax.all_gather(value_rows, "seq", axis=1, tiled=True)
    key_count = key_block.shape[1]
    key_heads = key_block.reshape(local_seqs, key_count, head_count, head_size)
    value_heads = value_block.reshape(local_seqs, key_count, head_count, head_size)
    scores = (
        jnp.einsum("sqhd,skhd->shqk", query_heads, key_heads, preferred_element_type=fl_type)
        * score_scale
    )
    keep_mask = key_valid(lengths, jnp.int32(0), key_count)
    probs_block = jnp.where(keep_mask, jnp.exp(scores - lse_heads[..., None]), 0.0)
    d_probs = jnp.einsum(
        "sqhd,skhd->shqk", d_attn_heads, value_heads, preferred_element_type=fl_type
    )
    d_scores = (probs_block * (d_probs - delta_heads[..., None])).astype(bf_type)
    d_query_f = jnp.einsum("shqk,skhd->sqhd", d_scores, key_heads, preferred_element_type=fl_type)
    all_lse, all_delta = (
        lax.all_gather(log_sum, "seq", axis=1, tiled=True),
        lax.all_gather(row_delta, "seq", axis=1, tiled=True),
    )
    local_mask = key_valid(lengths, row_offset, local_rows)
    query_block = lax.all_gather(query, "seq", axis=1, tiled=True)
    grad_block = lax.all_gather(d_attn, "seq", axis=1, tiled=True)
    query_count = query_block.shape[1]
    remote_query = query_block.reshape(local_seqs, query_count, head_count, head_size)
    remote_grad = grad_block.reshape(local_seqs, query_count, head_count, head_size)
    remote_lse = jnp.transpose(all_lse, (0, 2, 1))
    remote_delta = jnp.transpose(all_delta, (0, 2, 1))
    scores = (
        jnp.einsum("sqhd,skhd->shqk", remote_query, key_local, preferred_element_type=fl_type)
        * score_scale
    )
    probs_block = jnp.where(local_mask, jnp.exp(scores - remote_lse[..., None]), 0.0)
    d_value_sum = jnp.einsum(
        "shqk,sqhd->skhd", probs_block.astype(bf_type), remote_grad, preferred_element_type=fl_type
    )
    d_probs = jnp.einsum(
        "sqhd,skhd->shqk", remote_grad, value_local, preferred_element_type=fl_type
    )
    d_scores = (probs_block * (d_probs - remote_delta[..., None])).astype(bf_type)
    d_key_sum = jnp.einsum(
        "shqk,sqhd->skhd", d_scores, remote_query, preferred_element_type=fl_type
    )
    flat_shape = (local_seqs, local_rows, model_width)
    d_query = (d_query_f * score_scale).reshape(flat_shape).astype(bf_type)
    d_key = (d_key_sum * score_scale).reshape(flat_shape).astype(bf_type)
    d_value = d_value_sum.reshape(flat_shape).astype(bf_type)
    querybias_grad = row_total(d_query)
    valuebias_grad = row_total(d_value)
    query_grad = outer_sum(tokens, d_query)
    key_grad = outer_sum(tokens, d_key)
    value_grad = outer_sum(tokens, d_value)
    grad_inputs = (
        d_resid
        + project_back(d_query, back_query)
        + project_back(d_key, back_key)
        + project_back(d_value, back_value)
    )
    shards = (
        lax.psum_scatter(query_grad, ("dp", "seq"), scatter_dimension=0, tiled=True),
        lax.psum_scatter(key_grad, ("dp", "seq"), scatter_dimension=0, tiled=True),
        lax.psum_scatter(value_grad, ("dp", "seq"), scatter_dimension=0, tiled=True),
        lax.psum_scatter(outproj_grad, ("dp", "seq"), scatter_dimension=0, tiled=True),
        lax.psum_scatter(upproj_grad, ("dp", "seq"), scatter_dimension=0, tiled=True),
        lax.psum_scatter(downproj_grad, ("dp", "seq"), scatter_dimension=0, tiled=True),
        lax.psum_scatter(querybias_grad, ("dp", "seq"), scatter_dimension=0, tiled=True),
        lax.psum_scatter(valuebias_grad, ("dp", "seq"), scatter_dimension=0, tiled=True),
        lax.psum_scatter(outbias_grad, ("dp", "seq"), scatter_dimension=0, tiled=True),
        lax.psum_scatter(attngain_grad, ("dp", "seq"), scatter_dimension=0, tiled=True),
        lax.psum_scatter(attnshift_grad, ("dp", "seq"), scatter_dimension=0, tiled=True),
        lax.psum_scatter(upbias_grad, ("dp", "seq"), scatter_dimension=0, tiled=True),
        lax.psum_scatter(downbias_grad, ("dp", "seq"), scatter_dimension=0, tiled=True),
        lax.psum_scatter(ffngain_grad, ("dp", "seq"), scatter_dimension=0, tiled=True),
        lax.psum_scatter(ffnshift_grad, ("dp", "seq"), scatter_dimension=0, tiled=True),
    )
    return (
        out_tokens,
        grad_inputs.astype(bf_type),
        shards[0],
        shards[1],
        shards[2],
        shards[3],
        shards[4],
        shards[5],
        shards[6],
        shards[7],
        shards[8],
        shards[9],
        shards[10],
        shards[11],
        shards[12],
        shards[13],
        shards[14],
    )


BOTH = ("dp", "seq")
SMALL_ROWS = 8


def exchange(values, axis, split, join):
    return lax.all_to_all(values, axis, split_axis=split, concat_axis=join, tiled=True)


def pick(values, at, axis):
    return lax.dynamic_index_in_dim(values, at, axis, keepdims=False)


def swap(values, count, flip):
    return lax.ppermute(values, BOTH, [(source, source ^ flip) for source in range(count)])


def add_rounded(left, right):
    return (left.astype(jnp.float32) + right.astype(jnp.float32)).astype(jnp.bfloat16)


def halve(values, axis, at, count, flip):
    other = swap(pick(values, 1 - at, axis), count, flip)
    return add_rounded(pick(values, at, axis), other)


def tie(*values):
    return lax.optimization_barrier(values)


class Scatter:
    def __init__(self, dp_size, seq_size):
        self.count, self.near, self.far = dp_size * seq_size, seq_size, 2 * seq_size
        self.lines = seq_size // 2
        dp_at, seq_at = lax.axis_index("dp"), lax.axis_index("seq")
        self.core, self.line = seq_at % 2, seq_at // 2
        self.side, self.deep = dp_at % 2, dp_at // 2

    def cores(self, terms):
        rows = terms.shape[0] // self.count
        blocks = terms.reshape(2, 2, self.lines, 2, rows, terms.shape[1])
        return halve(blocks, 3, self.core, self.count, 1)

    def plane_one(self, blocks):
        half = blocks.shape[3] // 2
        one = halve(blocks[..., :half, :], 1, self.side, self.count, self.near)
        two = halve(blocks[..., half:, :], 0, self.deep, self.count, self.far)
        return one, two

    def plane_two(self, one, two):
        one = halve(one, 0, self.deep, self.count, self.far)
        two = halve(two, 0, self.side, self.count, self.near)
        return jnp.concatenate((one, two), axis=1)

    def line_sum(self, both):
        total = pick(both, self.line, 0).astype(jnp.float32)
        for step in range(1, self.lines):
            other = swap(pick(both, self.line ^ step, 0), self.count, 2 * step)
            total = total + other.astype(jnp.float32)
        return total


def join(own, other, at, axis):
    own, other = jnp.expand_dims(own, axis), jnp.expand_dims(other, axis)
    shape = own.shape[:axis] + (2,) + own.shape[axis + 1 :]
    return jnp.where(lax.broadcasted_iota(jnp.int32, shape, axis) == at, own, other)


class Gather(Scatter):
    def line_all(self, own):
        shape = (self.lines,) + own.shape
        apart = lax.broadcasted_iota(jnp.int32, shape, 0) ^ self.line
        blocks = jnp.broadcast_to(own, shape)
        for step in range(1, self.lines):
            blocks = jnp.where(apart == step, swap(own, self.count, 2 * step), blocks)
        return blocks

    def open_one(self, blocks):
        half = blocks.shape[1] // 2
        one, two = blocks[:, :half], blocks[:, half:]
        one = join(one, swap(one, self.count, self.near), self.side, 0)
        two = join(two, swap(two, self.count, self.far), self.deep, 0)
        return one, two

    def open_two(self, one, two):
        one = join(one, swap(one, self.count, self.far), self.deep, 0)
        two = join(two, swap(two, self.count, self.near), self.side, 1)
        return jnp.concatenate((one, two), axis=3)

    def open_cores(self, blocks):
        whole = join(blocks, swap(blocks, self.count, 1), self.core, 3)
        return whole.reshape(-1, blocks.shape[-1])


def local_heads(
    dp_size,
    seq_size,
    tokens,
    lengths,
    w_query,
    w_key,
    w_value,
    w_out,
    w_up,
    w_down,
    b_query,
    b_value,
    b_out,
    attn_gain,
    attn_shift,
    b_up,
    b_down,
    ffn_gain,
    ffn_shift,
    cotangent,
):
    bf_type = jnp.bfloat16
    fl_type = jnp.float32
    count = dp_size * seq_size
    seqs, rows, width = tokens.shape
    full_rows = rows * seq_size
    own_rows = w_query.shape[0]
    own_units = w_down.shape[0]
    head_size = width // HEADS
    own_heads = HEADS // seq_size
    columns = own_heads * head_size
    seq_at = lax.axis_index("seq")

    stacked = jnp.stack((w_query, w_key, w_value), axis=1).reshape(own_rows, 3, seq_size, columns)
    by_owner = jnp.transpose(stacked, (2, 0, 1, 3)).reshape(seq_size, own_rows, 3 * columns)
    vectors = (b_up, b_query, b_value, b_out, attn_gain, attn_shift, b_down, ffn_gain, ffn_shift)
    small_own = jnp.concatenate(vectors)
    small_room = SMALL_ROWS * 3 * columns
    small_block = jnp.pad(small_own, (0, small_room - small_own.shape[0])).reshape(SMALL_ROWS, 3 * columns)
    payload = jnp.concatenate(
        (by_owner, jnp.broadcast_to(small_block[None], (seq_size, SMALL_ROWS, 3 * columns))), axis=1
    )
    gather = Gather(dp_size, seq_size)
    arrived = exchange(payload, "seq", 0, 0)
    arrived = join(arrived, swap(arrived, count, gather.near), gather.side, 0)
    arrived = join(arrived, swap(arrived, count, gather.far), gather.deep, 0)
    arrived = arrived.reshape(count, own_rows + SMALL_ROWS, 3 * columns)
    head_weights = arrived[:, :own_rows].reshape(width, 3 * columns)
    small_all = arrived[:, own_rows:].reshape(count, small_room)
    full_vectors = []
    at = 0
    for item in vectors:
        size = item.shape[0]
        full_vectors.append(small_all[:, at : at + size].reshape(count * size).astype(fl_type))
        at += size
    (
        bias_up,
        bias_query,
        bias_value,
        bias_out,
        gain_one,
        shift_one,
        bias_down,
        gain_two,
        shift_two,
    ) = full_vectors

    all_tokens = lax.all_gather(tokens, "seq", axis=1, tiled=True)
    out_up = lax.all_gather(jnp.concatenate((w_out, w_up), axis=1), BOTH, axis=0, tiled=True)

    own_bias = jnp.concatenate(
        (
            lax.dynamic_slice_in_dim(bias_query, seq_at * columns, columns),
            jnp.zeros((columns,), fl_type),
            lax.dynamic_slice_in_dim(bias_value, seq_at * columns, columns),
        )
    )
    mixed = (project(all_tokens, head_weights) + own_bias).astype(bf_type)
    mixed, own_down = tie(mixed, w_down)
    down = gather.line_all(own_down)
    mixed = mixed.reshape(seqs, full_rows, 3, own_heads, head_size)
    query, keys, values = mixed[:, :, 0], mixed[:, :, 1], mixed[:, :, 2]
    keep = key_valid(lengths, jnp.int32(0), full_rows)
    scores = jnp.einsum("sqhd,skhd->shqk", query, keys, preferred_element_type=fl_type) * score_scale
    row_max = jnp.max(jnp.where(keep, scores, masked_score), axis=-1)
    exps = jnp.where(keep, jnp.exp(scores - row_max[..., None]), 0.0)
    row_sum = jnp.sum(exps, axis=-1)
    context = jnp.einsum("shqk,skhd->sqhd", exps.astype(bf_type), values, preferred_element_type=fl_type)
    context = context / jnp.transpose(row_sum, (0, 2, 1))[..., None]
    log_sum = row_max + jnp.log(row_sum)
    attn_heads = context.reshape(seqs, full_rows, columns).astype(bf_type)
    attn_heads, down = tie(attn_heads, down)
    down = gather.open_one(down)
    attn = exchange(attn_heads, "seq", 1, 2)
    attn, down = tie(attn, down)
    down = gather.open_two(*down)
    out_up, down = tie(out_up, down)
    full_down = gather.open_cores(down)
    full_out, full_up = out_up[:, :width], out_up[:, width:]
    own_qkv = jnp.concatenate((w_query, w_key, w_value), axis=1)
    full_qkv = lax.all_gather(own_qkv, BOTH, axis=0, tiled=True)

    resid = tokens.astype(fl_type) + project(attn, full_out) + bias_out
    first = layer_norm(resid, gain_one, shift_one).astype(bf_type)
    inner = project(first, full_up) + bias_up
    active = gelu_exact(inner).astype(bf_type)
    second = first.astype(fl_type) + project(active, full_down) + bias_down
    out_f, norm_two_pull = jax.vjp(layer_norm, second, gain_two, shift_two)
    out_tokens = out_f.astype(bf_type)

    scatter = Scatter(dp_size, seq_size)
    d_second, ffngain_grad, ffnshift_grad = norm_two_pull(cotangent.astype(fl_type))
    d_outer = d_second.astype(bf_type)
    downbias_grad = row_total(d_outer)
    down_terms = scatter.cores(outer_sum(active, d_outer).astype(bf_type))
    d_active = project_back(d_outer, full_down)
    gelu_value, gelu_pull = jax.vjp(gelu_exact, inner)
    d_inner = gelu_pull(d_active)[0].astype(bf_type)
    d_inner, down_terms = tie(d_inner, down_terms)
    down_one, down_two = scatter.plane_one(down_terms)
    upbias_grad = row_total(d_inner)
    upproj_grad = outer_sum(first, d_inner)
    d_first = d_second + project_back(d_inner, full_up)
    norm_one_value, norm_one_pull = jax.vjp(layer_norm, resid, gain_one, shift_one)
    d_resid, attngain_grad, attnshift_grad = norm_one_pull(d_first)
    d_attnout = d_resid.astype(bf_type)
    outbias_grad = row_total(d_attnout)
    outproj_grad = outer_sum(attn, d_attnout)
    d_attn_rows = project_back(d_attnout, full_out).astype(bf_type)
    d_attn_rows, down_one, down_two, full_qkv = tie(d_attn_rows, down_one, down_two, full_qkv)
    down_both = scatter.plane_two(down_one, down_two)
    outup_grad = jnp.concatenate((outproj_grad.astype(bf_type), upproj_grad.astype(bf_type)), axis=1)
    outup_terms = scatter.cores(outup_grad)

    d_attn = exchange(d_attn_rows, "seq", 2, 1).reshape(seqs, full_rows, own_heads, head_size)
    d_attn, outup_terms, down_both = tie(d_attn, outup_terms, down_both)
    outup_one, outup_two = scatter.plane_one(outup_terms)
    down_shard = scatter.line_sum(down_both)

    def attention_back(at, grad):
        part = slice(at, at + 1)
        query_s, keys_s, values_s, keep_s = query[part], keys[part], values[part], keep[part]
        delta = jnp.transpose(jnp.sum(grad.astype(fl_type) * context[part], axis=-1), (0, 2, 1))
        scores = jnp.einsum("sqhd,skhd->shqk", query_s, keys_s, preferred_element_type=fl_type) * score_scale
        probs = jnp.where(keep_s, jnp.exp(scores - log_sum[part][..., None]), 0.0)
        d_probs = jnp.einsum("sqhd,skhd->shqk", grad, values_s, preferred_element_type=fl_type)
        d_scores = (probs * (d_probs - delta[..., None])).astype(bf_type)
        d_query = jnp.einsum("shqk,skhd->sqhd", d_scores, keys_s, preferred_element_type=fl_type) * score_scale
        d_keys = jnp.einsum("shqk,sqhd->skhd", d_scores, query_s, preferred_element_type=fl_type) * score_scale
        d_values = jnp.einsum("shqk,sqhd->skhd", probs.astype(bf_type), grad, preferred_element_type=fl_type)
        d_mixed = jnp.stack((d_query, d_keys, d_values), axis=2).astype(bf_type)
        return d_mixed.reshape(1, full_rows, 3 * columns)

    def to_rows(d_mixed):
        spread = exchange(d_mixed.reshape(1, full_rows, 3, columns), "seq", 1, 3)
        return spread.reshape(1, rows, 3 * width)

    d_parts, d_rows = [], []
    for at in range(seqs):
        d_parts.append(attention_back(at, d_attn[at : at + 1]))
        d_rows.append(to_rows(d_parts[-1]))
        if at == 0:
            d_attn, outup_one, outup_two, down_shard = tie(d_attn, outup_one, outup_two, down_shard)
            outup_both = scatter.plane_two(outup_one, outup_two)
    d_mixed = jnp.concatenate(d_parts, axis=0)
    d_mixed, outup_both = tie(d_mixed, outup_both)
    outup_shard = scatter.line_sum(outup_both)

    mixed_grad = outer_sum(all_tokens, d_mixed).astype(bf_type).reshape(count, own_rows, 3 * columns)
    bias_mixed = row_total(d_mixed)
    empty = jnp.zeros((width,), fl_type)
    querybias_grad = lax.dynamic_update_slice_in_dim(empty, bias_mixed[:columns], seq_at * columns, 0)
    valuebias_grad = lax.dynamic_update_slice_in_dim(empty, bias_mixed[2 * columns :], seq_at * columns, 0)
    vector_grads = (
        upbias_grad,
        querybias_grad,
        valuebias_grad,
        outbias_grad,
        attngain_grad,
        attnshift_grad,
        downbias_grad,
        ffngain_grad,
        ffnshift_grad,
    )
    small_grads = jnp.concatenate([item.reshape(count, -1) for item in vector_grads], axis=1)
    small_size = small_grads.shape[1]
    small_grads = jnp.pad(small_grads, ((0, 0), (0, small_room - small_size)))
    small_grads = small_grads.reshape(count, SMALL_ROWS, 3 * columns).astype(bf_type)
    terms = jnp.concatenate((mixed_grad, small_grads), axis=1)
    terms = terms.reshape(2, 2, seq_size, own_rows + SMALL_ROWS, 3 * columns)
    terms = halve(terms, 0, scatter.deep, count, scatter.far)
    terms = halve(terms, 0, scatter.side, count, scatter.near)
    arrived = exchange(terms, "seq", 0, 0).astype(fl_type)
    qkv_shard = arrived[:, :own_rows].reshape(seq_size, own_rows, 3, columns)
    qkv_shard = jnp.transpose(qkv_shard, (2, 1, 0, 3)).reshape(3, own_rows, width)
    small_sums = jnp.sum(arrived[:, own_rows:], axis=0).reshape(small_room)
    vector_shards = []
    at = 0
    for item in vectors:
        vector_shards.append(small_sums[at : at + item.shape[0]])
        at += item.shape[0]

    d_rows = jnp.concatenate(d_rows, axis=0)
    grad_inputs = d_resid + project_back(d_rows, full_qkv)
    return (
        out_tokens,
        grad_inputs.astype(bf_type),
        qkv_shard[0],
        qkv_shard[1],
        qkv_shard[2],
        outup_shard[:, :width],
        outup_shard[:, width:],
        down_shard,
        vector_shards[1],
        vector_shards[2],
        vector_shards[3],
        vector_shards[4],
        vector_shards[5],
        vector_shards[0],
        vector_shards[6],
        vector_shards[7],
        vector_shards[8],
    )


def solution(mesh):
    seq_size = mesh.shape["seq"]
    by_heads = HEADS % seq_size == 0 and mesh.shape["dp"] == 4 and seq_size in (2, 4, 8, 16)
    body = functools.partial(local_heads, mesh.shape["dp"], seq_size) if by_heads else local_gathered
    return jax.shard_map(
        body,
        mesh=mesh,
        in_specs=(
            P("dp", "seq", None),
            P("dp"),
            P(("dp", "seq"), None),
            P(("dp", "seq"), None),
            P(("dp", "seq"), None),
            P(("dp", "seq"), None),
            P(("dp", "seq"), None),
            P(("dp", "seq"), None),
            P(("dp", "seq")),
            P(("dp", "seq")),
            P(("dp", "seq")),
            P(("dp", "seq")),
            P(("dp", "seq")),
            P(("dp", "seq")),
            P(("dp", "seq")),
            P(("dp", "seq")),
            P(("dp", "seq")),
            P("dp", "seq", None),
        ),
        out_specs=(
            P("dp", "seq", None),
            P("dp", "seq", None),
            P(("dp", "seq"), None),
            P(("dp", "seq"), None),
            P(("dp", "seq"), None),
            P(("dp", "seq"), None),
            P(("dp", "seq"), None),
            P(("dp", "seq"), None),
            P(("dp", "seq")),
            P(("dp", "seq")),
            P(("dp", "seq")),
            P(("dp", "seq")),
            P(("dp", "seq")),
            P(("dp", "seq")),
            P(("dp", "seq")),
            P(("dp", "seq")),
            P(("dp", "seq")),
        ),
        check_vma=False,
    )
```

```python
import functools

import jax
import jax.numpy as jnp
from jax import lax
from jax.sharding import PartitionSpec as P

HEADS = 16


score_scale = 0.125
epsilon = 1e-05
masked_score = -1e30


def layer_norm(values, gain, shift):
    average = jnp.mean(values, axis=-1, keepdims=True)
    centred = values - average
    variance = jnp.mean(centred * centred, axis=-1, keepdims=True)
    return centred * lax.rsqrt(variance + epsilon) * gain + shift


def gelu_exact(values):
    return jax.nn.gelu(values, approximate=False)


def project(values, weight):
    return jnp.einsum("srd,de->sre", values, weight, preferred_element_type=jnp.float32)


def project_back(grads, weight):
    return jnp.einsum("sre,de->srd", grads, weight, preferred_element_type=jnp.float32)


def outer_sum(values, grads):
    return jnp.einsum("srd,sre->de", values, grads, preferred_element_type=jnp.float32)


def row_total(grads):
    return jnp.sum(grads.astype(jnp.float32), axis=(0, 1))


def key_valid(lengths, first_index, key_count):
    places = first_index + jnp.arange(key_count, dtype=jnp.int32)
    return (places[None, :] < lengths[:, None])[:, None, None, :]


def local_gathered(
    tokens,
    lengths,
    w_query,
    w_key,
    w_value,
    w_out,
    w_up,
    w_down,
    b_query,
    b_value,
    b_out,
    attn_gain,
    attn_shift,
    b_up,
    b_down,
    ffn_gain,
    ffn_shift,
    cotangent,
):
    local_seqs, local_rows, model_width = tokens.shape
    head_count = HEADS
    head_size = model_width // head_count
    row_offset = lax.axis_index("seq") * local_rows
    bf_type = jnp.bfloat16
    fl_type = jnp.float32
    gathered = (
        lax.all_gather(w_query, ("dp", "seq"), axis=0, tiled=True),
        lax.all_gather(w_key, ("dp", "seq"), axis=0, tiled=True),
        lax.all_gather(w_value, ("dp", "seq"), axis=0, tiled=True),
        lax.all_gather(w_out, ("dp", "seq"), axis=0, tiled=True),
        lax.all_gather(w_up, ("dp", "seq"), axis=0, tiled=True),
        lax.all_gather(w_down, ("dp", "seq"), axis=0, tiled=True),
        lax.all_gather(b_query, ("dp", "seq"), axis=0, tiled=True),
        lax.all_gather(b_value, ("dp", "seq"), axis=0, tiled=True),
        lax.all_gather(b_out, ("dp", "seq"), axis=0, tiled=True),
        lax.all_gather(attn_gain, ("dp", "seq"), axis=0, tiled=True),
        lax.all_gather(attn_shift, ("dp", "seq"), axis=0, tiled=True),
        lax.all_gather(b_up, ("dp", "seq"), axis=0, tiled=True),
        lax.all_gather(b_down, ("dp", "seq"), axis=0, tiled=True),
        lax.all_gather(ffn_gain, ("dp", "seq"), axis=0, tiled=True),
        lax.all_gather(ffn_shift, ("dp", "seq"), axis=0, tiled=True),
    )
    full_query, full_key, full_value, full_out, full_up, full_down = gathered[:6]
    small_vectors = [item.astype(fl_type) for item in gathered[6:]]
    (
        bias_query,
        bias_value,
        bias_out,
        gain_one,
        shift_one,
        bias_up,
        bias_down,
        gain_two,
        shift_two,
    ) = small_vectors
    query = (project(tokens, full_query) + bias_query).astype(bf_type)
    key_rows = project(tokens, full_key).astype(bf_type)
    value_rows = (project(tokens, full_value) + bias_value).astype(bf_type)
    query_heads = query.reshape(local_seqs, local_rows, head_count, head_size)
    key_local = key_rows.reshape(local_seqs, local_rows, head_count, head_size)
    value_local = value_rows.reshape(local_seqs, local_rows, head_count, head_size)
    stat_shape = (local_seqs, head_count, local_rows)
    running_max = jnp.full(stat_shape, masked_score, fl_type)
    key_block = lax.all_gather(key_rows, "seq", axis=1, tiled=True)
    value_block = lax.all_gather(value_rows, "seq", axis=1, tiled=True)
    key_count = key_block.shape[1]
    key_heads = key_block.reshape(local_seqs, key_count, head_count, head_size)
    value_heads = value_block.reshape(local_seqs, key_count, head_count, head_size)
    scores = (
        jnp.einsum("sqhd,skhd->shqk", query_heads, key_heads, preferred_element_type=fl_type)
        * score_scale
    )
    keep_mask = key_valid(lengths, jnp.int32(0), key_count)
    new_max = jnp.maximum(running_max, jnp.max(jnp.where(keep_mask, scores, masked_score), axis=-1))
    exp_scores = jnp.where(keep_mask, jnp.exp(scores - new_max[..., None]), 0.0)
    running_sum = jnp.sum(exp_scores, axis=-1)
    update = jnp.einsum(
        "shqk,skhd->sqhd", exp_scores.astype(bf_type), value_heads, preferred_element_type=fl_type
    )
    context_sum = update
    final_max, final_sum, context_sum = (new_max, running_sum, context_sum)
    context_heads = context_sum / jnp.transpose(final_sum, (0, 2, 1))[..., None]
    log_sum = jnp.transpose(final_max + jnp.log(final_sum), (0, 2, 1))
    attn = context_heads.reshape(local_seqs, local_rows, model_width).astype(bf_type)
    resid = tokens.astype(fl_type) + project(attn, full_out) + bias_out
    first_f = layer_norm(resid, gain_one, shift_one)
    first = first_f.astype(bf_type)
    inner = project(first, full_up) + bias_up
    active = gelu_exact(inner).astype(bf_type)
    second = first.astype(fl_type) + project(active, full_down) + bias_down
    out_f, norm_two_pull = jax.vjp(layer_norm, second, gain_two, shift_two)
    out_tokens = out_f.astype(bf_type)
    back_weights = (
        lax.all_gather(w_query, ("dp", "seq"), axis=0, tiled=True),
        lax.all_gather(w_key, ("dp", "seq"), axis=0, tiled=True),
        lax.all_gather(w_value, ("dp", "seq"), axis=0, tiled=True),
        lax.all_gather(w_out, ("dp", "seq"), axis=0, tiled=True),
        lax.all_gather(w_up, ("dp", "seq"), axis=0, tiled=True),
        lax.all_gather(w_down, ("dp", "seq"), axis=0, tiled=True),
        lax.all_gather(b_query, ("dp", "seq"), axis=0, tiled=True),
        lax.all_gather(b_value, ("dp", "seq"), axis=0, tiled=True),
        lax.all_gather(b_out, ("dp", "seq"), axis=0, tiled=True),
        lax.all_gather(attn_gain, ("dp", "seq"), axis=0, tiled=True),
        lax.all_gather(attn_shift, ("dp", "seq"), axis=0, tiled=True),
        lax.all_gather(b_up, ("dp", "seq"), axis=0, tiled=True),
        lax.all_gather(b_down, ("dp", "seq"), axis=0, tiled=True),
        lax.all_gather(ffn_gain, ("dp", "seq"), axis=0, tiled=True),
        lax.all_gather(ffn_shift, ("dp", "seq"), axis=0, tiled=True),
    )
    back_query, back_key, back_value, back_out, back_up, back_down = back_weights[:6]
    d_second, ffngain_grad, ffnshift_grad = norm_two_pull(cotangent.astype(fl_type))
    d_outer = d_second.astype(bf_type)
    downbias_grad = row_total(d_outer)
    downproj_grad = outer_sum(active, d_outer)
    d_active = project_back(d_outer, back_down)
    gelu_value, gelu_pull = jax.vjp(gelu_exact, inner)
    d_inner = gelu_pull(d_active)[0].astype(bf_type)
    upbias_grad = row_total(d_inner)
    upproj_grad = outer_sum(first, d_inner)
    d_first = d_second + project_back(d_inner, back_up)
    norm_one_value, norm_one_pull = jax.vjp(layer_norm, resid, gain_one, shift_one)
    d_resid, attngain_grad, attnshift_grad = norm_one_pull(d_first)
    d_attnout = d_resid.astype(bf_type)
    outbias_grad = row_total(d_attnout)
    outproj_grad = outer_sum(attn, d_attnout)
    d_attn = project_back(d_attnout, back_out).astype(bf_type)
    d_attn_heads = d_attn.reshape(local_seqs, local_rows, head_count, head_size)
    row_delta = jnp.sum(d_attn_heads.astype(fl_type) * context_heads, axis=-1)
    lse_heads = jnp.transpose(log_sum, (0, 2, 1))
    delta_heads = jnp.transpose(row_delta, (0, 2, 1))
    key_block = lax.all_gather(key_rows, "seq", axis=1, tiled=True)
    value_block = lax.all_gather(value_rows, "seq", axis=1, tiled=True)
    key_count = key_block.shape[1]
    key_heads = key_block.reshape(local_seqs, key_count, head_count, head_size)
    value_heads = value_block.reshape(local_seqs, key_count, head_count, head_size)
    scores = (
        jnp.einsum("sqhd,skhd->shqk", query_heads, key_heads, preferred_element_type=fl_type)
        * score_scale
    )
    keep_mask = key_valid(lengths, jnp.int32(0), key_count)
    probs_block = jnp.where(keep_mask, jnp.exp(scores - lse_heads[..., None]), 0.0)
    d_probs = jnp.einsum(
        "sqhd,skhd->shqk", d_attn_heads, value_heads, preferred_element_type=fl_type
    )
    d_scores = (probs_block * (d_probs - delta_heads[..., None])).astype(bf_type)
    d_query_f = jnp.einsum("shqk,skhd->sqhd", d_scores, key_heads, preferred_element_type=fl_type)
    all_lse, all_delta = (
        lax.all_gather(log_sum, "seq", axis=1, tiled=True),
        lax.all_gather(row_delta, "seq", axis=1, tiled=True),
    )
    local_mask = key_valid(lengths, row_offset, local_rows)
    query_block = lax.all_gather(query, "seq", axis=1, tiled=True)
    grad_block = lax.all_gather(d_attn, "seq", axis=1, tiled=True)
    query_count = query_block.shape[1]
    remote_query = query_block.reshape(local_seqs, query_count, head_count, head_size)
    remote_grad = grad_block.reshape(local_seqs, query_count, head_count, head_size)
    remote_lse = jnp.transpose(all_lse, (0, 2, 1))
    remote_delta = jnp.transpose(all_delta, (0, 2, 1))
    scores = (
        jnp.einsum("sqhd,skhd->shqk", remote_query, key_local, preferred_element_type=fl_type)
        * score_scale
    )
    probs_block = jnp.where(local_mask, jnp.exp(scores - remote_lse[..., None]), 0.0)
    d_value_sum = jnp.einsum(
        "shqk,sqhd->skhd", probs_block.astype(bf_type), remote_grad, preferred_element_type=fl_type
    )
    d_probs = jnp.einsum(
        "sqhd,skhd->shqk", remote_grad, value_local, preferred_element_type=fl_type
    )
    d_scores = (probs_block * (d_probs - remote_delta[..., None])).astype(bf_type)
    d_key_sum = jnp.einsum(
        "shqk,sqhd->skhd", d_scores, remote_query, preferred_element_type=fl_type
    )
    flat_shape = (local_seqs, local_rows, model_width)
    d_query = (d_query_f * score_scale).reshape(flat_shape).astype(bf_type)
    d_key = (d_key_sum * score_scale).reshape(flat_shape).astype(bf_type)
    d_value = d_value_sum.reshape(flat_shape).astype(bf_type)
    querybias_grad = row_total(d_query)
    valuebias_grad = row_total(d_value)
    query_grad = outer_sum(tokens, d_query)
    key_grad = outer_sum(tokens, d_key)
    value_grad = outer_sum(tokens, d_value)
    grad_inputs = (
        d_resid
        + project_back(d_query, back_query)
        + project_back(d_key, back_key)
        + project_back(d_value, back_value)
    )
    shards = (
        lax.psum_scatter(query_grad, ("dp", "seq"), scatter_dimension=0, tiled=True),
        lax.psum_scatter(key_grad, ("dp", "seq"), scatter_dimension=0, tiled=True),
        lax.psum_scatter(value_grad, ("dp", "seq"), scatter_dimension=0, tiled=True),
        lax.psum_scatter(outproj_grad, ("dp", "seq"), scatter_dimension=0, tiled=True),
        lax.psum_scatter(upproj_grad, ("dp", "seq"), scatter_dimension=0, tiled=True),
        lax.psum_scatter(downproj_grad, ("dp", "seq"), scatter_dimension=0, tiled=True),
        lax.psum_scatter(querybias_grad, ("dp", "seq"), scatter_dimension=0, tiled=True),
        lax.psum_scatter(valuebias_grad, ("dp", "seq"), scatter_dimension=0, tiled=True),
        lax.psum_scatter(outbias_grad, ("dp", "seq"), scatter_dimension=0, tiled=True),
        lax.psum_scatter(attngain_grad, ("dp", "seq"), scatter_dimension=0, tiled=True),
        lax.psum_scatter(attnshift_grad, ("dp", "seq"), scatter_dimension=0, tiled=True),
        lax.psum_scatter(upbias_grad, ("dp", "seq"), scatter_dimension=0, tiled=True),
        lax.psum_scatter(downbias_grad, ("dp", "seq"), scatter_dimension=0, tiled=True),
        lax.psum_scatter(ffngain_grad, ("dp", "seq"), scatter_dimension=0, tiled=True),
        lax.psum_scatter(ffnshift_grad, ("dp", "seq"), scatter_dimension=0, tiled=True),
    )
    return (
        out_tokens,
        grad_inputs.astype(bf_type),
        shards[0],
        shards[1],
        shards[2],
        shards[3],
        shards[4],
        shards[5],
        shards[6],
        shards[7],
        shards[8],
        shards[9],
        shards[10],
        shards[11],
        shards[12],
        shards[13],
        shards[14],
    )


BOTH = ("dp", "seq")
SMALL_ROWS = 8


def exchange(values, axis, split, join):
    return lax.all_to_all(values, axis, split_axis=split, concat_axis=join, tiled=True)


def pick(values, at, axis):
    return lax.dynamic_index_in_dim(values, at, axis, keepdims=False)


def swap(values, count, flip):
    return lax.ppermute(values, BOTH, [(source, source ^ flip) for source in range(count)])


def add_rounded(left, right):
    return (left.astype(jnp.float32) + right.astype(jnp.float32)).astype(jnp.bfloat16)


def halve(values, axis, at, count, flip):
    other = swap(pick(values, 1 - at, axis), count, flip)
    return add_rounded(pick(values, at, axis), other)


def tie(*values):
    return lax.optimization_barrier(values)


class Scatter:
    def __init__(self, dp_size, seq_size):
        self.count, self.near, self.far = dp_size * seq_size, seq_size, 2 * seq_size
        self.lines = seq_size // 2
        dp_at, seq_at = lax.axis_index("dp"), lax.axis_index("seq")
        self.core, self.line = seq_at % 2, seq_at // 2
        self.side, self.deep = dp_at % 2, dp_at // 2

    def cores(self, terms):
        rows = terms.shape[0] // self.count
        blocks = terms.reshape(2, 2, self.lines, 2, rows, terms.shape[1])
        return halve(blocks, 3, self.core, self.count, 1)

    def plane_one(self, blocks):
        half = blocks.shape[3] // 2
        one = halve(blocks[..., :half, :], 1, self.side, self.count, self.near)
        two = halve(blocks[..., half:, :], 0, self.deep, self.count, self.far)
        return one, two

    def plane_two(self, one, two):
        one = halve(one, 0, self.deep, self.count, self.far)
        two = halve(two, 0, self.side, self.count, self.near)
        return jnp.concatenate((one, two), axis=1)

    def line_sum(self, both):
        total = pick(both, self.line, 0).astype(jnp.float32)
        for step in range(1, self.lines):
            other = swap(pick(both, self.line ^ step, 0), self.count, 2 * step)
            total = total + other.astype(jnp.float32)
        return total


def join(own, other, at, axis):
    own, other = jnp.expand_dims(own, axis), jnp.expand_dims(other, axis)
    shape = own.shape[:axis] + (2,) + own.shape[axis + 1 :]
    return jnp.where(lax.broadcasted_iota(jnp.int32, shape, axis) == at, own, other)


class Gather(Scatter):
    def line_all(self, own, axis=0):
        shape = own.shape[:axis] + (self.lines,) + own.shape[axis:]
        apart = lax.broadcasted_iota(jnp.int32, shape, axis) ^ self.line
        blocks = jnp.broadcast_to(jnp.expand_dims(own, axis), shape)
        for step in range(1, self.lines):
            other = jnp.expand_dims(swap(own, self.count, 2 * step), axis)
            blocks = jnp.where(apart == step, other, blocks)
        return blocks

    def open_one(self, blocks):
        half = blocks.shape[1] // 2
        one, two = blocks[:, :half], blocks[:, half:]
        one = join(one, swap(one, self.count, self.near), self.side, 0)
        two = join(two, swap(two, self.count, self.far), self.deep, 0)
        return one, two

    def open_two(self, one, two):
        one = join(one, swap(one, self.count, self.far), self.deep, 0)
        two = join(two, swap(two, self.count, self.near), self.side, 1)
        return jnp.concatenate((one, two), axis=3)

    def open_cores(self, blocks):
        whole = join(blocks, swap(blocks, self.count, 1), self.core, 3)
        return whole.reshape(-1, blocks.shape[-1])


def local_heads(
    dp_size,
    seq_size,
    tokens,
    lengths,
    w_query,
    w_key,
    w_value,
    w_out,
    w_up,
    w_down,
    b_query,
    b_value,
    b_out,
    attn_gain,
    attn_shift,
    b_up,
    b_down,
    ffn_gain,
    ffn_shift,
    cotangent,
):
    bf_type = jnp.bfloat16
    fl_type = jnp.float32
    count = dp_size * seq_size
    seqs, rows, width = tokens.shape
    full_rows = rows * seq_size
    own_rows = w_query.shape[0]
    own_units = w_down.shape[0]
    head_size = width // HEADS
    own_heads = HEADS // seq_size
    columns = own_heads * head_size
    seq_at = lax.axis_index("seq")

    stacked = jnp.stack((w_query, w_key, w_value), axis=1).reshape(own_rows, 3, seq_size, columns)
    by_owner = jnp.transpose(stacked, (2, 0, 1, 3)).reshape(seq_size, own_rows, 3 * columns)
    vectors = (b_up, b_query, b_value, b_out, attn_gain, attn_shift, b_down, ffn_gain, ffn_shift)
    small_own = jnp.concatenate(vectors)
    small_room = SMALL_ROWS * 3 * columns
    small_block = jnp.pad(small_own, (0, small_room - small_own.shape[0])).reshape(SMALL_ROWS, 3 * columns)
    payload = jnp.concatenate(
        (by_owner, jnp.broadcast_to(small_block[None], (seq_size, SMALL_ROWS, 3 * columns))), axis=1
    )
    gather = Gather(dp_size, seq_size)
    arrived = exchange(payload, "seq", 0, 0)
    arrived = join(arrived, swap(arrived, count, gather.near), gather.side, 0)
    arrived = join(arrived, swap(arrived, count, gather.far), gather.deep, 0)
    arrived = arrived.reshape(count, own_rows + SMALL_ROWS, 3 * columns)
    head_weights = arrived[:, :own_rows].reshape(width, 3 * columns)
    small_all = arrived[:, own_rows:].reshape(count, small_room)
    full_vectors = []
    at = 0
    for item in vectors:
        size = item.shape[0]
        full_vectors.append(small_all[:, at : at + size].reshape(count * size).astype(fl_type))
        at += size
    (
        bias_up,
        bias_query,
        bias_value,
        bias_out,
        gain_one,
        shift_one,
        bias_down,
        gain_two,
        shift_two,
    ) = full_vectors

    spread = gather.line_all(tokens, 1)
    spread = join(spread, swap(spread, count, 1), gather.core, 2)
    all_tokens = spread.reshape(seqs, full_rows, width)
    out_up = lax.all_gather(jnp.concatenate((w_out, w_up), axis=1), BOTH, axis=0, tiled=True)

    own_bias = jnp.concatenate(
        (
            lax.dynamic_slice_in_dim(bias_query, seq_at * columns, columns),
            jnp.zeros((columns,), fl_type),
            lax.dynamic_slice_in_dim(bias_value, seq_at * columns, columns),
        )
    )
    mixed = (project(all_tokens, head_weights) + own_bias).astype(bf_type)
    mixed, own_down = tie(mixed, w_down)
    down = gather.line_all(own_down)
    mixed = mixed.reshape(seqs, full_rows, 3, own_heads, head_size)
    query, keys, values = mixed[:, :, 0], mixed[:, :, 1], mixed[:, :, 2]
    keep = key_valid(lengths, jnp.int32(0), full_rows)
    scores = jnp.einsum("sqhd,skhd->shqk", query, keys, preferred_element_type=fl_type) * score_scale
    row_max = jnp.max(jnp.where(keep, scores, masked_score), axis=-1)
    exps = jnp.where(keep, jnp.exp(scores - row_max[..., None]), 0.0)
    row_sum = jnp.sum(exps, axis=-1)
    context = jnp.einsum("shqk,skhd->sqhd", exps.astype(bf_type), values, preferred_element_type=fl_type)
    context = context / jnp.transpose(row_sum, (0, 2, 1))[..., None]
    log_sum = row_max + jnp.log(row_sum)
    attn_heads = context.reshape(seqs, full_rows, columns).astype(bf_type)
    attn_heads, down = tie(attn_heads, down)
    down = gather.open_one(down)
    attn = exchange(attn_heads, "seq", 1, 2)
    attn, down = tie(attn, down)
    down = gather.open_two(*down)
    out_up, down = tie(out_up, down)
    full_down = gather.open_cores(down)
    full_out, full_up = out_up[:, :width], out_up[:, width:]
    own_qkv = jnp.concatenate((w_query, w_key, w_value), axis=1)
    full_qkv = lax.all_gather(own_qkv, BOTH, axis=0, tiled=True)

    resid = tokens.astype(fl_type) + project(attn, full_out) + bias_out
    first = layer_norm(resid, gain_one, shift_one).astype(bf_type)
    inner = project(first, full_up) + bias_up
    active = gelu_exact(inner).astype(bf_type)
    second = first.astype(fl_type) + project(active, full_down) + bias_down
    out_f, norm_two_pull = jax.vjp(layer_norm, second, gain_two, shift_two)
    out_tokens = out_f.astype(bf_type)

    scatter = Scatter(dp_size, seq_size)
    d_second, ffngain_grad, ffnshift_grad = norm_two_pull(cotangent.astype(fl_type))
    d_outer = d_second.astype(bf_type)
    downbias_grad = row_total(d_outer)
    down_terms = scatter.cores(outer_sum(active, d_outer).astype(bf_type))
    d_active = project_back(d_outer, full_down)
    gelu_value, gelu_pull = jax.vjp(gelu_exact, inner)
    d_inner = gelu_pull(d_active)[0].astype(bf_type)
    d_inner, down_terms = tie(d_inner, down_terms)
    down_one, down_two = scatter.plane_one(down_terms)
    upbias_grad = row_total(d_inner)
    upproj_grad = outer_sum(first, d_inner)
    d_first = d_second + project_back(d_inner, full_up)
    d_first, full_qkv = tie(d_first, full_qkv)
    norm_one_value, norm_one_pull = jax.vjp(layer_norm, resid, gain_one, shift_one)
    d_resid, attngain_grad, attnshift_grad = norm_one_pull(d_first)
    d_attnout = d_resid.astype(bf_type)
    outbias_grad = row_total(d_attnout)
    outproj_grad = outer_sum(attn, d_attnout)
    d_attn_rows = project_back(d_attnout, full_out).astype(bf_type)
    d_attn_rows, down_one, down_two = tie(d_attn_rows, down_one, down_two)
    down_both = scatter.plane_two(down_one, down_two)
    outup_grad = jnp.concatenate((outproj_grad.astype(bf_type), upproj_grad.astype(bf_type)), axis=1)
    outup_terms = scatter.cores(outup_grad)

    d_attn = exchange(d_attn_rows, "seq", 2, 1).reshape(seqs, full_rows, own_heads, head_size)
    d_attn, outup_terms, down_both = tie(d_attn, outup_terms, down_both)
    outup_one, outup_two = scatter.plane_one(outup_terms)
    down_shard = scatter.line_sum(down_both)

    def attention_back(at, grad):
        part = slice(at, at + 1)
        query_s, keys_s, values_s, keep_s = query[part], keys[part], values[part], keep[part]
        delta = jnp.transpose(jnp.sum(grad.astype(fl_type) * context[part], axis=-1), (0, 2, 1))
        scores = jnp.einsum("sqhd,skhd->shqk", query_s, keys_s, preferred_element_type=fl_type) * score_scale
        probs = jnp.where(keep_s, jnp.exp(scores - log_sum[part][..., None]), 0.0)
        d_probs = jnp.einsum("sqhd,skhd->shqk", grad, values_s, preferred_element_type=fl_type)
        d_scores = (probs * (d_probs - delta[..., None])).astype(bf_type)
        d_query = jnp.einsum("shqk,skhd->sqhd", d_scores, keys_s, preferred_element_type=fl_type) * score_scale
        d_keys = jnp.einsum("shqk,sqhd->skhd", d_scores, query_s, preferred_element_type=fl_type) * score_scale
        d_values = jnp.einsum("shqk,sqhd->skhd", probs.astype(bf_type), grad, preferred_element_type=fl_type)
        d_mixed = jnp.stack((d_query, d_keys, d_values), axis=2).astype(bf_type)
        return d_mixed.reshape(1, full_rows, 3 * columns)

    def to_rows(d_mixed):
        spread = exchange(d_mixed.reshape(1, full_rows, 3, columns), "seq", 1, 3)
        return spread.reshape(1, rows, 3 * width)

    d_parts, d_rows = [], []
    for at in range(seqs):
        d_parts.append(attention_back(at, d_attn[at : at + 1]))
        d_rows.append(to_rows(d_parts[-1]))
        if at == 0:
            d_attn, outup_one, outup_two, down_shard = tie(d_attn, outup_one, outup_two, down_shard)
            outup_both = scatter.plane_two(outup_one, outup_two)
    d_mixed = jnp.concatenate(d_parts, axis=0)
    d_mixed, outup_both = tie(d_mixed, outup_both)
    outup_shard = scatter.line_sum(outup_both)

    mixed_grad = outer_sum(all_tokens, d_mixed).astype(bf_type).reshape(count, own_rows, 3 * columns)
    bias_mixed = row_total(d_mixed)
    empty = jnp.zeros((width,), fl_type)
    querybias_grad = lax.dynamic_update_slice_in_dim(empty, bias_mixed[:columns], seq_at * columns, 0)
    valuebias_grad = lax.dynamic_update_slice_in_dim(empty, bias_mixed[2 * columns :], seq_at * columns, 0)
    vector_grads = (
        upbias_grad,
        querybias_grad,
        valuebias_grad,
        outbias_grad,
        attngain_grad,
        attnshift_grad,
        downbias_grad,
        ffngain_grad,
        ffnshift_grad,
    )
    small_grads = jnp.concatenate([item.reshape(count, -1) for item in vector_grads], axis=1)
    small_size = small_grads.shape[1]
    small_grads = jnp.pad(small_grads, ((0, 0), (0, small_room - small_size)))
    small_grads = small_grads.reshape(count, SMALL_ROWS, 3 * columns).astype(bf_type)
    terms = jnp.concatenate((mixed_grad, small_grads), axis=1)
    terms = terms.reshape(2, 2, seq_size, own_rows + SMALL_ROWS, 3 * columns)
    terms = halve(terms, 0, scatter.deep, count, scatter.far)
    terms = halve(terms, 0, scatter.side, count, scatter.near)
    arrived = exchange(terms, "seq", 0, 0).astype(fl_type)
    qkv_shard = arrived[:, :own_rows].reshape(seq_size, own_rows, 3, columns)
    qkv_shard = jnp.transpose(qkv_shard, (2, 1, 0, 3)).reshape(3, own_rows, width)
    small_sums = jnp.sum(arrived[:, own_rows:], axis=0).reshape(small_room)
    vector_shards = []
    at = 0
    for item in vectors:
        vector_shards.append(small_sums[at : at + item.shape[0]])
        at += item.shape[0]

    d_rows = jnp.concatenate(d_rows, axis=0)
    grad_inputs = d_resid + project_back(d_rows, full_qkv)
    return (
        out_tokens,
        grad_inputs.astype(bf_type),
        qkv_shard[0],
        qkv_shard[1],
        qkv_shard[2],
        outup_shard[:, :width],
        outup_shard[:, width:],
        down_shard,
        vector_shards[1],
        vector_shards[2],
        vector_shards[3],
        vector_shards[4],
        vector_shards[5],
        vector_shards[0],
        vector_shards[6],
        vector_shards[7],
        vector_shards[8],
    )


def solution(mesh):
    seq_size = mesh.shape["seq"]
    by_heads = HEADS % seq_size == 0 and mesh.shape["dp"] == 4 and seq_size in (2, 4, 8, 16)
    body = functools.partial(local_heads, mesh.shape["dp"], seq_size) if by_heads else local_gathered
    return jax.shard_map(
        body,
        mesh=mesh,
        in_specs=(
            P("dp", "seq", None),
            P("dp"),
            P(("dp", "seq"), None),
            P(("dp", "seq"), None),
            P(("dp", "seq"), None),
            P(("dp", "seq"), None),
            P(("dp", "seq"), None),
            P(("dp", "seq"), None),
            P(("dp", "seq")),
            P(("dp", "seq")),
            P(("dp", "seq")),
            P(("dp", "seq")),
            P(("dp", "seq")),
            P(("dp", "seq")),
            P(("dp", "seq")),
            P(("dp", "seq")),
            P(("dp", "seq")),
            P("dp", "seq", None),
        ),
        out_specs=(
            P("dp", "seq", None),
            P("dp", "seq", None),
            P(("dp", "seq"), None),
            P(("dp", "seq"), None),
            P(("dp", "seq"), None),
            P(("dp", "seq"), None),
            P(("dp", "seq"), None),
            P(("dp", "seq"), None),
            P(("dp", "seq")),
            P(("dp", "seq")),
            P(("dp", "seq")),
            P(("dp", "seq")),
            P(("dp", "seq")),
            P(("dp", "seq")),
            P(("dp", "seq")),
            P(("dp", "seq")),
            P(("dp", "seq")),
        ),
        check_vma=False,
    )
```

```python
import functools

import jax
import jax.numpy as jnp
from jax import lax
from jax.sharding import PartitionSpec as P

HEADS = 16


score_scale = 0.125
epsilon = 1e-05
masked_score = -1e30


def layer_norm(values, gain, shift):
    average = jnp.mean(values, axis=-1, keepdims=True)
    centred = values - average
    variance = jnp.mean(centred * centred, axis=-1, keepdims=True)
    return centred * lax.rsqrt(variance + epsilon) * gain + shift


def gelu_exact(values):
    return jax.nn.gelu(values, approximate=False)


def project(values, weight):
    return jnp.einsum("srd,de->sre", values, weight, preferred_element_type=jnp.float32)


def project_back(grads, weight):
    return jnp.einsum("sre,de->srd", grads, weight, preferred_element_type=jnp.float32)


def outer_sum(values, grads):
    return jnp.einsum("srd,sre->de", values, grads, preferred_element_type=jnp.float32)


def row_total(grads):
    return jnp.sum(grads.astype(jnp.float32), axis=(0, 1))


def key_valid(lengths, first_index, key_count):
    places = first_index + jnp.arange(key_count, dtype=jnp.int32)
    return (places[None, :] < lengths[:, None])[:, None, None, :]


def local_gathered(
    tokens,
    lengths,
    w_query,
    w_key,
    w_value,
    w_out,
    w_up,
    w_down,
    b_query,
    b_value,
    b_out,
    attn_gain,
    attn_shift,
    b_up,
    b_down,
    ffn_gain,
    ffn_shift,
    cotangent,
):
    local_seqs, local_rows, model_width = tokens.shape
    head_count = HEADS
    head_size = model_width // head_count
    row_offset = lax.axis_index("seq") * local_rows
    bf_type = jnp.bfloat16
    fl_type = jnp.float32
    gathered = (
        lax.all_gather(w_query, ("dp", "seq"), axis=0, tiled=True),
        lax.all_gather(w_key, ("dp", "seq"), axis=0, tiled=True),
        lax.all_gather(w_value, ("dp", "seq"), axis=0, tiled=True),
        lax.all_gather(w_out, ("dp", "seq"), axis=0, tiled=True),
        lax.all_gather(w_up, ("dp", "seq"), axis=0, tiled=True),
        lax.all_gather(w_down, ("dp", "seq"), axis=0, tiled=True),
        lax.all_gather(b_query, ("dp", "seq"), axis=0, tiled=True),
        lax.all_gather(b_value, ("dp", "seq"), axis=0, tiled=True),
        lax.all_gather(b_out, ("dp", "seq"), axis=0, tiled=True),
        lax.all_gather(attn_gain, ("dp", "seq"), axis=0, tiled=True),
        lax.all_gather(attn_shift, ("dp", "seq"), axis=0, tiled=True),
        lax.all_gather(b_up, ("dp", "seq"), axis=0, tiled=True),
        lax.all_gather(b_down, ("dp", "seq"), axis=0, tiled=True),
        lax.all_gather(ffn_gain, ("dp", "seq"), axis=0, tiled=True),
        lax.all_gather(ffn_shift, ("dp", "seq"), axis=0, tiled=True),
    )
    full_query, full_key, full_value, full_out, full_up, full_down = gathered[:6]
    small_vectors = [item.astype(fl_type) for item in gathered[6:]]
    (
        bias_query,
        bias_value,
        bias_out,
        gain_one,
        shift_one,
        bias_up,
        bias_down,
        gain_two,
        shift_two,
    ) = small_vectors
    query = (project(tokens, full_query) + bias_query).astype(bf_type)
    key_rows = project(tokens, full_key).astype(bf_type)
    value_rows = (project(tokens, full_value) + bias_value).astype(bf_type)
    query_heads = query.reshape(local_seqs, local_rows, head_count, head_size)
    key_local = key_rows.reshape(local_seqs, local_rows, head_count, head_size)
    value_local = value_rows.reshape(local_seqs, local_rows, head_count, head_size)
    stat_shape = (local_seqs, head_count, local_rows)
    running_max = jnp.full(stat_shape, masked_score, fl_type)
    key_block = lax.all_gather(key_rows, "seq", axis=1, tiled=True)
    value_block = lax.all_gather(value_rows, "seq", axis=1, tiled=True)
    key_count = key_block.shape[1]
    key_heads = key_block.reshape(local_seqs, key_count, head_count, head_size)
    value_heads = value_block.reshape(local_seqs, key_count, head_count, head_size)
    scores = (
        jnp.einsum("sqhd,skhd->shqk", query_heads, key_heads, preferred_element_type=fl_type)
        * score_scale
    )
    keep_mask = key_valid(lengths, jnp.int32(0), key_count)
    new_max = jnp.maximum(running_max, jnp.max(jnp.where(keep_mask, scores, masked_score), axis=-1))
    exp_scores = jnp.where(keep_mask, jnp.exp(scores - new_max[..., None]), 0.0)
    running_sum = jnp.sum(exp_scores, axis=-1)
    update = jnp.einsum(
        "shqk,skhd->sqhd", exp_scores.astype(bf_type), value_heads, preferred_element_type=fl_type
    )
    context_sum = update
    final_max, final_sum, context_sum = (new_max, running_sum, context_sum)
    context_heads = context_sum / jnp.transpose(final_sum, (0, 2, 1))[..., None]
    log_sum = jnp.transpose(final_max + jnp.log(final_sum), (0, 2, 1))
    attn = context_heads.reshape(local_seqs, local_rows, model_width).astype(bf_type)
    resid = tokens.astype(fl_type) + project(attn, full_out) + bias_out
    first_f = layer_norm(resid, gain_one, shift_one)
    first = first_f.astype(bf_type)
    inner = project(first, full_up) + bias_up
    active = gelu_exact(inner).astype(bf_type)
    second = first.astype(fl_type) + project(active, full_down) + bias_down
    out_f, norm_two_pull = jax.vjp(layer_norm, second, gain_two, shift_two)
    out_tokens = out_f.astype(bf_type)
    back_weights = (
        lax.all_gather(w_query, ("dp", "seq"), axis=0, tiled=True),
        lax.all_gather(w_key, ("dp", "seq"), axis=0, tiled=True),
        lax.all_gather(w_value, ("dp", "seq"), axis=0, tiled=True),
        lax.all_gather(w_out, ("dp", "seq"), axis=0, tiled=True),
        lax.all_gather(w_up, ("dp", "seq"), axis=0, tiled=True),
        lax.all_gather(w_down, ("dp", "seq"), axis=0, tiled=True),
        lax.all_gather(b_query, ("dp", "seq"), axis=0, tiled=True),
        lax.all_gather(b_value, ("dp", "seq"), axis=0, tiled=True),
        lax.all_gather(b_out, ("dp", "seq"), axis=0, tiled=True),
        lax.all_gather(attn_gain, ("dp", "seq"), axis=0, tiled=True),
        lax.all_gather(attn_shift, ("dp", "seq"), axis=0, tiled=True),
        lax.all_gather(b_up, ("dp", "seq"), axis=0, tiled=True),
        lax.all_gather(b_down, ("dp", "seq"), axis=0, tiled=True),
        lax.all_gather(ffn_gain, ("dp", "seq"), axis=0, tiled=True),
        lax.all_gather(ffn_shift, ("dp", "seq"), axis=0, tiled=True),
    )
    back_query, back_key, back_value, back_out, back_up, back_down = back_weights[:6]
    d_second, ffngain_grad, ffnshift_grad = norm_two_pull(cotangent.astype(fl_type))
    d_outer = d_second.astype(bf_type)
    downbias_grad = row_total(d_outer)
    downproj_grad = outer_sum(active, d_outer)
    d_active = project_back(d_outer, back_down)
    gelu_value, gelu_pull = jax.vjp(gelu_exact, inner)
    d_inner = gelu_pull(d_active)[0].astype(bf_type)
    upbias_grad = row_total(d_inner)
    upproj_grad = outer_sum(first, d_inner)
    d_first = d_second + project_back(d_inner, back_up)
    norm_one_value, norm_one_pull = jax.vjp(layer_norm, resid, gain_one, shift_one)
    d_resid, attngain_grad, attnshift_grad = norm_one_pull(d_first)
    d_attnout = d_resid.astype(bf_type)
    outbias_grad = row_total(d_attnout)
    outproj_grad = outer_sum(attn, d_attnout)
    d_attn = project_back(d_attnout, back_out).astype(bf_type)
    d_attn_heads = d_attn.reshape(local_seqs, local_rows, head_count, head_size)
    row_delta = jnp.sum(d_attn_heads.astype(fl_type) * context_heads, axis=-1)
    lse_heads = jnp.transpose(log_sum, (0, 2, 1))
    delta_heads = jnp.transpose(row_delta, (0, 2, 1))
    key_block = lax.all_gather(key_rows, "seq", axis=1, tiled=True)
    value_block = lax.all_gather(value_rows, "seq", axis=1, tiled=True)
    key_count = key_block.shape[1]
    key_heads = key_block.reshape(local_seqs, key_count, head_count, head_size)
    value_heads = value_block.reshape(local_seqs, key_count, head_count, head_size)
    scores = (
        jnp.einsum("sqhd,skhd->shqk", query_heads, key_heads, preferred_element_type=fl_type)
        * score_scale
    )
    keep_mask = key_valid(lengths, jnp.int32(0), key_count)
    probs_block = jnp.where(keep_mask, jnp.exp(scores - lse_heads[..., None]), 0.0)
    d_probs = jnp.einsum(
        "sqhd,skhd->shqk", d_attn_heads, value_heads, preferred_element_type=fl_type
    )
    d_scores = (probs_block * (d_probs - delta_heads[..., None])).astype(bf_type)
    d_query_f = jnp.einsum("shqk,skhd->sqhd", d_scores, key_heads, preferred_element_type=fl_type)
    all_lse, all_delta = (
        lax.all_gather(log_sum, "seq", axis=1, tiled=True),
        lax.all_gather(row_delta, "seq", axis=1, tiled=True),
    )
    local_mask = key_valid(lengths, row_offset, local_rows)
    query_block = lax.all_gather(query, "seq", axis=1, tiled=True)
    grad_block = lax.all_gather(d_attn, "seq", axis=1, tiled=True)
    query_count = query_block.shape[1]
    remote_query = query_block.reshape(local_seqs, query_count, head_count, head_size)
    remote_grad = grad_block.reshape(local_seqs, query_count, head_count, head_size)
    remote_lse = jnp.transpose(all_lse, (0, 2, 1))
    remote_delta = jnp.transpose(all_delta, (0, 2, 1))
    scores = (
        jnp.einsum("sqhd,skhd->shqk", remote_query, key_local, preferred_element_type=fl_type)
        * score_scale
    )
    probs_block = jnp.where(local_mask, jnp.exp(scores - remote_lse[..., None]), 0.0)
    d_value_sum = jnp.einsum(
        "shqk,sqhd->skhd", probs_block.astype(bf_type), remote_grad, preferred_element_type=fl_type
    )
    d_probs = jnp.einsum(
        "sqhd,skhd->shqk", remote_grad, value_local, preferred_element_type=fl_type
    )
    d_scores = (probs_block * (d_probs - remote_delta[..., None])).astype(bf_type)
    d_key_sum = jnp.einsum(
        "shqk,sqhd->skhd", d_scores, remote_query, preferred_element_type=fl_type
    )
    flat_shape = (local_seqs, local_rows, model_width)
    d_query = (d_query_f * score_scale).reshape(flat_shape).astype(bf_type)
    d_key = (d_key_sum * score_scale).reshape(flat_shape).astype(bf_type)
    d_value = d_value_sum.reshape(flat_shape).astype(bf_type)
    querybias_grad = row_total(d_query)
    valuebias_grad = row_total(d_value)
    query_grad = outer_sum(tokens, d_query)
    key_grad = outer_sum(tokens, d_key)
    value_grad = outer_sum(tokens, d_value)
    grad_inputs = (
        d_resid
        + project_back(d_query, back_query)
        + project_back(d_key, back_key)
        + project_back(d_value, back_value)
    )
    shards = (
        lax.psum_scatter(query_grad, ("dp", "seq"), scatter_dimension=0, tiled=True),
        lax.psum_scatter(key_grad, ("dp", "seq"), scatter_dimension=0, tiled=True),
        lax.psum_scatter(value_grad, ("dp", "seq"), scatter_dimension=0, tiled=True),
        lax.psum_scatter(outproj_grad, ("dp", "seq"), scatter_dimension=0, tiled=True),
        lax.psum_scatter(upproj_grad, ("dp", "seq"), scatter_dimension=0, tiled=True),
        lax.psum_scatter(downproj_grad, ("dp", "seq"), scatter_dimension=0, tiled=True),
        lax.psum_scatter(querybias_grad, ("dp", "seq"), scatter_dimension=0, tiled=True),
        lax.psum_scatter(valuebias_grad, ("dp", "seq"), scatter_dimension=0, tiled=True),
        lax.psum_scatter(outbias_grad, ("dp", "seq"), scatter_dimension=0, tiled=True),
        lax.psum_scatter(attngain_grad, ("dp", "seq"), scatter_dimension=0, tiled=True),
        lax.psum_scatter(attnshift_grad, ("dp", "seq"), scatter_dimension=0, tiled=True),
        lax.psum_scatter(upbias_grad, ("dp", "seq"), scatter_dimension=0, tiled=True),
        lax.psum_scatter(downbias_grad, ("dp", "seq"), scatter_dimension=0, tiled=True),
        lax.psum_scatter(ffngain_grad, ("dp", "seq"), scatter_dimension=0, tiled=True),
        lax.psum_scatter(ffnshift_grad, ("dp", "seq"), scatter_dimension=0, tiled=True),
    )
    return (
        out_tokens,
        grad_inputs.astype(bf_type),
        shards[0],
        shards[1],
        shards[2],
        shards[3],
        shards[4],
        shards[5],
        shards[6],
        shards[7],
        shards[8],
        shards[9],
        shards[10],
        shards[11],
        shards[12],
        shards[13],
        shards[14],
    )


BOTH = ("dp", "seq")
SMALL_ROWS = 8


def exchange(values, axis, split, join):
    return lax.all_to_all(values, axis, split_axis=split, concat_axis=join, tiled=True)


def pick(values, at, axis):
    return lax.dynamic_index_in_dim(values, at, axis, keepdims=False)


def swap(values, count, flip):
    return lax.ppermute(values, BOTH, [(source, source ^ flip) for source in range(count)])


def add_rounded(left, right):
    return (left.astype(jnp.float32) + right.astype(jnp.float32)).astype(jnp.bfloat16)


def halve(values, axis, at, count, flip):
    other = swap(pick(values, 1 - at, axis), count, flip)
    return add_rounded(pick(values, at, axis), other)


def tie(*values):
    return lax.optimization_barrier(values)


class Scatter:
    def __init__(self, dp_size, seq_size):
        self.count, self.near, self.far = dp_size * seq_size, seq_size, 2 * seq_size
        self.lines = seq_size // 2
        dp_at, seq_at = lax.axis_index("dp"), lax.axis_index("seq")
        self.core, self.line = seq_at % 2, seq_at // 2
        self.side, self.deep = dp_at % 2, dp_at // 2

    def cores(self, terms):
        rows = terms.shape[0] // self.count
        blocks = terms.reshape(2, 2, self.lines, 2, rows, terms.shape[1])
        return halve(blocks, 3, self.core, self.count, 1)

    def plane_one(self, blocks):
        half = blocks.shape[3] // 2
        one = halve(blocks[..., :half, :], 1, self.side, self.count, self.near)
        two = halve(blocks[..., half:, :], 0, self.deep, self.count, self.far)
        return one, two

    def plane_two(self, one, two):
        one = halve(one, 0, self.deep, self.count, self.far)
        two = halve(two, 0, self.side, self.count, self.near)
        return jnp.concatenate((one, two), axis=1)

    def line_sum(self, both):
        total = pick(both, self.line, 0).astype(jnp.float32)
        for step in range(1, self.lines):
            other = swap(pick(both, self.line ^ step, 0), self.count, 2 * step)
            total = total + other.astype(jnp.float32)
        return total


def join(own, other, at, axis):
    own, other = jnp.expand_dims(own, axis), jnp.expand_dims(other, axis)
    shape = own.shape[:axis] + (2,) + own.shape[axis + 1 :]
    return jnp.where(lax.broadcasted_iota(jnp.int32, shape, axis) == at, own, other)


class Gather(Scatter):
    def line_all(self, own):
        shape = (self.lines,) + own.shape
        apart = lax.broadcasted_iota(jnp.int32, shape, 0) ^ self.line
        blocks = jnp.broadcast_to(own, shape)
        for step in range(1, self.lines):
            blocks = jnp.where(apart == step, swap(own, self.count, 2 * step), blocks)
        return blocks

    def open_one(self, blocks):
        half = blocks.shape[1] // 2
        one, two = blocks[:, :half], blocks[:, half:]
        one = join(one, swap(one, self.count, self.near), self.side, 0)
        two = join(two, swap(two, self.count, self.far), self.deep, 0)
        return one, two

    def open_two(self, one, two):
        one = join(one, swap(one, self.count, self.far), self.deep, 0)
        two = join(two, swap(two, self.count, self.near), self.side, 1)
        return jnp.concatenate((one, two), axis=3)

    def open_cores(self, blocks):
        whole = join(blocks, swap(blocks, self.count, 1), self.core, 3)
        return whole.reshape(-1, blocks.shape[-1])


def local_heads(
    dp_size,
    seq_size,
    tokens,
    lengths,
    w_query,
    w_key,
    w_value,
    w_out,
    w_up,
    w_down,
    b_query,
    b_value,
    b_out,
    attn_gain,
    attn_shift,
    b_up,
    b_down,
    ffn_gain,
    ffn_shift,
    cotangent,
):
    bf_type = jnp.bfloat16
    fl_type = jnp.float32
    count = dp_size * seq_size
    seqs, rows, width = tokens.shape
    full_rows = rows * seq_size
    own_rows = w_query.shape[0]
    own_units = w_down.shape[0]
    head_size = width // HEADS
    own_heads = HEADS // seq_size
    columns = own_heads * head_size
    seq_at = lax.axis_index("seq")

    stacked = jnp.stack((w_query, w_key, w_value), axis=1).reshape(own_rows, 3, seq_size, columns)
    by_owner = jnp.transpose(stacked, (2, 0, 1, 3)).reshape(seq_size, own_rows, 3 * columns)
    vectors = (b_up, b_query, b_value, b_out, attn_gain, attn_shift, b_down, ffn_gain, ffn_shift)
    small_own = jnp.concatenate(vectors)
    small_room = SMALL_ROWS * 3 * columns
    small_block = jnp.pad(small_own, (0, small_room - small_own.shape[0])).reshape(SMALL_ROWS, 3 * columns)
    payload = jnp.concatenate(
        (by_owner, jnp.broadcast_to(small_block[None], (seq_size, SMALL_ROWS, 3 * columns))), axis=1
    )
    gather = Gather(dp_size, seq_size)
    arrived = exchange(payload, "seq", 0, 0)
    arrived = join(arrived, swap(arrived, count, gather.near), gather.side, 0)
    arrived = join(arrived, swap(arrived, count, gather.far), gather.deep, 0)
    arrived = arrived.reshape(count, own_rows + SMALL_ROWS, 3 * columns)
    head_weights = arrived[:, :own_rows].reshape(width, 3 * columns)
    small_all = arrived[:, own_rows:].reshape(count, small_room)
    full_vectors = []
    at = 0
    for item in vectors:
        size = item.shape[0]
        full_vectors.append(small_all[:, at : at + size].reshape(count * size).astype(fl_type))
        at += size
    (
        bias_up,
        bias_query,
        bias_value,
        bias_out,
        gain_one,
        shift_one,
        bias_down,
        gain_two,
        shift_two,
    ) = full_vectors

    all_tokens = lax.all_gather(tokens, "seq", axis=1, tiled=True)
    out_up = lax.all_gather(jnp.concatenate((w_out, w_up), axis=1), BOTH, axis=0, tiled=True)

    own_bias = jnp.concatenate(
        (
            lax.dynamic_slice_in_dim(bias_query, seq_at * columns, columns),
            jnp.zeros((columns,), fl_type),
            lax.dynamic_slice_in_dim(bias_value, seq_at * columns, columns),
        )
    )
    mixed = (project(all_tokens, head_weights) + own_bias).astype(bf_type)
    mixed, own_down = tie(mixed, w_down)
    down = gather.line_all(own_down)
    mixed = mixed.reshape(seqs, full_rows, 3, own_heads, head_size)
    query, keys, values = mixed[:, :, 0], mixed[:, :, 1], mixed[:, :, 2]
    keep = key_valid(lengths, jnp.int32(0), full_rows)
    scores = jnp.einsum("sqhd,skhd->shqk", query, keys, preferred_element_type=fl_type) * score_scale
    row_max = jnp.max(jnp.where(keep, scores, masked_score), axis=-1)
    exps = jnp.where(keep, jnp.exp(scores - row_max[..., None]), 0.0)
    row_sum = jnp.sum(exps, axis=-1)
    context = jnp.einsum("shqk,skhd->sqhd", exps.astype(bf_type), values, preferred_element_type=fl_type)
    context = context / jnp.transpose(row_sum, (0, 2, 1))[..., None]
    log_sum = row_max + jnp.log(row_sum)
    attn_heads = context.reshape(seqs, full_rows, columns).astype(bf_type)
    attn_heads, down = tie(attn_heads, down)
    down = gather.open_one(down)
    attn = exchange(attn_heads, "seq", 1, 2)
    attn, down = tie(attn, down)
    down = gather.open_two(*down)
    out_up, down = tie(out_up, down)
    full_down = gather.open_cores(down)
    full_out, full_up = out_up[:, :width], out_up[:, width:]
    own_qkv = jnp.concatenate((w_query, w_key, w_value), axis=1)
    full_qkv = lax.all_gather(own_qkv, BOTH, axis=0, tiled=True)

    resid = tokens.astype(fl_type) + project(attn, full_out) + bias_out
    first = layer_norm(resid, gain_one, shift_one).astype(bf_type)
    inner = project(first, full_up) + bias_up
    active = gelu_exact(inner).astype(bf_type)
    second = first.astype(fl_type) + project(active, full_down) + bias_down
    out_f, norm_two_pull = jax.vjp(layer_norm, second, gain_two, shift_two)
    out_tokens = out_f.astype(bf_type)

    scatter = Scatter(dp_size, seq_size)
    d_second, ffngain_grad, ffnshift_grad = norm_two_pull(cotangent.astype(fl_type))
    d_outer = d_second.astype(bf_type)
    downbias_grad = row_total(d_outer)
    down_terms = scatter.cores(outer_sum(active, d_outer).astype(bf_type))
    d_active = project_back(d_outer, full_down)
    gelu_value, gelu_pull = jax.vjp(gelu_exact, inner)
    d_inner = gelu_pull(d_active)[0].astype(bf_type)
    d_inner, down_terms = tie(d_inner, down_terms)
    down_one, down_two = scatter.plane_one(down_terms)
    upbias_grad = row_total(d_inner)
    upproj_grad = outer_sum(first, d_inner)
    d_first = d_second + project_back(d_inner, full_up)
    norm_one_value, norm_one_pull = jax.vjp(layer_norm, resid, gain_one, shift_one)
    d_resid, attngain_grad, attnshift_grad = norm_one_pull(d_first)
    d_attnout = d_resid.astype(bf_type)
    outbias_grad = row_total(d_attnout)
    outproj_grad = outer_sum(attn, d_attnout)
    d_attn_rows = project_back(d_attnout, full_out).astype(bf_type)
    outup_grad = jnp.concatenate((outproj_grad.astype(bf_type), upproj_grad.astype(bf_type)), axis=1)
    outup_terms = scatter.cores(outup_grad)
    d_attn_rows, down_one, down_two, full_qkv, outup_terms = tie(
        d_attn_rows, down_one, down_two, full_qkv, outup_terms
    )
    down_both = scatter.plane_two(down_one, down_two)
    outup_one, outup_two = scatter.plane_one(outup_terms)

    d_attn = exchange(d_attn_rows, "seq", 2, 1).reshape(seqs, full_rows, own_heads, head_size)
    d_attn, outup_one, outup_two, down_both = tie(d_attn, outup_one, outup_two, down_both)
    outup_both = scatter.plane_two(outup_one, outup_two)
    down_shard = scatter.line_sum(down_both)

    def attention_back(at, grad):
        part = slice(at, at + 1)
        query_s, keys_s, values_s, keep_s = query[part], keys[part], values[part], keep[part]
        delta = jnp.transpose(jnp.sum(grad.astype(fl_type) * context[part], axis=-1), (0, 2, 1))
        scores = jnp.einsum("sqhd,skhd->shqk", query_s, keys_s, preferred_element_type=fl_type) * score_scale
        probs = jnp.where(keep_s, jnp.exp(scores - log_sum[part][..., None]), 0.0)
        d_probs = jnp.einsum("sqhd,skhd->shqk", grad, values_s, preferred_element_type=fl_type)
        d_scores = (probs * (d_probs - delta[..., None])).astype(bf_type)
        d_query = jnp.einsum("shqk,skhd->sqhd", d_scores, keys_s, preferred_element_type=fl_type) * score_scale
        d_keys = jnp.einsum("shqk,sqhd->skhd", d_scores, query_s, preferred_element_type=fl_type) * score_scale
        d_values = jnp.einsum("shqk,sqhd->skhd", probs.astype(bf_type), grad, preferred_element_type=fl_type)
        d_mixed = jnp.stack((d_query, d_keys, d_values), axis=2).astype(bf_type)
        return d_mixed.reshape(1, full_rows, 3 * columns)

    def to_rows(d_mixed):
        spread = exchange(d_mixed.reshape(1, full_rows, 3, columns), "seq", 1, 3)
        return spread.reshape(1, rows, 3 * width)

    d_parts, d_rows = [], []
    for at in range(seqs):
        d_parts.append(attention_back(at, d_attn[at : at + 1]))
        d_rows.append(to_rows(d_parts[-1]))
        if at == 0:
            d_attn, outup_both, down_shard = tie(d_attn, outup_both, down_shard)
            outup_shard = scatter.line_sum(outup_both)
    d_mixed = jnp.concatenate(d_parts, axis=0)
    d_mixed, outup_shard = tie(d_mixed, outup_shard)

    mixed_grad = outer_sum(all_tokens, d_mixed).astype(bf_type).reshape(count, own_rows, 3 * columns)
    bias_mixed = row_total(d_mixed)
    empty = jnp.zeros((width,), fl_type)
    querybias_grad = lax.dynamic_update_slice_in_dim(empty, bias_mixed[:columns], seq_at * columns, 0)
    valuebias_grad = lax.dynamic_update_slice_in_dim(empty, bias_mixed[2 * columns :], seq_at * columns, 0)
    vector_grads = (
        upbias_grad,
        querybias_grad,
        valuebias_grad,
        outbias_grad,
        attngain_grad,
        attnshift_grad,
        downbias_grad,
        ffngain_grad,
        ffnshift_grad,
    )
    small_grads = jnp.concatenate([item.reshape(count, -1) for item in vector_grads], axis=1)
    small_size = small_grads.shape[1]
    small_grads = jnp.pad(small_grads, ((0, 0), (0, small_room - small_size)))
    small_grads = small_grads.reshape(count, SMALL_ROWS, 3 * columns).astype(bf_type)
    terms = jnp.concatenate((mixed_grad, small_grads), axis=1)
    terms = terms.reshape(2, 2, seq_size, own_rows + SMALL_ROWS, 3 * columns)
    terms = halve(terms, 0, scatter.deep, count, scatter.far)
    terms = halve(terms, 0, scatter.side, count, scatter.near)
    arrived = exchange(terms, "seq", 0, 0).astype(fl_type)
    qkv_shard = arrived[:, :own_rows].reshape(seq_size, own_rows, 3, columns)
    qkv_shard = jnp.transpose(qkv_shard, (2, 1, 0, 3)).reshape(3, own_rows, width)
    small_sums = jnp.sum(arrived[:, own_rows:], axis=0).reshape(small_room)
    vector_shards = []
    at = 0
    for item in vectors:
        vector_shards.append(small_sums[at : at + item.shape[0]])
        at += item.shape[0]

    d_rows = jnp.concatenate(d_rows, axis=0)
    grad_inputs = d_resid + project_back(d_rows, full_qkv)
    return (
        out_tokens,
        grad_inputs.astype(bf_type),
        qkv_shard[0],
        qkv_shard[1],
        qkv_shard[2],
        outup_shard[:, :width],
        outup_shard[:, width:],
        down_shard,
        vector_shards[1],
        vector_shards[2],
        vector_shards[3],
        vector_shards[4],
        vector_shards[5],
        vector_shards[0],
        vector_shards[6],
        vector_shards[7],
        vector_shards[8],
    )


def solution(mesh):
    seq_size = mesh.shape["seq"]
    by_heads = HEADS % seq_size == 0 and mesh.shape["dp"] == 4 and seq_size in (2, 4, 8, 16)
    body = functools.partial(local_heads, mesh.shape["dp"], seq_size) if by_heads else local_gathered
    return jax.shard_map(
        body,
        mesh=mesh,
        in_specs=(
            P("dp", "seq", None),
            P("dp"),
            P(("dp", "seq"), None),
            P(("dp", "seq"), None),
            P(("dp", "seq"), None),
            P(("dp", "seq"), None),
            P(("dp", "seq"), None),
            P(("dp", "seq"), None),
            P(("dp", "seq")),
            P(("dp", "seq")),
            P(("dp", "seq")),
            P(("dp", "seq")),
            P(("dp", "seq")),
            P(("dp", "seq")),
            P(("dp", "seq")),
            P(("dp", "seq")),
            P(("dp", "seq")),
            P("dp", "seq", None),
        ),
        out_specs=(
            P("dp", "seq", None),
            P("dp", "seq", None),
            P(("dp", "seq"), None),
            P(("dp", "seq"), None),
            P(("dp", "seq"), None),
            P(("dp", "seq"), None),
            P(("dp", "seq"), None),
            P(("dp", "seq"), None),
            P(("dp", "seq")),
            P(("dp", "seq")),
            P(("dp", "seq")),
            P(("dp", "seq")),
            P(("dp", "seq")),
            P(("dp", "seq")),
            P(("dp", "seq")),
            P(("dp", "seq")),
            P(("dp", "seq")),
        ),
        check_vma=False,
    )
```

```python
import functools

import jax
import jax.numpy as jnp
from jax import lax
from jax.sharding import PartitionSpec as P

HEADS = 16


score_scale = 0.125
epsilon = 1e-05
masked_score = -1e30


def layer_norm(values, gain, shift):
    average = jnp.mean(values, axis=-1, keepdims=True)
    centred = values - average
    variance = jnp.mean(centred * centred, axis=-1, keepdims=True)
    return centred * lax.rsqrt(variance + epsilon) * gain + shift


def gelu_exact(values):
    return jax.nn.gelu(values, approximate=False)


def project(values, weight):
    return jnp.einsum("srd,de->sre", values, weight, preferred_element_type=jnp.float32)


def project_back(grads, weight):
    return jnp.einsum("sre,de->srd", grads, weight, preferred_element_type=jnp.float32)


def outer_sum(values, grads):
    return jnp.einsum("srd,sre->de", values, grads, preferred_element_type=jnp.float32)


def row_total(grads):
    return jnp.sum(grads.astype(jnp.float32), axis=(0, 1))


def key_valid(lengths, first_index, key_count):
    places = first_index + jnp.arange(key_count, dtype=jnp.int32)
    return (places[None, :] < lengths[:, None])[:, None, None, :]


def local_gathered(
    tokens,
    lengths,
    w_query,
    w_key,
    w_value,
    w_out,
    w_up,
    w_down,
    b_query,
    b_value,
    b_out,
    attn_gain,
    attn_shift,
    b_up,
    b_down,
    ffn_gain,
    ffn_shift,
    cotangent,
):
    local_seqs, local_rows, model_width = tokens.shape
    head_count = HEADS
    head_size = model_width // head_count
    row_offset = lax.axis_index("seq") * local_rows
    bf_type = jnp.bfloat16
    fl_type = jnp.float32
    gathered = (
        lax.all_gather(w_query, ("dp", "seq"), axis=0, tiled=True),
        lax.all_gather(w_key, ("dp", "seq"), axis=0, tiled=True),
        lax.all_gather(w_value, ("dp", "seq"), axis=0, tiled=True),
        lax.all_gather(w_out, ("dp", "seq"), axis=0, tiled=True),
        lax.all_gather(w_up, ("dp", "seq"), axis=0, tiled=True),
        lax.all_gather(w_down, ("dp", "seq"), axis=0, tiled=True),
        lax.all_gather(b_query, ("dp", "seq"), axis=0, tiled=True),
        lax.all_gather(b_value, ("dp", "seq"), axis=0, tiled=True),
        lax.all_gather(b_out, ("dp", "seq"), axis=0, tiled=True),
        lax.all_gather(attn_gain, ("dp", "seq"), axis=0, tiled=True),
        lax.all_gather(attn_shift, ("dp", "seq"), axis=0, tiled=True),
        lax.all_gather(b_up, ("dp", "seq"), axis=0, tiled=True),
        lax.all_gather(b_down, ("dp", "seq"), axis=0, tiled=True),
        lax.all_gather(ffn_gain, ("dp", "seq"), axis=0, tiled=True),
        lax.all_gather(ffn_shift, ("dp", "seq"), axis=0, tiled=True),
    )
    full_query, full_key, full_value, full_out, full_up, full_down = gathered[:6]
    small_vectors = [item.astype(fl_type) for item in gathered[6:]]
    (
        bias_query,
        bias_value,
        bias_out,
        gain_one,
        shift_one,
        bias_up,
        bias_down,
        gain_two,
        shift_two,
    ) = small_vectors
    query = (project(tokens, full_query) + bias_query).astype(bf_type)
    key_rows = project(tokens, full_key).astype(bf_type)
    value_rows = (project(tokens, full_value) + bias_value).astype(bf_type)
    query_heads = query.reshape(local_seqs, local_rows, head_count, head_size)
    key_local = key_rows.reshape(local_seqs, local_rows, head_count, head_size)
    value_local = value_rows.reshape(local_seqs, local_rows, head_count, head_size)
    stat_shape = (local_seqs, head_count, local_rows)
    running_max = jnp.full(stat_shape, masked_score, fl_type)
    key_block = lax.all_gather(key_rows, "seq", axis=1, tiled=True)
    value_block = lax.all_gather(value_rows, "seq", axis=1, tiled=True)
    key_count = key_block.shape[1]
    key_heads = key_block.reshape(local_seqs, key_count, head_count, head_size)
    value_heads = value_block.reshape(local_seqs, key_count, head_count, head_size)
    scores = (
        jnp.einsum("sqhd,skhd->shqk", query_heads, key_heads, preferred_element_type=fl_type)
        * score_scale
    )
    keep_mask = key_valid(lengths, jnp.int32(0), key_count)
    new_max = jnp.maximum(running_max, jnp.max(jnp.where(keep_mask, scores, masked_score), axis=-1))
    exp_scores = jnp.where(keep_mask, jnp.exp(scores - new_max[..., None]), 0.0)
    running_sum = jnp.sum(exp_scores, axis=-1)
    update = jnp.einsum(
        "shqk,skhd->sqhd", exp_scores.astype(bf_type), value_heads, preferred_element_type=fl_type
    )
    context_sum = update
    final_max, final_sum, context_sum = (new_max, running_sum, context_sum)
    context_heads = context_sum / jnp.transpose(final_sum, (0, 2, 1))[..., None]
    log_sum = jnp.transpose(final_max + jnp.log(final_sum), (0, 2, 1))
    attn = context_heads.reshape(local_seqs, local_rows, model_width).astype(bf_type)
    resid = tokens.astype(fl_type) + project(attn, full_out) + bias_out
    first_f = layer_norm(resid, gain_one, shift_one)
    first = first_f.astype(bf_type)
    inner = project(first, full_up) + bias_up
    active = gelu_exact(inner).astype(bf_type)
    second = first.astype(fl_type) + project(active, full_down) + bias_down
    out_f, norm_two_pull = jax.vjp(layer_norm, second, gain_two, shift_two)
    out_tokens = out_f.astype(bf_type)
    back_weights = (
        lax.all_gather(w_query, ("dp", "seq"), axis=0, tiled=True),
        lax.all_gather(w_key, ("dp", "seq"), axis=0, tiled=True),
        lax.all_gather(w_value, ("dp", "seq"), axis=0, tiled=True),
        lax.all_gather(w_out, ("dp", "seq"), axis=0, tiled=True),
        lax.all_gather(w_up, ("dp", "seq"), axis=0, tiled=True),
        lax.all_gather(w_down, ("dp", "seq"), axis=0, tiled=True),
        lax.all_gather(b_query, ("dp", "seq"), axis=0, tiled=True),
        lax.all_gather(b_value, ("dp", "seq"), axis=0, tiled=True),
        lax.all_gather(b_out, ("dp", "seq"), axis=0, tiled=True),
        lax.all_gather(attn_gain, ("dp", "seq"), axis=0, tiled=True),
        lax.all_gather(attn_shift, ("dp", "seq"), axis=0, tiled=True),
        lax.all_gather(b_up, ("dp", "seq"), axis=0, tiled=True),
        lax.all_gather(b_down, ("dp", "seq"), axis=0, tiled=True),
        lax.all_gather(ffn_gain, ("dp", "seq"), axis=0, tiled=True),
        lax.all_gather(ffn_shift, ("dp", "seq"), axis=0, tiled=True),
    )
    back_query, back_key, back_value, back_out, back_up, back_down = back_weights[:6]
    d_second, ffngain_grad, ffnshift_grad = norm_two_pull(cotangent.astype(fl_type))
    d_outer = d_second.astype(bf_type)
    downbias_grad = row_total(d_outer)
    downproj_grad = outer_sum(active, d_outer)
    d_active = project_back(d_outer, back_down)
    gelu_value, gelu_pull = jax.vjp(gelu_exact, inner)
    d_inner = gelu_pull(d_active)[0].astype(bf_type)
    upbias_grad = row_total(d_inner)
    upproj_grad = outer_sum(first, d_inner)
    d_first = d_second + project_back(d_inner, back_up)
    norm_one_value, norm_one_pull = jax.vjp(layer_norm, resid, gain_one, shift_one)
    d_resid, attngain_grad, attnshift_grad = norm_one_pull(d_first)
    d_attnout = d_resid.astype(bf_type)
    outbias_grad = row_total(d_attnout)
    outproj_grad = outer_sum(attn, d_attnout)
    d_attn = project_back(d_attnout, back_out).astype(bf_type)
    d_attn_heads = d_attn.reshape(local_seqs, local_rows, head_count, head_size)
    row_delta = jnp.sum(d_attn_heads.astype(fl_type) * context_heads, axis=-1)
    lse_heads = jnp.transpose(log_sum, (0, 2, 1))
    delta_heads = jnp.transpose(row_delta, (0, 2, 1))
    key_block = lax.all_gather(key_rows, "seq", axis=1, tiled=True)
    value_block = lax.all_gather(value_rows, "seq", axis=1, tiled=True)
    key_count = key_block.shape[1]
    key_heads = key_block.reshape(local_seqs, key_count, head_count, head_size)
    value_heads = value_block.reshape(local_seqs, key_count, head_count, head_size)
    scores = (
        jnp.einsum("sqhd,skhd->shqk", query_heads, key_heads, preferred_element_type=fl_type)
        * score_scale
    )
    keep_mask = key_valid(lengths, jnp.int32(0), key_count)
    probs_block = jnp.where(keep_mask, jnp.exp(scores - lse_heads[..., None]), 0.0)
    d_probs = jnp.einsum(
        "sqhd,skhd->shqk", d_attn_heads, value_heads, preferred_element_type=fl_type
    )
    d_scores = (probs_block * (d_probs - delta_heads[..., None])).astype(bf_type)
    d_query_f = jnp.einsum("shqk,skhd->sqhd", d_scores, key_heads, preferred_element_type=fl_type)
    all_lse, all_delta = (
        lax.all_gather(log_sum, "seq", axis=1, tiled=True),
        lax.all_gather(row_delta, "seq", axis=1, tiled=True),
    )
    local_mask = key_valid(lengths, row_offset, local_rows)
    query_block = lax.all_gather(query, "seq", axis=1, tiled=True)
    grad_block = lax.all_gather(d_attn, "seq", axis=1, tiled=True)
    query_count = query_block.shape[1]
    remote_query = query_block.reshape(local_seqs, query_count, head_count, head_size)
    remote_grad = grad_block.reshape(local_seqs, query_count, head_count, head_size)
    remote_lse = jnp.transpose(all_lse, (0, 2, 1))
    remote_delta = jnp.transpose(all_delta, (0, 2, 1))
    scores = (
        jnp.einsum("sqhd,skhd->shqk", remote_query, key_local, preferred_element_type=fl_type)
        * score_scale
    )
    probs_block = jnp.where(local_mask, jnp.exp(scores - remote_lse[..., None]), 0.0)
    d_value_sum = jnp.einsum(
        "shqk,sqhd->skhd", probs_block.astype(bf_type), remote_grad, preferred_element_type=fl_type
    )
    d_probs = jnp.einsum(
        "sqhd,skhd->shqk", remote_grad, value_local, preferred_element_type=fl_type
    )
    d_scores = (probs_block * (d_probs - remote_delta[..., None])).astype(bf_type)
    d_key_sum = jnp.einsum(
        "shqk,sqhd->skhd", d_scores, remote_query, preferred_element_type=fl_type
    )
    flat_shape = (local_seqs, local_rows, model_width)
    d_query = (d_query_f * score_scale).reshape(flat_shape).astype(bf_type)
    d_key = (d_key_sum * score_scale).reshape(flat_shape).astype(bf_type)
    d_value = d_value_sum.reshape(flat_shape).astype(bf_type)
    querybias_grad = row_total(d_query)
    valuebias_grad = row_total(d_value)
    query_grad = outer_sum(tokens, d_query)
    key_grad = outer_sum(tokens, d_key)
    value_grad = outer_sum(tokens, d_value)
    grad_inputs = (
        d_resid
        + project_back(d_query, back_query)
        + project_back(d_key, back_key)
        + project_back(d_value, back_value)
    )
    shards = (
        lax.psum_scatter(query_grad, ("dp", "seq"), scatter_dimension=0, tiled=True),
        lax.psum_scatter(key_grad, ("dp", "seq"), scatter_dimension=0, tiled=True),
        lax.psum_scatter(value_grad, ("dp", "seq"), scatter_dimension=0, tiled=True),
        lax.psum_scatter(outproj_grad, ("dp", "seq"), scatter_dimension=0, tiled=True),
        lax.psum_scatter(upproj_grad, ("dp", "seq"), scatter_dimension=0, tiled=True),
        lax.psum_scatter(downproj_grad, ("dp", "seq"), scatter_dimension=0, tiled=True),
        lax.psum_scatter(querybias_grad, ("dp", "seq"), scatter_dimension=0, tiled=True),
        lax.psum_scatter(valuebias_grad, ("dp", "seq"), scatter_dimension=0, tiled=True),
        lax.psum_scatter(outbias_grad, ("dp", "seq"), scatter_dimension=0, tiled=True),
        lax.psum_scatter(attngain_grad, ("dp", "seq"), scatter_dimension=0, tiled=True),
        lax.psum_scatter(attnshift_grad, ("dp", "seq"), scatter_dimension=0, tiled=True),
        lax.psum_scatter(upbias_grad, ("dp", "seq"), scatter_dimension=0, tiled=True),
        lax.psum_scatter(downbias_grad, ("dp", "seq"), scatter_dimension=0, tiled=True),
        lax.psum_scatter(ffngain_grad, ("dp", "seq"), scatter_dimension=0, tiled=True),
        lax.psum_scatter(ffnshift_grad, ("dp", "seq"), scatter_dimension=0, tiled=True),
    )
    return (
        out_tokens,
        grad_inputs.astype(bf_type),
        shards[0],
        shards[1],
        shards[2],
        shards[3],
        shards[4],
        shards[5],
        shards[6],
        shards[7],
        shards[8],
        shards[9],
        shards[10],
        shards[11],
        shards[12],
        shards[13],
        shards[14],
    )


BOTH = ("dp", "seq")
SMALL_ROWS = 8


def exchange(values, axis, split, join):
    return lax.all_to_all(values, axis, split_axis=split, concat_axis=join, tiled=True)


def pick(values, at, axis):
    return lax.dynamic_index_in_dim(values, at, axis, keepdims=False)


def swap(values, count, flip):
    return lax.ppermute(values, BOTH, [(source, source ^ flip) for source in range(count)])


def add_rounded(left, right):
    return (left.astype(jnp.float32) + right.astype(jnp.float32)).astype(jnp.bfloat16)


def halve(values, axis, at, count, flip):
    other = swap(pick(values, 1 - at, axis), count, flip)
    return add_rounded(pick(values, at, axis), other)


def tie(*values):
    return lax.optimization_barrier(values)


class Scatter:
    def __init__(self, dp_size, seq_size):
        self.count, self.near, self.far = dp_size * seq_size, seq_size, 2 * seq_size
        self.lines = seq_size // 2
        dp_at, seq_at = lax.axis_index("dp"), lax.axis_index("seq")
        self.core, self.line = seq_at % 2, seq_at // 2
        self.side, self.deep = dp_at % 2, dp_at // 2

    def cores(self, terms):
        rows = terms.shape[0] // self.count
        blocks = terms.reshape(2, 2, self.lines, 2, rows, terms.shape[1])
        return halve(blocks, 3, self.core, self.count, 1)

    def plane_one(self, blocks):
        half = blocks.shape[3] // 2
        one = halve(blocks[..., :half, :], 1, self.side, self.count, self.near)
        two = halve(blocks[..., half:, :], 0, self.deep, self.count, self.far)
        return one, two

    def plane_two(self, one, two):
        one = halve(one, 0, self.deep, self.count, self.far)
        two = halve(two, 0, self.side, self.count, self.near)
        return jnp.concatenate((one, two), axis=1)

    def line_sum(self, both):
        total = pick(both, self.line, 0).astype(jnp.float32)
        for step in range(1, self.lines):
            other = swap(pick(both, self.line ^ step, 0), self.count, 2 * step)
            total = total + other.astype(jnp.float32)
        return total


def join(own, other, at, axis):
    own, other = jnp.expand_dims(own, axis), jnp.expand_dims(other, axis)
    shape = own.shape[:axis] + (2,) + own.shape[axis + 1 :]
    return jnp.where(lax.broadcasted_iota(jnp.int32, shape, axis) == at, own, other)


class Gather(Scatter):
    def line_all(self, own):
        shape = (self.lines,) + own.shape
        apart = lax.broadcasted_iota(jnp.int32, shape, 0) ^ self.line
        blocks = jnp.broadcast_to(own, shape)
        for step in range(1, self.lines):
            blocks = jnp.where(apart == step, swap(own, self.count, 2 * step), blocks)
        return blocks

    def open_one(self, blocks):
        half = blocks.shape[1] // 2
        one, two = blocks[:, :half], blocks[:, half:]
        one = join(one, swap(one, self.count, self.near), self.side, 0)
        two = join(two, swap(two, self.count, self.far), self.deep, 0)
        return one, two

    def open_two(self, one, two):
        one = join(one, swap(one, self.count, self.far), self.deep, 0)
        two = join(two, swap(two, self.count, self.near), self.side, 1)
        return jnp.concatenate((one, two), axis=3)

    def open_cores(self, blocks):
        whole = join(blocks, swap(blocks, self.count, 1), self.core, 3)
        return whole.reshape(-1, blocks.shape[-1])


def local_heads(
    dp_size,
    seq_size,
    tokens,
    lengths,
    w_query,
    w_key,
    w_value,
    w_out,
    w_up,
    w_down,
    b_query,
    b_value,
    b_out,
    attn_gain,
    attn_shift,
    b_up,
    b_down,
    ffn_gain,
    ffn_shift,
    cotangent,
):
    bf_type = jnp.bfloat16
    fl_type = jnp.float32
    count = dp_size * seq_size
    seqs, rows, width = tokens.shape
    full_rows = rows * seq_size
    own_rows = w_query.shape[0]
    own_units = w_down.shape[0]
    head_size = width // HEADS
    own_heads = HEADS // seq_size
    columns = own_heads * head_size
    seq_at = lax.axis_index("seq")

    stacked = jnp.stack((w_query, w_key, w_value), axis=1).reshape(own_rows, 3, seq_size, columns)
    by_owner = jnp.transpose(stacked, (2, 0, 1, 3)).reshape(seq_size, own_rows, 3 * columns)
    vectors = (b_up, b_query, b_value, b_out, attn_gain, attn_shift, b_down, ffn_gain, ffn_shift)
    small_own = jnp.concatenate(vectors)
    small_room = SMALL_ROWS * 3 * columns
    small_block = jnp.pad(small_own, (0, small_room - small_own.shape[0])).reshape(SMALL_ROWS, 3 * columns)
    payload = jnp.concatenate(
        (by_owner, jnp.broadcast_to(small_block[None], (seq_size, SMALL_ROWS, 3 * columns))), axis=1
    )
    gather = Gather(dp_size, seq_size)
    arrived = exchange(payload, "seq", 0, 0)
    arrived = join(arrived, swap(arrived, count, gather.near), gather.side, 0)
    arrived = join(arrived, swap(arrived, count, gather.far), gather.deep, 0)
    arrived = arrived.reshape(count, own_rows + SMALL_ROWS, 3 * columns)
    head_weights = arrived[:, :own_rows].reshape(width, 3 * columns)
    small_all = arrived[:, own_rows:].reshape(count, small_room)
    full_vectors = []
    at = 0
    for item in vectors:
        size = item.shape[0]
        full_vectors.append(small_all[:, at : at + size].reshape(count * size).astype(fl_type))
        at += size
    (
        bias_up,
        bias_query,
        bias_value,
        bias_out,
        gain_one,
        shift_one,
        bias_down,
        gain_two,
        shift_two,
    ) = full_vectors

    all_tokens = lax.all_gather(tokens, "seq", axis=1, tiled=True)
    out_up = lax.all_gather(jnp.concatenate((w_out, w_up), axis=1), BOTH, axis=0, tiled=True)

    own_bias = jnp.concatenate(
        (
            lax.dynamic_slice_in_dim(bias_query, seq_at * columns, columns),
            jnp.zeros((columns,), fl_type),
            lax.dynamic_slice_in_dim(bias_value, seq_at * columns, columns),
        )
    )
    mixed = (project(all_tokens, head_weights) + own_bias).astype(bf_type)
    mixed, own_down = tie(mixed, w_down)
    down = gather.line_all(own_down)
    mixed = mixed.reshape(seqs, full_rows, 3, own_heads, head_size)
    query, keys, values = mixed[:, :, 0], mixed[:, :, 1], mixed[:, :, 2]
    keep = key_valid(lengths, jnp.int32(0), full_rows)
    scores = jnp.einsum("sqhd,skhd->shqk", query, keys, preferred_element_type=fl_type) * score_scale
    row_max = jnp.max(jnp.where(keep, scores, masked_score), axis=-1)
    exps = jnp.where(keep, jnp.exp(scores - row_max[..., None]), 0.0)
    row_sum = jnp.sum(exps, axis=-1)
    context = jnp.einsum("shqk,skhd->sqhd", exps.astype(bf_type), values, preferred_element_type=fl_type)
    context = context / jnp.transpose(row_sum, (0, 2, 1))[..., None]
    log_sum = row_max + jnp.log(row_sum)
    attn_heads = context.reshape(seqs, full_rows, columns).astype(bf_type)
    attn_heads, down = tie(attn_heads, down)
    down = gather.open_one(down)
    attn = exchange(attn_heads, "seq", 1, 2)
    attn, down = tie(attn, down)
    down = gather.open_two(*down)
    out_up, down = tie(out_up, down)
    full_down = gather.open_cores(down)
    full_out, full_up = out_up[:, :width], out_up[:, width:]
    own_qkv = jnp.concatenate((w_query, w_key, w_value), axis=1)
    full_qkv = lax.all_gather(own_qkv, BOTH, axis=0, tiled=True)

    resid = tokens.astype(fl_type) + project(attn, full_out) + bias_out
    first = layer_norm(resid, gain_one, shift_one).astype(bf_type)
    inner = project(first, full_up) + bias_up
    active = gelu_exact(inner).astype(bf_type)
    second = first.astype(fl_type) + project(active, full_down) + bias_down
    out_f, norm_two_pull = jax.vjp(layer_norm, second, gain_two, shift_two)
    out_tokens = out_f.astype(bf_type)

    scatter = Scatter(dp_size, seq_size)
    d_second, ffngain_grad, ffnshift_grad = norm_two_pull(cotangent.astype(fl_type))
    d_outer = d_second.astype(bf_type)
    downbias_grad = row_total(d_outer)
    down_terms = scatter.cores(outer_sum(active, d_outer).astype(bf_type))
    d_active = project_back(d_outer, full_down)
    gelu_value, gelu_pull = jax.vjp(gelu_exact, inner)
    d_inner = gelu_pull(d_active)[0].astype(bf_type)
    d_inner, down_terms = tie(d_inner, down_terms)
    down_one, down_two = scatter.plane_one(down_terms)
    upbias_grad = row_total(d_inner)
    upproj_grad = outer_sum(first, d_inner)
    d_first = d_second + project_back(d_inner, full_up)
    norm_one_value, norm_one_pull = jax.vjp(layer_norm, resid, gain_one, shift_one)
    d_resid, attngain_grad, attnshift_grad = norm_one_pull(d_first)
    d_attnout = d_resid.astype(bf_type)
    outbias_grad = row_total(d_attnout)
    outproj_grad = outer_sum(attn, d_attnout)
    d_attn_rows = project_back(d_attnout, full_out).astype(bf_type)
    d_attn_rows, down_one, down_two, full_qkv = tie(d_attn_rows, down_one, down_two, full_qkv)
    down_both = scatter.plane_two(down_one, down_two)
    outup_grad = jnp.concatenate((outproj_grad.astype(bf_type), upproj_grad.astype(bf_type)), axis=1)
    outup_terms = scatter.cores(outup_grad)

    d_attn = exchange(d_attn_rows, "seq", 2, 1).reshape(seqs, full_rows, own_heads, head_size)
    d_attn, outup_terms, down_both = tie(d_attn, outup_terms, down_both)
    outup_one, outup_two = scatter.plane_one(outup_terms)
    down_shard = scatter.line_sum(down_both)

    def attention_back(at, grad):
        part = slice(at, at + 1)
        query_s, keys_s, values_s, keep_s = query[part], keys[part], values[part], keep[part]
        delta = jnp.transpose(jnp.sum(grad.astype(fl_type) * context[part], axis=-1), (0, 2, 1))
        scores = jnp.einsum("sqhd,skhd->shqk", query_s, keys_s, preferred_element_type=fl_type) * score_scale
        probs = jnp.where(keep_s, jnp.exp(scores - log_sum[part][..., None]), 0.0)
        d_probs = jnp.einsum("sqhd,skhd->shqk", grad, values_s, preferred_element_type=fl_type)
        d_scores = (probs * (d_probs - delta[..., None])).astype(bf_type)
        d_query = jnp.einsum("shqk,skhd->sqhd", d_scores, keys_s, preferred_element_type=fl_type) * score_scale
        d_keys = jnp.einsum("shqk,sqhd->skhd", d_scores, query_s, preferred_element_type=fl_type) * score_scale
        d_values = jnp.einsum("shqk,sqhd->skhd", probs.astype(bf_type), grad, preferred_element_type=fl_type)
        d_mixed = jnp.stack((d_query, d_keys, d_values), axis=2).astype(bf_type)
        return d_mixed.reshape(1, full_rows, 3 * columns)

    def to_rows(d_mixed):
        spread = exchange(d_mixed.reshape(1, full_rows, 3, columns), "seq", 1, 3)
        return spread.reshape(1, rows, 3 * width)

    d_parts, d_rows = [], []
    for at in range(seqs):
        d_parts.append(attention_back(at, d_attn[at : at + 1]))
        d_rows.append(to_rows(d_parts[-1]))
        if at == 0:
            d_attn, outup_one, outup_two = tie(d_attn, outup_one, outup_two)
            outup_both = scatter.plane_two(outup_one, outup_two)
    d_mixed = jnp.concatenate(d_parts, axis=0)
    d_mixed, outup_both, down_shard = tie(d_mixed, outup_both, down_shard)
    outup_shard = scatter.line_sum(outup_both)

    mixed_grad = outer_sum(all_tokens, d_mixed).astype(bf_type).reshape(count, own_rows, 3 * columns)
    bias_mixed = row_total(d_mixed)
    empty = jnp.zeros((width,), fl_type)
    querybias_grad = lax.dynamic_update_slice_in_dim(empty, bias_mixed[:columns], seq_at * columns, 0)
    valuebias_grad = lax.dynamic_update_slice_in_dim(empty, bias_mixed[2 * columns :], seq_at * columns, 0)
    vector_grads = (
        upbias_grad,
        querybias_grad,
        valuebias_grad,
        outbias_grad,
        attngain_grad,
        attnshift_grad,
        downbias_grad,
        ffngain_grad,
        ffnshift_grad,
    )
    small_grads = jnp.concatenate([item.reshape(count, -1) for item in vector_grads], axis=1)
    small_size = small_grads.shape[1]
    small_grads = jnp.pad(small_grads, ((0, 0), (0, small_room - small_size)))
    small_grads = small_grads.reshape(count, SMALL_ROWS, 3 * columns).astype(bf_type)
    terms = jnp.concatenate((mixed_grad, small_grads), axis=1)
    terms = terms.reshape(2, 2, seq_size, own_rows + SMALL_ROWS, 3 * columns)
    terms = halve(terms, 0, scatter.deep, count, scatter.far)
    terms = halve(terms, 0, scatter.side, count, scatter.near)
    arrived = exchange(terms, "seq", 0, 0).astype(fl_type)
    qkv_shard = arrived[:, :own_rows].reshape(seq_size, own_rows, 3, columns)
    qkv_shard = jnp.transpose(qkv_shard, (2, 1, 0, 3)).reshape(3, own_rows, width)
    small_sums = jnp.sum(arrived[:, own_rows:], axis=0).reshape(small_room)
    vector_shards = []
    at = 0
    for item in vectors:
        vector_shards.append(small_sums[at : at + item.shape[0]])
        at += item.shape[0]

    d_rows = jnp.concatenate(d_rows, axis=0)
    grad_inputs = d_resid + project_back(d_rows, full_qkv)
    return (
        out_tokens,
        grad_inputs.astype(bf_type),
        qkv_shard[0],
        qkv_shard[1],
        qkv_shard[2],
        outup_shard[:, :width],
        outup_shard[:, width:],
        down_shard,
        vector_shards[1],
        vector_shards[2],
        vector_shards[3],
        vector_shards[4],
        vector_shards[5],
        vector_shards[0],
        vector_shards[6],
        vector_shards[7],
        vector_shards[8],
    )


def solution(mesh):
    seq_size = mesh.shape["seq"]
    by_heads = HEADS % seq_size == 0 and mesh.shape["dp"] == 4 and seq_size in (2, 4, 8, 16)
    body = functools.partial(local_heads, mesh.shape["dp"], seq_size) if by_heads else local_gathered
    return jax.shard_map(
        body,
        mesh=mesh,
        in_specs=(
            P("dp", "seq", None),
            P("dp"),
            P(("dp", "seq"), None),
            P(("dp", "seq"), None),
            P(("dp", "seq"), None),
            P(("dp", "seq"), None),
            P(("dp", "seq"), None),
            P(("dp", "seq"), None),
            P(("dp", "seq")),
            P(("dp", "seq")),
            P(("dp", "seq")),
            P(("dp", "seq")),
            P(("dp", "seq")),
            P(("dp", "seq")),
            P(("dp", "seq")),
            P(("dp", "seq")),
            P(("dp", "seq")),
            P("dp", "seq", None),
        ),
        out_specs=(
            P("dp", "seq", None),
            P("dp", "seq", None),
            P(("dp", "seq"), None),
            P(("dp", "seq"), None),
            P(("dp", "seq"), None),
            P(("dp", "seq"), None),
            P(("dp", "seq"), None),
            P(("dp", "seq"), None),
            P(("dp", "seq")),
            P(("dp", "seq")),
            P(("dp", "seq")),
            P(("dp", "seq")),
            P(("dp", "seq")),
            P(("dp", "seq")),
            P(("dp", "seq")),
            P(("dp", "seq")),
            P(("dp", "seq")),
        ),
        check_vma=False,
    )
```
